32 devices in a mesh: fsdp: 8 (over z, core), seq: 4 (over y, x).
Axes of the slice: x: 2, y: 2, z: 4, core: 2. Of those that a mesh axis runs over, the one named last changes fastest.
Arguments:
- inputs: bfloat16 [8, 1024, 2048], P('fsdp', 'seq'), may hold values from -6 to 6
- cotangent: bfloat16 [8, 1024, 2048], P('fsdp', 'seq'), may hold values from -6 to 6
- norm1_gain: bfloat16 [2048], P('fsdp'), may hold values from 0.5 to 1.5
- w_qkv: bfloat16 [2048, 6144], P('fsdp'), may hold values from -0.125 to 0.125
- w_beta: bfloat16 [2048, 16], P('fsdp'), may hold values from -0.125 to 0.125
- conv_weight: bfloat16 [2048, 12], P('fsdp'), may hold values from -3 to 3
- out_gain: bfloat16 [128], replicated, may hold values from 0.5 to 1.5
- w_out: bfloat16 [2048, 2048], P('fsdp'), may hold values from -0.125 to 0.125
- norm2_gain: bfloat16 [2048], P('fsdp'), may hold values from 0.5 to 1.5
- w_gate_up: bfloat16 [2048, 11264], P('fsdp'), may hold values from -0.125 to 0.125
- w_down: bfloat16 [5632, 2048], P('fsdp'), may hold values from -0.15625 to 0.15625
Outputs:
- output: bfloat16 [8, 1024, 2048], P('fsdp', 'seq')
- grad_input: float32 [8, 1024, 2048], P('fsdp', 'seq')
- grad_norm1_gain: float32 [2048], P('fsdp')
- grad_w_qkv: float32 [2048, 6144], P('fsdp')
- grad_w_beta: float32 [2048, 16], P('fsdp')
- grad_conv_weight: float32 [2048, 12], P('fsdp')
- grad_out_gain: float32 [128], replicated
- grad_w_out: float32 [2048, 2048], P('fsdp')
- grad_norm2_gain: float32 [2048], P('fsdp')
- grad_w_gate_up: float32 [2048, 11264], P('fsdp')
- grad_w_down: float32 [5632, 2048], P('fsdp')
The draws below stay inside these ranges and needn't reach their ends.
All inputs are finite; a program needn't handle non-finite values.
Results may differ from the reference program's by a relative error of at most 0.023.
Values may be sent and summed in bfloat16 or wider, within the bound.
A program may use at most 448 MiB of HBM per device.

```python
import math
import jax
import jax.numpy as jnp
from jax import lax

D = 2048
H = 16
DK = 128
FF = 5632
CONV = 4
SPAN = 64
LENGTH = 1024
SEQUENCES = 8


def strengthened(values, own_key, source, target, parts, factor):
    def block_of(dim):
        return (jnp.arange(values.shape[dim]) // (values.shape[dim] // parts)).reshape((-1,) + (1,) * (values.ndim - 1 - dim))

    first = jax.random.permutation(own_key, parts)[block_of(target)]
    other_side = (block_of(target) + parts // 2) % parts
    return jnp.where((block_of(source) == first) | (block_of(source) == other_side), factor * values, values)


def shard_levels(stream_key, extent, cuts, least, top_value):
    level = 1.0
    for dim, blocks in cuts:
        steps = jax.random.uniform(jax.random.fold_in(jax.random.fold_in(stream_key, 6), dim), (blocks,), jnp.float32, least / len(cuts), top_value / len(cuts))
        level = level * jnp.repeat(jnp.exp(steps), extent[dim] // blocks).reshape((-1,) + (1,) * (len(extent) - 1 - dim))
    return level


def noise(stream_key, shape, width, limit, cuts=(), kind=jnp.bfloat16):
    values = width * jax.random.normal(stream_key, shape, jnp.float32)
    if cuts:
        values = values * shard_levels(stream_key, shape, cuts, -0.22, 0.18)
    return jnp.clip(values, -limit, limit).astype(kind)


def gaussian_with(stream_key, extent, deviation, limit, cuts, heavy, kind=jnp.bfloat16):
    values = deviation * jax.random.normal(stream_key, extent, jnp.float32)
    if cuts:
        values = values * shard_levels(stream_key, extent, cuts, -0.22, 0.18)
    return jnp.clip(strengthened(values, jax.random.fold_in(stream_key, 3), *heavy), -limit, limit).astype(kind)


def setup_inputs(seed: int = 0) -> dict:
    key_of = jax.random.split(jax.random.key(seed), 12)
    inputs = gaussian_with(key_of[0], (SEQUENCES, LENGTH, D), 1.0, 6.0, ((0, 8), (1, 4)), (0, 2, 8, 2.0))
    cotangent = noise(key_of[1], (SEQUENCES, LENGTH, D), 1.0, 6.0, ((0, 8), (1, 4)))
    norm1_gain = jnp.clip(1.0 + 0.1 * jax.random.normal(key_of[2], (D,), jnp.float32), 0.5, 1.5).astype(jnp.bfloat16)
    w_qkv = noise(key_of[3], (D, 3 * D), D ** -0.5, 0.125, ((0, 8),))
    w_beta = noise(key_of[4], (D, H), D ** -0.5, 0.125, ((0, 8),))
    conv_weight = noise(key_of[5], (D, 3 * CONV), 0.5, 3.0, ((0, 8),))
    out_gain = jnp.clip(1.0 + 0.1 * jax.random.normal(key_of[6], (DK,), jnp.float32), 0.5, 1.5).astype(jnp.bfloat16)
    w_out = noise(key_of[7], (D, D), D ** -0.5, 0.125, ((0, 8),))
    norm2_gain = jnp.clip(1.0 + 0.1 * jax.random.normal(key_of[8], (D,), jnp.float32), 0.5, 1.5).astype(jnp.bfloat16)
    w_gate_up = noise(key_of[9], (D, 2 * FF), D ** -0.5, 0.125, ((0, 8),))
    w_down = noise(key_of[10], (FF, D), (FF // 4) ** -0.5, 0.15625, ((0, 8),))
    return dict(inputs=inputs, cotangent=cotangent, norm1_gain=norm1_gain, w_qkv=w_qkv, w_beta=w_beta, conv_weight=conv_weight, out_gain=out_gain, w_out=w_out, norm2_gain=norm2_gain, w_gate_up=w_gate_up, w_down=w_down)


EPS = 1e-06
HIGH = lax.Precision.HIGHEST

@jax.custom_vjp
def low(v):
    return lax.optimization_barrier(v.astype(jnp.bfloat16)).astype(jnp.float32)

@jax.custom_vjp
def low_back(v):
    return v

def low_keep(v):
    return (low(v), None)

def low_pass(kept, grad):
    return (grad,)

def back_keep(v):
    return (v, None)

def back_low(kept, grad):
    return (low(grad),)
low.defvjp(low_keep, low_pass)
low_back.defvjp(back_keep, back_low)

def rms_scale(values, gain):
    return values * lax.rsqrt(lax.optimization_barrier(jnp.mean(values * values, axis=-1, keepdims=True)) + EPS) * gain

def delta_reference(query, key, value, beta):
    groups, length = (query.shape[0], query.shape[1])
    count = length // SPAN

    def blocks(array):
        moved = jnp.moveaxis(array, 1, 0)
        return moved.reshape((count, SPAN) + moved.shape[1:])

    def token(state, pieces):
        q_now, k_now, v_now, b_now = pieces
        recalled = jnp.einsum('ghd,ghde->ghe', k_now, state, precision=HIGH)
        update = b_now[..., None] * (v_now - recalled)
        state = state + k_now[..., :, None] * update[..., None, :]
        return (state, jnp.einsum('ghd,ghde->ghe', q_now, state, precision=HIGH))

    def block_step(state, pieces):
        return lax.scan(token, state, pieces)
    start = jnp.zeros((groups, H, DK, DK), jnp.float32)
    final, outputs = lax.scan(jax.checkpoint(block_step), start, (blocks(query), blocks(key), blocks(value), blocks(beta)))
    return jnp.moveaxis(outputs.reshape((length, groups, H, DK)), 0, 1)

def layer(source, gain_first, qkv_weight, beta_weight, conv_weight, gain_heads, out_weight, gain_second, gate_up_weight, down_weight):
    groups = source.shape[0]
    normed_first = low(rms_scale(source, gain_first))
    projected = low_back(low(jnp.matmul(normed_first, qkv_weight, precision=HIGH)))
    beta_logits = low_back(jnp.matmul(normed_first, beta_weight, precision=HIGH))
    padded = jnp.pad(projected, ((0, 0), (CONV - 1, 0), (0, 0)))
    table = conv_weight.reshape(D, 3, CONV).transpose(1, 0, 2).reshape(3 * D, CONV)
    mixed = padded[:, 0:LENGTH, :] * table[:, 0]
    for tap_index in range(1, CONV):
        mixed = mixed + padded[:, tap_index:tap_index + LENGTH, :] * table[:, tap_index]
    active = jax.nn.silu(mixed)
    query = active[..., :D].reshape(groups, LENGTH, H, DK) * DK ** (-0.5)
    key = active[..., D:2 * D].reshape(groups, LENGTH, H, DK)
    key = key * lax.rsqrt(lax.optimization_barrier(jnp.sum(key * key, axis=-1, keepdims=True)) + EPS)
    value = active[..., 2 * D:].reshape(groups, LENGTH, H, DK)
    beta = jax.nn.sigmoid(beta_logits)
    query = low_back(low(query))
    key = low_back(low(key))
    value = low_back(low(value))
    beta = low_back(low(beta))
    heads_out = low_back(low(delta_reference(query, key, value, beta)))
    normed_heads = low(rms_scale(heads_out, gain_heads)).reshape(groups, LENGTH, D)
    middle = source + low_back(jnp.matmul(normed_heads, out_weight, precision=HIGH))
    normed_second = low(rms_scale(middle, gain_second))
    gate_up = low_back(jnp.matmul(normed_second, gate_up_weight, precision=HIGH))
    hidden = low(jax.nn.silu(gate_up[..., :FF]) * gate_up[..., FF:])
    return middle + jnp.matmul(hidden, down_weight, precision=HIGH)

def reference(inputs, cotangent, norm1_gain, w_qkv, w_beta, conv_weight, out_gain, w_out, norm2_gain, w_gate_up, w_down):
    weights = tuple((item.astype(jnp.float32) for item in (norm1_gain, w_qkv, w_beta, conv_weight, out_gain, w_out, norm2_gain, w_gate_up, w_down)))
    group = math.gcd(SEQUENCES, max(1, 4096 // LENGTH))
    sources = inputs.astype(jnp.float32).reshape(SEQUENCES // group, group, LENGTH, D)
    upstream = cotangent.astype(jnp.float32).reshape(SEQUENCES // group, group, LENGTH, D)

    def one_group(totals, pieces):
        source, grad_out = pieces
        result, back = jax.vjp(layer, source, *weights)
        grads = back(grad_out)
        totals = tuple((total + grad for total, grad in zip(totals, grads[1:])))
        return (totals, (result, grads[0]))
    zeros = tuple((jnp.zeros_like(item) for item in weights))
    totals, (results, grad_sources) = lax.scan(one_group, zeros, (sources, upstream))
    output = results.reshape(SEQUENCES, LENGTH, D).astype(jnp.bfloat16)
    grad_input = grad_sources.reshape(SEQUENCES, LENGTH, D)
    return (output, grad_input, totals[0], totals[1], totals[2], totals[3], totals[4], totals[5], totals[6], totals[7], totals[8])
```

```python
import functools

import jax
import jax.numpy as jnp
from jax import lax
from jax.experimental import pallas as pl
from jax.experimental.pallas import tpu as pltpu
from jax.sharding import PartitionSpec as P

H = 16
DK = 128
EPS = 1e-06
CHUNK = 128
HEAD_ROOM = 8


def dotf(left, right, dims):
    return lax.dot_general(left, right, (dims, ((), ())), preferred_element_type=jnp.float32)


NN = ((1,), (0,))
NT = ((1,), (1,))
TN = ((0,), (0,))


def low(value):
    return value.astype(jnp.bfloat16)


def square_iota(axis):
    return lax.broadcasted_iota(jnp.int32, (CHUNK, CHUNK), axis)


def sigmoid(value):
    return 1.0 / (1.0 + jnp.exp(-value))


def conv_chunk(window, taps, count):
    mixed = window[HEAD_ROOM:] * taps[count - 1]
    for back in range(1, count):
        mixed = mixed + pltpu.roll(window, back, 0)[HEAD_ROOM:] * taps[count - 1 - back]
    return mixed


def window_of(proj_ref, chunk, column):
    lanes = pl.ds(column, DK)
    start = pl.multiple_of(chunk * CHUNK, CHUNK)
    ahead = pl.multiple_of(jnp.maximum(start - 16, 0), 16)
    before = proj_ref[pl.ds(ahead, 16), lanes].astype(jnp.float32)[8:]
    before = jnp.where(chunk > 0, before, 0.0)
    return jnp.concatenate(
        [before, proj_ref[pl.ds(start, CHUNK), lanes].astype(jnp.float32)], axis=0
    )


def head_inputs(proj_ref, table_ref, chunk, head, heads, taps):
    wide = heads * DK
    found = []
    for part in range(3):
        window = window_of(proj_ref, chunk, part * wide + head * DK)
        weights = [
            table_ref[pl.ds(part * taps + tap, 1), pl.ds(head * DK, DK)] for tap in range(taps)
        ]
        mixed = conv_chunk(window, weights, taps)
        gate = sigmoid(mixed)
        found.append((window, weights, mixed, gate, mixed * gate))
    active_key = found[1][4]
    scale = lax.rsqrt(jnp.sum(active_key * active_key, axis=-1, keepdims=True) + EPS)
    key = active_key * scale
    return found, found[0][4] * DK**-0.5, key, scale, found[2][4]


def inverse_of(strict):
    row, column = square_iota(0), square_iota(1)
    eye = (row == column).astype(jnp.float32)
    solved = eye - jnp.where(row // 2 == column // 2, strict, 0.0)
    half = 2
    while half < CHUNK:
        below = (row // (2 * half) == column // (2 * half)) & (row // half != column // half)
        off = low(jnp.where(below, strict, 0.0))
        known = low(solved)
        solved = solved - dotf(low(dotf(known, off, NN)), known, NN)
        half *= 2
    return solved


def forward_kernel(
    heads, taps, proj_ref, logit_ref, table_ref, gain_ref,
    normed_ref, raw_ref, fresh_ref, solve_ref, state_ref, carry,
):
    length = proj_ref.shape[0]
    carry[...] = jnp.zeros_like(carry)

    def step(chunk, _):
        start = pl.multiple_of(chunk * CHUNK, CHUNK)
        here = pl.ds(start, CHUNK)
        row, column = square_iota(0), square_iota(1)
        beta_all = low(sigmoid(logit_ref[here, :])).astype(jnp.float32)
        for head in range(heads):
            lanes = pl.ds(head * DK, DK)
            _, query, key, _, value = head_inputs(proj_ref, table_ref, chunk, head, heads, taps)
            query, key, value = low(query), low(key), low(value).astype(jnp.float32)
            beta = beta_all[:, head : head + 1]
            strict = jnp.where(row > column, dotf(key, key, NT) * beta, 0.0)
            solved = low(inverse_of(strict))
            within = low(jnp.where(row >= column, dotf(query, key, NT), 0.0))
            state = carry[head]
            state_low = low(state)
            rest = value - dotf(key, state_low, NN)
            fresh = low(dotf(solved, low(beta * rest), NN))
            raw = low(dotf(query, state_low, NN) + dotf(within, fresh, NN))
            carry[head] = state + dotf(key, fresh, TN)
            wide_raw = raw.astype(jnp.float32)
            normed = wide_raw * lax.rsqrt(
                jnp.mean(wide_raw * wide_raw, axis=-1, keepdims=True) + EPS
            )
            normed_ref[here, lanes] = low(normed * gain_ref[...])
            raw_ref[here, lanes] = raw
            fresh_ref[here, lanes] = fresh
            solve_ref[chunk, head] = solved
            state_ref[chunk, head] = state_low
        return 0

    lax.fori_loop(0, length // CHUNK, step, 0)


def backward_kernel(
    heads, taps, proj_ref, logit_ref, table_ref, gain_ref, raw_ref, fresh_ref, solve_ref,
    state_ref, grad_ref, gproj_ref, gtable_ref, ggain_ref, carry, after,
):
    length = proj_ref.shape[0]
    count = length // CHUNK
    wide = heads * DK
    carry[...] = jnp.zeros_like(carry)
    after[...] = jnp.zeros_like(after)
    gtable_ref[...] = jnp.zeros_like(gtable_ref)
    ggain_ref[...] = jnp.zeros_like(ggain_ref)

    def step(index, _):
        chunk = count - 1 - index
        start = pl.multiple_of(chunk * CHUNK, CHUNK)
        here = pl.ds(start, CHUNK)
        row, column = square_iota(0), square_iota(1)
        beta_wide = sigmoid(logit_ref[here, :])
        beta_all = low(beta_wide).astype(jnp.float32)
        lane = lax.broadcasted_iota(jnp.int32, (CHUNK, DK), 1)
        glogit = jnp.zeros((CHUNK, DK), jnp.float32)
        for head in range(heads):
            lanes = pl.ds(head * DK, DK)
            found, query_wide, key_wide, scale, value_wide = head_inputs(
                proj_ref, table_ref, chunk, head, heads, taps
            )
            query, key, value = low(query_wide), low(key_wide), low(value_wide)
            beta = beta_all[:, head : head + 1]
            raw = raw_ref[here, lanes].astype(jnp.float32)
            grad_normed = grad_ref[here, lanes].astype(jnp.float32)
            r = lax.rsqrt(jnp.mean(raw * raw, axis=-1, keepdims=True) + EPS)
            scaled = grad_normed * gain_ref[...]
            grad_out = low(
                r * (scaled - raw * (r * r) * jnp.mean(scaled * raw, axis=-1, keepdims=True))
            )
            ggain_ref[...] += jnp.sum(grad_normed * raw * r, axis=0, keepdims=True)

            state, solved, fresh = state_ref[chunk, head], solve_ref[chunk, head], fresh_ref[here, lanes]
            later = carry[head]
            later_low = low(later)
            gram = dotf(key, key, NT)
            within = low(jnp.where(row >= column, dotf(query, key, NT), 0.0))
            grad_fresh = dotf(within, grad_out, TN) + dotf(key, later_low, NN)
            grad_solved = dotf(solved, low(grad_fresh), TN)
            grad_value = beta * grad_solved
            grad_rest = low(grad_value)
            carry[head] = later + dotf(query, grad_out, TN) - dotf(key, grad_rest, TN)
            rest = value.astype(jnp.float32) - dotf(key, state, NN)
            grad_within = low(jnp.where(row >= column, dotf(grad_out, fresh, NT), 0.0))
            grad_strict = jnp.where(row > column, -dotf(low(grad_solved), fresh, NT), 0.0)
            grad_beta = jnp.sum(grad_solved * rest, axis=-1, keepdims=True) + jnp.sum(
                grad_strict * gram, axis=-1, keepdims=True
            )
            mixing = low(beta * grad_strict)
            grad_query = dotf(grad_out, state, NT) + dotf(grad_within, key, NN)
            grad_key = (
                dotf(grad_within, query, TN)
                + dotf(fresh, later_low, NT)
                - dotf(grad_rest, state, NT)
                + dotf(mixing, key, NN)
                + dotf(mixing, key, TN)
            )
            bw = beta_wide[:, head : head + 1]
            grad_beta = low(grad_beta).astype(jnp.float32) * bw * (1.0 - bw)
            glogit = glogit + jnp.where(lane == head, grad_beta, 0.0)

            grad_query = low(grad_query).astype(jnp.float32) * DK**-0.5
            grad_key = low(grad_key).astype(jnp.float32)
            grad_key = scale * (
                grad_key - key_wide * jnp.sum(grad_key * key_wide, axis=-1, keepdims=True)
            )
            grad_value = low(grad_value).astype(jnp.float32)
            for part, grad_active in enumerate((grad_query, grad_key, grad_value)):
                window, weights, mixed, gate, _ = found[part]
                grad_conv = grad_active * (gate * (1.0 + mixed * (1.0 - gate)))
                columns = pl.ds(part * wide + head * DK, DK)
                tail = jnp.concatenate([grad_conv, after[:, columns]], axis=0)
                size = CHUNK + HEAD_ROOM
                total = grad_conv * weights[taps - 1]
                for back in range(1, taps):
                    total = total + pltpu.roll(tail, size - back, 0)[:CHUNK] * weights[taps - 1 - back]
                gproj_ref[here, columns] = low(total)
                after[:, columns] = grad_conv[:HEAD_ROOM]
                for back in range(taps):
                    shifted = pltpu.roll(window, back, 0)[HEAD_ROOM:] if back else window[HEAD_ROOM:]
                    spot = pl.ds(part * taps + taps - 1 - back, 1)
                    gtable_ref[spot, lanes] += jnp.sum(grad_conv * shifted, axis=0, keepdims=True)
        gproj_ref[here, pl.ds(3 * wide, DK)] = low(glogit)
        return 0

    lax.fori_loop(0, count, step, 0)


def in_vmem(count):
    return [pl.BlockSpec(memory_space=pltpu.VMEM)] * count


def mix_forward(proj, logits, table, gain):
    length = proj.shape[0]
    heads = table.shape[1] // DK
    taps = table.shape[0] // 3
    count = length // CHUNK
    wide = heads * DK
    shape = jax.ShapeDtypeStruct
    return pl.pallas_call(
        functools.partial(forward_kernel, heads, taps),
        out_shape=(
            shape((length, wide), jnp.bfloat16),
            shape((length, wide), jnp.bfloat16),
            shape((length, wide), jnp.bfloat16),
            shape((count, heads, CHUNK, CHUNK), jnp.bfloat16),
            shape((count, heads, DK, DK), jnp.bfloat16),
        ),
        in_specs=in_vmem(4),
        out_specs=tuple(in_vmem(5)),
        scratch_shapes=[pltpu.VMEM((heads, DK, DK), jnp.float32)],
        compiler_params=pltpu.CompilerParams(vmem_limit_bytes=40 * 2**20),
        cost_estimate=pl.CostEstimate(
            flops=length * heads * DK * 8000, bytes_accessed=16 * length * wide, transcendentals=3 * length * wide
        ),
        name="mix_forward",
    )(proj, logits, table, gain)


def mix_backward(proj, logits, table, gain, raw, fresh, solved, states, grad):
    length = proj.shape[0]
    heads = table.shape[1] // DK
    taps = table.shape[0] // 3
    wide = heads * DK
    shape = jax.ShapeDtypeStruct
    return pl.pallas_call(
        functools.partial(backward_kernel, heads, taps),
        out_shape=(
            shape((length, 3 * wide + DK), jnp.bfloat16),
            shape((3 * taps, wide), jnp.float32),
            shape((1, DK), jnp.float32),
        ),
        in_specs=in_vmem(9),
        out_specs=tuple(in_vmem(3)),
        scratch_shapes=[
            pltpu.VMEM((heads, DK, DK), jnp.float32),
            pltpu.VMEM((HEAD_ROOM, 3 * wide), jnp.float32),
        ],
        compiler_params=pltpu.CompilerParams(vmem_limit_bytes=40 * 2**20),
        cost_estimate=pl.CostEstimate(
            flops=length * heads * DK * 10000, bytes_accessed=26 * length * wide, transcendentals=3 * length * wide
        ),
        name="mix_backward",
    )(proj, logits, table, gain, raw, fresh, solved, states, grad)


def neighbours():
    me = lax.axis_index("seq")
    return me, me + 1 - 2 * (me % 2), me + 2 - 4 * (me // 2), 3 - me


def greet(across, along):
    barrier = pltpu.get_barrier_semaphore()
    for other in (across, along):
        pl.semaphore_signal(
            barrier, inc=1, device_id={"seq": other}, device_id_type=pl.DeviceIdType.MESH
        )
    pl.semaphore_wait(barrier, 2)


def remote(source, target, send, arrive, slot, other):
    return pltpu.make_async_remote_copy(
        src_ref=source,
        dst_ref=target,
        send_sem=send.at[slot],
        recv_sem=arrive.at[slot],
        device_id={"seq": other},
        device_id_type=pl.DeviceIdType.MESH,
    )


def half_of(rows):
    return (rows // 2 + 15) // 16 * 16


def gather_start(source, target, near, send, arrive, keep):
    me, across, along, _ = near
    own = pltpu.make_async_copy(source, target.at[me], keep)
    first = remote(source, target.at[me], send, arrive, 0, across)
    second = remote(source, target.at[me], send, arrive, 1, along)
    own.start()
    first.start()
    second.start()
    return own, first, second


def gather_finish(started, target, near, send, arrive):
    _, across, along, _ = near
    own, first, second = started
    rows = target.shape[1]
    split = half_of(rows)
    head, rest = pl.ds(0, split), pl.ds(split, rows - split)
    first.wait_recv()
    third = remote(target.at[across, head], target.at[across, head], send, arrive, 2, along)
    third.start()
    second.wait_recv()
    fourth = remote(target.at[along, rest], target.at[along, rest], send, arrive, 3, across)
    fourth.start()
    third.wait_recv()
    fourth.wait_recv()
    for copy in (first, second, third, fourth):
        copy.wait_send()
    own.wait()


def gather_kernel(count, *refs):
    sources, targets = refs[:count], refs[count : 2 * count]
    send, arrive, keep = refs[2 * count :]
    near = neighbours()
    greet(near[1], near[2])
    started = [
        gather_start(sources[i], targets[i], near, send.at[i], arrive.at[i], keep.at[i])
        for i in range(count)
    ]
    for i in range(count):
        gather_finish(started[i], targets[i], near, send.at[i], arrive.at[i])


def seq_gather(name, number, *blocks):
    count = len(blocks)
    side = lax.axis_size("seq")
    if side != 4:
        return [lax.all_gather(block, "seq", axis=0) for block in blocks]
    moved = sum(block.size for block in blocks)
    return pl.pallas_call(
        functools.partial(gather_kernel, count),
        out_shape=[
            jax.ShapeDtypeStruct((side,) + block.shape, block.dtype) for block in blocks
        ],
        in_specs=[pl.BlockSpec(memory_space=pl.ANY)] * count,
        out_specs=[pl.BlockSpec(memory_space=pl.ANY)] * count,
        scratch_shapes=[
            pltpu.SemaphoreType.DMA((count, 4)),
            pltpu.SemaphoreType.DMA((count, 4)),
            pltpu.SemaphoreType.DMA((count,)),
        ],
        compiler_params=pltpu.CompilerParams(collective_id=number, has_side_effects=True),
        cost_estimate=pl.CostEstimate(flops=0, bytes_accessed=160 * moved, transcendentals=0),
        name=name,
    )(*blocks)


TILE = 256
STEP = 16


def reduce_rows_kernel(flip, gathers, epilogue, in_count, out_count, *refs):
    left_ref, right_ref, *extra = refs[:in_count]
    outs = refs[in_count : in_count + out_count]
    far, wide_x, wide_y, own, get_a, get_b, get_x, get_y, send, arrive = refs[
        in_count + out_count : in_count + out_count + 10
    ]
    rest_refs = refs[in_count + out_count + 10 :]
    near = neighbours()
    me, across, along, opposite = near
    greet(across, along)
    rows, width = own.shape
    split = half_of(rows)
    head, rest = pl.ds(0, split), pl.ds(split, rows - split)

    def part(block, store):
        here = pl.ds(pl.multiple_of(block * rows, rows), rows)

        @pl.loop(0, width // TILE)
        def _(tile):
            columns = pl.ds(pl.multiple_of(tile * TILE, TILE), TILE)
            if flip:
                value = dotf(left_ref[here, :], right_ref[columns, :], NT)
            else:
                value = dotf(left_ref[here, :], right_ref[:, columns], NN)
            store[:, columns] = value.astype(store.dtype)

    def add_into(store, base, source):
        @pl.loop(0, source.shape[0] // STEP)
        def _(index):
            start = pl.multiple_of(index * STEP, STEP)
            there = pl.ds(pl.multiple_of(base + start, STEP), STEP)
            total = store[there, :].astype(jnp.float32) + source[pl.ds(start, STEP), :].astype(
                jnp.float32
            )
            store[there, :] = low(total)

    part(opposite, far)
    copies = [
        remote(far.at[head], get_a, send, arrive, 0, across),
        remote(far.at[rest], get_b, send, arrive, 1, along),
    ]
    copies[0].start()
    copies[1].start()
    part(across, wide_x)
    copies.append(remote(wide_x.at[head], get_x.at[head], send, arrive, 2, across))
    copies[2].start()
    part(along, wide_y)
    copies.append(remote(wide_y.at[rest], get_y.at[rest], send, arrive, 3, along))
    copies[3].start()
    copies[0].wait_recv()
    add_into(wide_y, 0, get_a)
    copies.append(remote(wide_y.at[head], get_y.at[head], send, arrive, 4, along))
    copies[4].start()
    copies[1].wait_recv()
    add_into(wide_x, split, get_b)
    copies.append(remote(wide_x.at[rest], get_x.at[rest], send, arrive, 5, across))
    copies[5].start()
    part(me, own)
    for copy in copies[2:]:
        copy.wait_recv()
    epilogue_prepare = rest_refs[0] if gathers else None

    @pl.loop(0, rows // STEP)
    def _(index):
        here = pl.ds(pl.multiple_of(index * STEP, STEP), STEP)
        total = (
            own[here, :] + get_x[here, :].astype(jnp.float32) + get_y[here, :].astype(jnp.float32)
        )
        epilogue(index, here, total, extra, outs, epilogue_prepare)

    for copy in copies:
        copy.wait_send()
    if gathers:
        block, send_2, arrive_2, keep = rest_refs
        target = outs[0]
        started = gather_start(block, target, near, send_2, arrive_2, keep.at[0])
        gather_finish(started, target, near, send_2, arrive_2)


def rms_back(grad, values, gain):
    r = lax.rsqrt(jnp.mean(values * values, axis=-1, keepdims=True) + EPS)
    scaled = grad * gain
    change = r * (scaled - values * (r * r) * jnp.mean(scaled * values, axis=-1, keepdims=True))
    return change, jnp.sum(grad * values * r, axis=0, keepdims=True)


def middle_epilogue(index, here, total, extra, outs, block):
    source_ref, gain_ref = extra
    middle = source_ref[here, :].astype(jnp.float32) + total
    outs[1][here, :] = middle
    r = lax.rsqrt(jnp.mean(middle * middle, axis=-1, keepdims=True) + EPS)
    block[here, :] = low(middle * r * gain_ref[...])


def output_epilogue(index, here, total, extra, outs, block):
    outs[0][here, :] = low(extra[0][here, :] + total)


def branch_epilogue(index, here, total, extra, outs, block):
    middle_ref, upstream_ref, gain_ref = extra
    change, gain_part = rms_back(total, middle_ref[here, :], gain_ref[...])
    grad = upstream_ref[here, :].astype(jnp.float32) + change
    outs[1][here, :] = grad
    block[here, :] = low(grad)
    outs[2][...] = jnp.where(index > 0, outs[2][...], 0.0) + gain_part


def input_epilogue(index, here, total, extra, outs, block):
    source_ref, carried_ref, gain_ref = extra
    change, gain_part = rms_back(total, source_ref[here, :].astype(jnp.float32), gain_ref[...])
    outs[0][here, :] = carried_ref[here, :] + change
    outs[1][...] = jnp.where(index > 0, outs[1][...], 0.0) + gain_part


def fused_reduce(name, number, flip, gathers, epilogue, outs, left, right, *extra):
    side = lax.axis_size("seq")
    length = left.shape[0]
    rows = length // side
    width = right.shape[0] if flip else right.shape[1]
    split = half_of(rows)
    scratch = [
        pltpu.VMEM((rows, width), jnp.bfloat16),
        pltpu.VMEM((rows, width), jnp.bfloat16),
        pltpu.VMEM((rows, width), jnp.bfloat16),
        pltpu.VMEM((rows, width), jnp.float32),
        pltpu.VMEM((split, width), jnp.bfloat16),
        pltpu.VMEM((rows - split, width), jnp.bfloat16),
        pltpu.VMEM((rows, width), jnp.bfloat16),
        pltpu.VMEM((rows, width), jnp.bfloat16),
        pltpu.SemaphoreType.DMA((6,)),
        pltpu.SemaphoreType.DMA((6,)),
    ]
    out_specs = in_vmem(len(outs))
    if gathers:
        scratch += [
            pltpu.VMEM((rows, width), jnp.bfloat16),
            pltpu.SemaphoreType.DMA((4,)),
            pltpu.SemaphoreType.DMA((4,)),
            pltpu.SemaphoreType.DMA((1,)),
        ]
        out_specs[0] = pl.BlockSpec(memory_space=pl.ANY)
    return pl.pallas_call(
        functools.partial(
            reduce_rows_kernel, flip, gathers, epilogue, 2 + len(extra), len(outs)
        ),
        out_shape=outs,
        in_specs=in_vmem(2 + len(extra)),
        out_specs=out_specs,
        scratch_shapes=scratch,
        compiler_params=pltpu.CompilerParams(
            collective_id=number, has_side_effects=True, vmem_limit_bytes=50 * 2**20
        ),
        cost_estimate=pl.CostEstimate(
            flops=2 * left.size * width,
            bytes_accessed=(320 if gathers else 160) * rows * width,
            transcendentals=0,
        ),
        name=name,
    )(left, right, *extra)


def seq_sum(partial, side):
    block = low(partial).reshape(side, -1, partial.shape[-1])
    return lax.psum_scatter(block, "seq", scatter_dimension=0).astype(jnp.float32)


def out_and_norm(attn_in, weight, source, gain):
    side = lax.axis_size("seq")
    rows, width = source.shape
    if side != 4:
        middle = source.astype(jnp.float32) + seq_sum(dotf(attn_in, weight, NN), side)
        r = lax.rsqrt(jnp.mean(middle * middle, axis=-1, keepdims=True) + EPS)
        return lax.all_gather(low(middle * r * gain), "seq", axis=0), middle
    outs = (
        jax.ShapeDtypeStruct((side, rows, width), jnp.bfloat16),
        jax.ShapeDtypeStruct((rows, width), jnp.float32),
    )
    return fused_reduce(
        "out_and_norm", 2, False, True, middle_epilogue, outs, attn_in, weight, source, gain
    )


def down_and_add(hidden, weight, middle):
    side = lax.axis_size("seq")
    if side != 4:
        return low(middle + seq_sum(dotf(hidden, weight, NN), side))
    outs = (jax.ShapeDtypeStruct(middle.shape, jnp.bfloat16),)
    return fused_reduce(
        "down_and_add", 3, False, False, output_epilogue, outs, hidden, weight, middle
    )[0]


def branch_grad(grad, weight, middle, upstream, gain):
    side = lax.axis_size("seq")
    rows, width = middle.shape
    if side != 4:
        change, gain_part = rms_back(seq_sum(dotf(grad, weight, NT), side), middle, gain)
        total = upstream.astype(jnp.float32) + change
        return lax.all_gather(low(total), "seq", axis=0), total, gain_part
    outs = (
        jax.ShapeDtypeStruct((side, rows, width), jnp.bfloat16),
        jax.ShapeDtypeStruct((rows, width), jnp.float32),
        jax.ShapeDtypeStruct((1, width), jnp.float32),
    )
    return fused_reduce(
        "branch_grad", 4, True, True, branch_epilogue, outs, grad, weight, middle, upstream, gain
    )


def input_grad(grad, weight, source, carried, gain):
    side = lax.axis_size("seq")
    if side != 4:
        change, gain_part = rms_back(
            seq_sum(dotf(grad, weight, NT), side), source.astype(jnp.float32), gain
        )
        return carried + change, gain_part
    outs = (
        jax.ShapeDtypeStruct(carried.shape, jnp.float32),
        jax.ShapeDtypeStruct(gain.shape, jnp.float32),
    )
    return fused_reduce(
        "input_grad", 5, True, False, input_epilogue, outs, grad, weight, source, carried, gain
    )


def pick_kernel(side, share, source_ref, target_ref):
    me = lax.axis_index("seq")
    count = target_ref.shape[1] // share
    for index in range(side):

        @pl.when(me == index)
        def _():
            pieces = [
                source_ref[:, pl.ds((k * side + index) * share, share)].astype(jnp.float32)
                for k in range(count)
            ]
            target_ref[...] = low(jnp.concatenate(pieces, axis=1))


def pick_columns(weight, share):
    side = lax.axis_size("seq")
    rows, width = weight.shape
    tile = 32
    return pl.pallas_call(
        functools.partial(pick_kernel, side, share),
        grid=(rows // tile,),
        out_shape=jax.ShapeDtypeStruct((rows, width // side), weight.dtype),
        in_specs=[pl.BlockSpec((tile, width), lambda i: (i, 0))],
        out_specs=pl.BlockSpec((tile, width // side), lambda i: (i, 0)),
        name="pick_columns",
    )(weight)


def spread_kernel(side, share, source_ref, target_ref):
    count = source_ref.shape[2] // share
    pieces = [
        source_ref[index, :, pl.ds(k * share, share)].astype(jnp.float32)
        for k in range(count)
        for index in range(side)
    ]
    target_ref[...] = jnp.concatenate(pieces, axis=1)


def spread_columns(parts, share):
    side, rows, width = parts.shape
    tile = 32
    return pl.pallas_call(
        functools.partial(spread_kernel, side, share),
        grid=(rows // tile,),
        out_shape=jax.ShapeDtypeStruct((rows, width * side), jnp.float32),
        in_specs=[pl.BlockSpec((side, tile, width), lambda i: (0, i, 0))],
        out_specs=pl.BlockSpec((tile, width * side), lambda i: (i, 0)),
        name="spread_columns",
    )(parts)


def fsdp_sum(term):
    return lax.psum_scatter(low(term), "fsdp", scatter_dimension=0, tiled=True)


def per_device(
    inputs,
    cotangent,
    norm1_gain,
    w_qkv,
    w_beta,
    conv_weight,
    out_gain,
    w_out,
    norm2_gain,
    w_gate_up,
    w_down,
):
    side = lax.axis_size("seq")
    s = lax.axis_index("seq")
    f = lax.axis_index("fsdp")
    shape = inputs.shape
    width = shape[2]
    source = inputs.reshape(-1, width)
    upstream = cotangent.reshape(-1, width)
    length = source.shape[0] * side
    heads = H // side
    wide = heads * DK
    rows = w_qkv.shape[0]
    share = w_down.shape[0] // side
    taps = conv_weight.shape[1] // 3

    def everywhere(block):
        return lax.all_gather(block, "fsdp", axis=0, tiled=True)

    qkv_part = lax.dynamic_slice_in_dim(w_qkv.reshape(rows, 3, width), s * wide, wide, 2)
    beta_part = lax.dynamic_slice_in_dim(w_beta, s * heads, heads, 1)
    qkv_part = everywhere(
        jnp.concatenate(
            [qkv_part.reshape(rows, 3 * wide), jnp.pad(beta_part, ((0, 0), (0, DK - heads)))],
            axis=1,
        )
    )
    small = jnp.concatenate([norm1_gain[None], norm2_gain[None], conv_weight.T], axis=0)
    small = lax.all_gather(small, "fsdp", axis=0)
    small = small.transpose(1, 0, 2).reshape(small.shape[1], width).astype(jnp.float32)
    gain_first = small[0:1]
    gain_second = small[1:2]
    table = lax.dynamic_slice_in_dim(small[2:], s * wide, wide, 1)
    gain_heads = out_gain.astype(jnp.float32)[None]

    out_part = everywhere(lax.dynamic_slice_in_dim(w_out, s * wide, wide, 1))
    out_part = lax.all_to_all(out_part, "seq", split_axis=0, concat_axis=1, tiled=True)
    gate_up_part = everywhere(pick_columns(w_gate_up, share))
    down_part = everywhere(lax.dynamic_slice_in_dim(w_down, s * share, share, 0))

    source_all, upstream_all = seq_gather("gather_tokens", 1, source, upstream)
    source_all = source_all.reshape(length, width).astype(jnp.float32)
    upstream_all = upstream_all.reshape(length, width)
    normed_first = low(
        source_all
        * lax.rsqrt(jnp.mean(source_all * source_all, axis=-1, keepdims=True) + EPS)
        * gain_first
    )
    projected = low(dotf(normed_first, qkv_part[:, : 3 * wide], NN))
    beta_logits = dotf(normed_first, qkv_part[:, 3 * wide :], NN)
    attn_in, *kept = mix_forward(projected, beta_logits, table, gain_heads)
    ffn_in, middle = out_and_norm(attn_in, out_part, source, gain_second)
    ffn_in = ffn_in.reshape(length, width)
    gate_up = dotf(ffn_in, gate_up_part, NN)
    hidden_width = gate_up.shape[1] // 2
    gate = gate_up[:, :hidden_width]
    upward = gate_up[:, hidden_width:]
    sigma = jax.nn.sigmoid(gate)
    hidden = low(gate * sigma * upward)

    grad_down = fsdp_sum(dotf(hidden, upstream_all, TN))
    grad_hidden = dotf(upstream_all, down_part, NT)
    grad_gate = grad_hidden * upward * sigma * (1.0 + gate * (1.0 - sigma))
    grad_up = grad_hidden * gate * sigma
    grad_gate_up = low(jnp.concatenate([grad_gate, grad_up], axis=1))
    grad_w_gate_up = fsdp_sum(dotf(ffn_in, grad_gate_up, TN))
    grad_branch, grad_middle, grad_gain_second = branch_grad(
        grad_gate_up, gate_up_part, middle, upstream, gain_second
    )
    grad_branch = grad_branch.reshape(length, width)
    output = down_and_add(hidden, down_part, middle)

    grad_w_out = low(dotf(attn_in, grad_branch, TN))
    grad_w_out = lax.all_to_all(grad_w_out, "seq", split_axis=1, concat_axis=0, tiled=True)
    grad_w_out = fsdp_sum(grad_w_out)
    grad_proj, grad_table, grad_gain_heads = mix_backward(
        projected, beta_logits, table, gain_heads, *kept, dotf(grad_branch, out_part, NT)
    )
    grad_qkv = low(dotf(normed_first, grad_proj, TN))
    grad_qkv = lax.dynamic_update_slice(
        grad_qkv, low(grad_table.T), (s * wide, 3 * wide + heads)
    )
    grad_qkv = fsdp_sum(grad_qkv)
    grad_input, grad_gain_first = input_grad(
        grad_proj, qkv_part, source, grad_middle, gain_first
    )
    gains = jnp.concatenate(
        [grad_gain_first, grad_gain_second, jnp.pad(grad_gain_heads, ((0, 0), (0, width - DK)))]
    )
    summed = lax.psum(gains, ("fsdp", "seq"))
    own = lax.dynamic_slice_in_dim(summed, f * rows, rows, 1)

    (grad_down,) = seq_gather("gather_down", 6, grad_down)
    (grad_w_gate_up,) = seq_gather("gather_gate_up", 7, grad_w_gate_up)
    (grad_w_out,) = seq_gather("gather_out", 8, grad_w_out)
    (grad_qkv,) = seq_gather("gather_qkv", 9, grad_qkv)
    grad_w_qkv = jnp.concatenate(
        [grad_qkv[i, :, j * wide : (j + 1) * wide] for j in range(3) for i in range(side)], axis=1
    )
    sides = grad_qkv[:, :, 3 * wide :].astype(jnp.float32)
    grad_w_beta = jnp.concatenate([sides[i, :, :heads] for i in range(side)], axis=1)
    grad_conv = jnp.sum(sides[:, :, heads : heads + 3 * taps], axis=0)
    return (
        output.reshape(shape),
        grad_input.reshape(shape),
        own[0],
        grad_w_qkv.astype(jnp.float32),
        grad_w_beta,
        grad_conv,
        summed[2, :DK],
        jnp.concatenate([grad_w_out[i] for i in range(side)], axis=1).astype(jnp.float32),
        own[1],
        spread_columns(grad_w_gate_up, share),
        grad_down.reshape(-1, width).astype(jnp.float32),
    )


def solution(mesh):
    by_row = P("fsdp", None)
    tokens = P("fsdp", "seq", None)
    specs = (tokens, tokens, P("fsdp"), by_row, by_row, by_row, P(), by_row, P("fsdp"))
    specs = specs + (by_row, by_row)
    return jax.shard_map(per_device, mesh=mesh, in_specs=specs, out_specs=specs, check_vma=False)
```

```python
import functools

import jax
import jax.numpy as jnp
from jax import lax
from jax.experimental import pallas as pl
from jax.experimental.pallas import tpu as pltpu
from jax.sharding import PartitionSpec as P

H = 16
DK = 128
EPS = 1e-06
CHUNK = 128
HEAD_ROOM = 8


def dotf(left, right, dims):
    return lax.dot_general(left, right, (dims, ((), ())), preferred_element_type=jnp.float32)


NN = ((1,), (0,))
NT = ((1,), (1,))
TN = ((0,), (0,))


def low(value):
    return value.astype(jnp.bfloat16)


def square_iota(axis):
    return lax.broadcasted_iota(jnp.int32, (CHUNK, CHUNK), axis)


def sigmoid(value):
    return 1.0 / (1.0 + jnp.exp(-value))


def conv_chunk(window, taps, count):
    mixed = window[HEAD_ROOM:] * taps[count - 1]
    for back in range(1, count):
        mixed = mixed + pltpu.roll(window, back, 0)[HEAD_ROOM:] * taps[count - 1 - back]
    return mixed


def window_of(proj_ref, chunk, column):
    lanes = pl.ds(column, DK)
    start = pl.multiple_of(chunk * CHUNK, CHUNK)
    ahead = pl.multiple_of(jnp.maximum(start - 16, 0), 16)
    before = proj_ref[pl.ds(ahead, 16), lanes].astype(jnp.float32)[8:]
    before = jnp.where(chunk > 0, before, 0.0)
    return jnp.concatenate(
        [before, proj_ref[pl.ds(start, CHUNK), lanes].astype(jnp.float32)], axis=0
    )


def head_inputs(proj_ref, table_ref, chunk, head, heads, taps):
    wide = heads * DK
    found = []
    for part in range(3):
        window = window_of(proj_ref, chunk, part * wide + head * DK)
        weights = [
            table_ref[pl.ds(part * taps + tap, 1), pl.ds(head * DK, DK)] for tap in range(taps)
        ]
        mixed = conv_chunk(window, weights, taps)
        gate = sigmoid(mixed)
        found.append((window, weights, mixed, gate, mixed * gate))
    active_key = found[1][4]
    scale = lax.rsqrt(jnp.sum(active_key * active_key, axis=-1, keepdims=True) + EPS)
    key = active_key * scale
    return found, found[0][4] * DK**-0.5, key, scale, found[2][4]


def inverses_of(stricts):
    row, column = square_iota(0), square_iota(1)
    eye = (row == column).astype(jnp.float32)
    solved = [eye - jnp.where(row // 2 == column // 2, strict, 0.0) for strict in stricts]
    half = 2
    while half < CHUNK:
        below = (row // (2 * half) == column // (2 * half)) & (row // half != column // half)
        off = [low(jnp.where(below, strict, 0.0)) for strict in stricts]
        known = [low(item) for item in solved]
        first = [low(dotf(k, o, NN)) for k, o in zip(known, off)]
        second = [dotf(p, k, NN) for p, k in zip(first, known)]
        solved = [item - change for item, change in zip(solved, second)]
        half *= 2
    return [low(item) for item in solved]


def forward_kernel(
    heads, taps, proj_ref, logit_ref, table_ref, gain_ref,
    normed_ref, raw_ref, fresh_ref, solve_ref, state_ref, carry,
):
    length = proj_ref.shape[0]
    carry[...] = jnp.zeros_like(carry)
    every = range(heads)

    def step(chunk, _):
        start = pl.multiple_of(chunk * CHUNK, CHUNK)
        here = pl.ds(start, CHUNK)
        row, column = square_iota(0), square_iota(1)
        beta_all = low(sigmoid(logit_ref[here, :])).astype(jnp.float32)
        beta = [beta_all[:, h : h + 1] for h in every]
        ready = [head_inputs(proj_ref, table_ref, chunk, h, heads, taps) for h in every]
        query = [low(item[1]) for item in ready]
        key = [low(item[2]) for item in ready]
        value = [low(item[4]) for item in ready]
        gram = [dotf(key[h], key[h], NT) for h in every]
        score = [dotf(query[h], key[h], NT) for h in every]
        strict = [jnp.where(row > column, gram[h] * beta[h], 0.0) for h in every]
        within = [low(jnp.where(row >= column, score[h], 0.0)) for h in every]
        solved = inverses_of(strict)
        state = [carry[h] for h in every]
        state_low = [low(item) for item in state]
        recalled = [dotf(key[h], state_low[h], NN) for h in every]
        rest = [low(beta[h] * (value[h].astype(jnp.float32) - recalled[h])) for h in every]
        fresh = [low(dotf(solved[h], rest[h], NN)) for h in every]
        grown = [dotf(key[h], fresh[h], TN) for h in every]
        for h in every:
            carry[h] = state[h] + grown[h]
        past = [dotf(query[h], state_low[h], NN) for h in every]
        inner = [dotf(within[h], fresh[h], NN) for h in every]
        for h in every:
            lanes = pl.ds(h * DK, DK)
            raw = low(past[h] + inner[h])
            wide_raw = raw.astype(jnp.float32)
            normed = wide_raw * lax.rsqrt(
                jnp.mean(wide_raw * wide_raw, axis=-1, keepdims=True) + EPS
            )
            normed_ref[here, lanes] = low(normed * gain_ref[...])
            raw_ref[here, lanes] = raw
            fresh_ref[here, lanes] = fresh[h]
            solve_ref[chunk, h] = solved[h]
            state_ref[chunk, h] = state_low[h]
        return 0

    lax.fori_loop(0, length // CHUNK, step, 0)


def backward_kernel(
    heads, taps, proj_ref, logit_ref, table_ref, gain_ref, raw_ref, fresh_ref, solve_ref,
    state_ref, grad_ref, gproj_ref, gtable_ref, ggain_ref, carry, after,
):
    length = proj_ref.shape[0]
    count = length // CHUNK
    wide = heads * DK
    carry[...] = jnp.zeros_like(carry)
    after[...] = jnp.zeros_like(after)
    gtable_ref[...] = jnp.zeros_like(gtable_ref)
    ggain_ref[...] = jnp.zeros_like(ggain_ref)
    every = range(heads)

    def step(index, _):
        chunk = count - 1 - index
        start = pl.multiple_of(chunk * CHUNK, CHUNK)
        here = pl.ds(start, CHUNK)
        row, column = square_iota(0), square_iota(1)
        beta_wide = sigmoid(logit_ref[here, :])
        beta_all = low(beta_wide).astype(jnp.float32)
        beta = [beta_all[:, h : h + 1] for h in every]
        lane = lax.broadcasted_iota(jnp.int32, (CHUNK, DK), 1)
        ready = [head_inputs(proj_ref, table_ref, chunk, h, heads, taps) for h in every]
        query = [low(item[1]) for item in ready]
        key = [low(item[2]) for item in ready]
        value = [low(item[4]) for item in ready]
        grad_out = []
        for h in every:
            lanes = pl.ds(h * DK, DK)
            raw = raw_ref[here, lanes].astype(jnp.float32)
            grad_normed = grad_ref[here, lanes].astype(jnp.float32)
            r = lax.rsqrt(jnp.mean(raw * raw, axis=-1, keepdims=True) + EPS)
            scaled = grad_normed * gain_ref[...]
            mean = jnp.mean(scaled * raw, axis=-1, keepdims=True)
            grad_out.append(low(r * (scaled - raw * (r * r) * mean)))
            ggain_ref[...] += jnp.sum(grad_normed * raw * r, axis=0, keepdims=True)
        state = [state_ref[chunk, h] for h in every]
        solved = [solve_ref[chunk, h] for h in every]
        fresh = [fresh_ref[here, pl.ds(h * DK, DK)] for h in every]
        later = [carry[h] for h in every]
        later_low = [low(item) for item in later]
        score = [dotf(query[h], key[h], NT) for h in every]
        onward = [dotf(key[h], later_low[h], NN) for h in every]
        within = [low(jnp.where(row >= column, item, 0.0)) for item in score]
        grad_fresh = [low(dotf(within[h], grad_out[h], TN) + onward[h]) for h in every]
        grad_solved = [dotf(solved[h], grad_fresh[h], TN) for h in every]
        grad_value = [beta[h] * grad_solved[h] for h in every]
        grad_rest = [low(item) for item in grad_value]
        asked = [dotf(query[h], grad_out[h], TN) for h in every]
        taken = [dotf(key[h], grad_rest[h], TN) for h in every]
        for h in every:
            carry[h] = later[h] + asked[h] - taken[h]
        gram = [dotf(key[h], key[h], NT) for h in every]
        recalled = [dotf(key[h], state[h], NN) for h in every]
        product = [dotf(grad_out[h], fresh[h], NT) for h in every]
        cross = [dotf(low(grad_solved[h]), fresh[h], NT) for h in every]
        grad_within = [low(jnp.where(row >= column, item, 0.0)) for item in product]
        grad_strict = [jnp.where(row > column, -item, 0.0) for item in cross]
        mixing = [low(beta[h] * grad_strict[h]) for h in every]
        grad_query = [
            dotf(grad_out[h], state[h], NT) + dotf(grad_within[h], key[h], NN) for h in every
        ]
        grad_key = [
            dotf(grad_within[h], query[h], TN)
            + dotf(fresh[h], later_low[h], NT)
            - dotf(grad_rest[h], state[h], NT)
            + dotf(mixing[h], key[h], NN)
            + dotf(mixing[h], key[h], TN)
            for h in every
        ]
        glogit = jnp.zeros((CHUNK, DK), jnp.float32)
        for h in every:
            rest = value[h].astype(jnp.float32) - recalled[h]
            grad_beta = jnp.sum(grad_solved[h] * rest, axis=-1, keepdims=True) + jnp.sum(
                grad_strict[h] * gram[h], axis=-1, keepdims=True
            )
            bw = beta_wide[:, h : h + 1]
            grad_beta = low(grad_beta).astype(jnp.float32) * bw * (1.0 - bw)
            glogit = glogit + jnp.where(lane == h, grad_beta, 0.0)
        gproj_ref[here, pl.ds(3 * wide, DK)] = low(glogit)
        for h in every:
            found, _, key_wide, scale, _ = ready[h]
            lanes = pl.ds(h * DK, DK)
            back_query = low(grad_query[h]).astype(jnp.float32) * DK**-0.5
            back_key = low(grad_key[h]).astype(jnp.float32)
            back_key = scale * (
                back_key - key_wide * jnp.sum(back_key * key_wide, axis=-1, keepdims=True)
            )
            back_value = low(grad_value[h]).astype(jnp.float32)
            for part, grad_active in enumerate((back_query, back_key, back_value)):
                window, weights, mixed, gate, _ = found[part]
                grad_conv = grad_active * (gate * (1.0 + mixed * (1.0 - gate)))
                columns = pl.ds(part * wide + h * DK, DK)
                tail = jnp.concatenate([grad_conv, after[:, columns]], axis=0)
                size = CHUNK + HEAD_ROOM
                total = grad_conv * weights[taps - 1]
                for back in range(1, taps):
                    ahead = pltpu.roll(tail, size - back, 0)[:CHUNK]
                    total = total + ahead * weights[taps - 1 - back]
                gproj_ref[here, columns] = low(total)
                after[:, columns] = grad_conv[:HEAD_ROOM]
                for back in range(taps):
                    shifted = pltpu.roll(window, back, 0)[HEAD_ROOM:] if back else window[HEAD_ROOM:]
                    spot = pl.ds(part * taps + taps - 1 - back, 1)
                    gtable_ref[spot, lanes] += jnp.sum(grad_conv * shifted, axis=0, keepdims=True)
        return 0

    lax.fori_loop(0, count, step, 0)


def in_vmem(count):
    return [pl.BlockSpec(memory_space=pltpu.VMEM)] * count


def mix_forward(proj, logits, table, gain):
    length = proj.shape[0]
    heads = table.shape[1] // DK
    taps = table.shape[0] // 3
    count = length // CHUNK
    wide = heads * DK
    shape = jax.ShapeDtypeStruct
    return pl.pallas_call(
        functools.partial(forward_kernel, heads, taps),
        out_shape=(
            shape((length, wide), jnp.bfloat16),
            shape((length, wide), jnp.bfloat16),
            shape((length, wide), jnp.bfloat16),
            shape((count, heads, CHUNK, CHUNK), jnp.bfloat16),
            shape((count, heads, DK, DK), jnp.bfloat16),
        ),
        in_specs=in_vmem(4),
        out_specs=tuple(in_vmem(5)),
        scratch_shapes=[pltpu.VMEM((heads, DK, DK), jnp.float32)],
        compiler_params=pltpu.CompilerParams(vmem_limit_bytes=40 * 2**20),
        cost_estimate=pl.CostEstimate(
            flops=length * heads * DK * 8000, bytes_accessed=16 * length * wide, transcendentals=3 * length * wide
        ),
        name="mix_forward",
    )(proj, logits, table, gain)


def mix_backward(proj, logits, table, gain, raw, fresh, solved, states, grad):
    length = proj.shape[0]
    heads = table.shape[1] // DK
    taps = table.shape[0] // 3
    wide = heads * DK
    shape = jax.ShapeDtypeStruct
    return pl.pallas_call(
        functools.partial(backward_kernel, heads, taps),
        out_shape=(
            shape((length, 3 * wide + DK), jnp.bfloat16),
            shape((3 * taps, wide), jnp.float32),
            shape((1, DK), jnp.float32),
        ),
        in_specs=in_vmem(9),
        out_specs=tuple(in_vmem(3)),
        scratch_shapes=[
            pltpu.VMEM((heads, DK, DK), jnp.float32),
            pltpu.VMEM((HEAD_ROOM, 3 * wide), jnp.float32),
        ],
        compiler_params=pltpu.CompilerParams(vmem_limit_bytes=40 * 2**20),
        cost_estimate=pl.CostEstimate(
            flops=length * heads * DK * 10000, bytes_accessed=26 * length * wide, transcendentals=3 * length * wide
        ),
        name="mix_backward",
    )(proj, logits, table, gain, raw, fresh, solved, states, grad)


def neighbours():
    me = lax.axis_index("seq")
    return me, me + 1 - 2 * (me % 2), me + 2 - 4 * (me // 2), 3 - me


def greet(across, along):
    barrier = pltpu.get_barrier_semaphore()
    for other in (across, along):
        pl.semaphore_signal(
            barrier, inc=1, device_id={"seq": other}, device_id_type=pl.DeviceIdType.MESH
        )
    pl.semaphore_wait(barrier, 2)


def remote(source, target, send, arrive, slot, other):
    return pltpu.make_async_remote_copy(
        src_ref=source,
        dst_ref=target,
        send_sem=send.at[slot],
        recv_sem=arrive.at[slot],
        device_id={"seq": other},
        device_id_type=pl.DeviceIdType.MESH,
    )


def half_of(rows):
    return (rows // 2 + 15) // 16 * 16


def gather_start(source, target, near, send, arrive, keep):
    me, across, along, _ = near
    own = pltpu.make_async_copy(source, target.at[me], keep)
    first = remote(source, target.at[me], send, arrive, 0, across)
    second = remote(source, target.at[me], send, arrive, 1, along)
    own.start()
    first.start()
    second.start()
    return own, first, second


def gather_finish(started, target, near, send, arrive):
    _, across, along, _ = near
    own, first, second = started
    rows = target.shape[1]
    split = half_of(rows)
    head, rest = pl.ds(0, split), pl.ds(split, rows - split)
    first.wait_recv()
    third = remote(target.at[across, head], target.at[across, head], send, arrive, 2, along)
    third.start()
    second.wait_recv()
    fourth = remote(target.at[along, rest], target.at[along, rest], send, arrive, 3, across)
    fourth.start()
    third.wait_recv()
    fourth.wait_recv()
    for copy in (first, second, third, fourth):
        copy.wait_send()
    own.wait()


def gather_kernel(count, *refs):
    sources, targets = refs[:count], refs[count : 2 * count]
    send, arrive, keep = refs[2 * count :]
    near = neighbours()
    greet(near[1], near[2])
    started = [
        gather_start(sources[i], targets[i], near, send.at[i], arrive.at[i], keep.at[i])
        for i in range(count)
    ]
    for i in range(count):
        gather_finish(started[i], targets[i], near, send.at[i], arrive.at[i])


def seq_gather(name, number, *blocks):
    count = len(blocks)
    side = lax.axis_size("seq")
    if side != 4:
        return [lax.all_gather(block, "seq", axis=0) for block in blocks]
    moved = sum(block.size for block in blocks)
    return pl.pallas_call(
        functools.partial(gather_kernel, count),
        out_shape=[
            jax.ShapeDtypeStruct((side,) + block.shape, block.dtype) for block in blocks
        ],
        in_specs=[pl.BlockSpec(memory_space=pl.ANY)] * count,
        out_specs=[pl.BlockSpec(memory_space=pl.ANY)] * count,
        scratch_shapes=[
            pltpu.SemaphoreType.DMA((count, 4)),
            pltpu.SemaphoreType.DMA((count, 4)),
            pltpu.SemaphoreType.DMA((count,)),
        ],
        compiler_params=pltpu.CompilerParams(collective_id=number, has_side_effects=True),
        cost_estimate=pl.CostEstimate(flops=0, bytes_accessed=160 * moved, transcendentals=0),
        name=name,
    )(*blocks)


def start_kernel(
    source_ref, small_ref, sources, smalls,
    send, arrive, keep, send_z, arrive_z, keep_z,
):
    near = neighbours()
    _, across, along, _ = near
    here, count = lax.axis_index("fsdp"), lax.axis_size("fsdp")
    sibling = here + 1 - 2 * (here % 2)
    others = [(here + 2 * step) % count for step in range(1, count // 2)]
    barrier = pltpu.get_barrier_semaphore()
    peers = [{"seq": across}, {"seq": along}, {"fsdp": sibling}]
    peers += [{"fsdp": other} for other in others]
    for peer in peers:
        pl.semaphore_signal(barrier, inc=1, device_id=peer, device_id_type=pl.DeviceIdType.MESH)
    pl.semaphore_wait(barrier, len(peers))

    def send_to(source, target, row, slot, other):
        return pltpu.make_async_remote_copy(
            src_ref=source,
            dst_ref=target,
            send_sem=send_z.at[row, slot],
            recv_sem=arrive_z.at[row, slot],
            device_id={"fsdp": other},
            device_id_type=pl.DeviceIdType.MESH,
        )

    flow = [(small_ref, smalls)]
    first = []
    for row, (source, target) in enumerate(flow):
        own = pltpu.make_async_copy(source, target.at[here], keep_z.at[row])
        own.start()
        copies = [send_to(source, target.at[here], row, 0, sibling)]
        copies += [
            send_to(source, target.at[here], row, 1 + i, other) for i, other in enumerate(others)
        ]
        for copy in copies:
            copy.start()
        first.append((own, copies))
    started = [
        gather_start(block, target, near, send.at[i], arrive.at[i], keep.at[i])
        for i, (block, target) in enumerate([(source_ref, sources)])
    ]
    gather_finish(started[0], sources, near, send.at[0], arrive.at[0])
    for row, (source, target) in enumerate(flow):
        own, copies = first[row]
        passed = []
        for i in range(len(others)):
            copies[1 + i].wait_recv()
            origin = target.at[(here + count - 2 * (i + 1)) % count]
            passed.append(send_to(origin, origin, row, 1 + len(others) + i, sibling))
            passed[-1].start()
        copies[0].wait_recv()
        for copy in passed:
            copy.wait_recv()
        for copy in copies + passed:
            copy.wait_send()
        own.wait()


def start_gathers(source, small):
    side, count = lax.axis_size("seq"), lax.axis_size("fsdp")
    if side != 4:
        return (
            lax.all_gather(source, "seq", axis=0),
            lax.all_gather(small, "fsdp", axis=0),
        )
    slots = count - 1
    return pl.pallas_call(
        start_kernel,
        out_shape=[
            jax.ShapeDtypeStruct((many,) + block.shape, block.dtype)
            for block, many in ((source, side), (small, count))
        ],
        in_specs=[pl.BlockSpec(memory_space=pl.ANY)] * 2,
        out_specs=[pl.BlockSpec(memory_space=pl.ANY)] * 2,
        scratch_shapes=[
            pltpu.SemaphoreType.DMA((2, 4)),
            pltpu.SemaphoreType.DMA((2, 4)),
            pltpu.SemaphoreType.DMA((2,)),
            pltpu.SemaphoreType.DMA((2, slots)),
            pltpu.SemaphoreType.DMA((2, slots)),
            pltpu.SemaphoreType.DMA((2,)),
        ],
        compiler_params=pltpu.CompilerParams(collective_id=1, has_side_effects=True),
        cost_estimate=pl.CostEstimate(
            flops=0, bytes_accessed=160 * source.size, transcendentals=0
        ),
        name="start_gathers",
    )(source, small)


TILE = 256
STEP = 16


def reduce_rows_kernel(flip, gathers, epilogue, lefts, in_count, out_count, *refs):
    left_refs, right_ref, extra = refs[:lefts], refs[lefts], refs[lefts + 1 : in_count]
    outs = refs[in_count : in_count + out_count]
    far, wide_x, wide_y, own, get_a, get_b, get_x, get_y, send, arrive = refs[
        in_count + out_count : in_count + out_count + 10
    ]
    rest_refs = refs[in_count + out_count + 10 :]
    near = neighbours()
    me, across, along, opposite = near
    greet(across, along)
    rows, width = own.shape
    split = half_of(rows)
    head, rest = pl.ds(0, split), pl.ds(split, rows - split)

    def part(block, store):
        here = pl.ds(pl.multiple_of(block * rows, rows), rows)

        @pl.loop(0, width // TILE)
        def _(tile):
            columns = pl.ds(pl.multiple_of(tile * TILE, TILE), TILE)
            value, base = 0.0, 0
            for left_ref in left_refs:
                depth = pl.ds(base, left_ref.shape[1])
                if flip:
                    value = value + dotf(left_ref[here, :], right_ref[columns, depth], NT)
                else:
                    value = value + dotf(left_ref[here, :], right_ref[depth, columns], NN)
                base += left_ref.shape[1]
            store[:, columns] = value.astype(store.dtype)

    def add_into(store, base, source):
        @pl.loop(0, source.shape[0] // STEP)
        def _(index):
            start = pl.multiple_of(index * STEP, STEP)
            there = pl.ds(pl.multiple_of(base + start, STEP), STEP)
            total = store[there, :].astype(jnp.float32) + source[pl.ds(start, STEP), :].astype(
                jnp.float32
            )
            store[there, :] = low(total)

    part(opposite, far)
    copies = [
        remote(far.at[head], get_a, send, arrive, 0, across),
        remote(far.at[rest], get_b, send, arrive, 1, along),
    ]
    copies[0].start()
    copies[1].start()
    part(across, wide_x)
    copies.append(remote(wide_x.at[head], get_x.at[head], send, arrive, 2, across))
    copies[2].start()
    part(along, wide_y)
    copies.append(remote(wide_y.at[rest], get_y.at[rest], send, arrive, 3, along))
    copies[3].start()
    copies[0].wait_recv()
    add_into(wide_y, 0, get_a)
    copies.append(remote(wide_y.at[head], get_y.at[head], send, arrive, 4, along))
    copies[4].start()
    copies[1].wait_recv()
    add_into(wide_x, split, get_b)
    copies.append(remote(wide_x.at[rest], get_x.at[rest], send, arrive, 5, across))
    copies[5].start()
    part(me, own)
    for copy in copies[2:]:
        copy.wait_recv()
    epilogue_prepare = rest_refs[0] if gathers else None

    @pl.loop(0, rows // STEP)
    def _(index):
        here = pl.ds(pl.multiple_of(index * STEP, STEP), STEP)
        total = (
            own[here, :] + get_x[here, :].astype(jnp.float32) + get_y[here, :].astype(jnp.float32)
        )
        epilogue(index, here, total, extra, outs, epilogue_prepare)

    for copy in copies:
        copy.wait_send()
    if gathers:
        block, send_2, arrive_2, keep = rest_refs
        target = outs[0]
        started = gather_start(block, target, near, send_2, arrive_2, keep.at[0])
        gather_finish(started, target, near, send_2, arrive_2)


def rms_back(grad, values, gain):
    r = lax.rsqrt(jnp.mean(values * values, axis=-1, keepdims=True) + EPS)
    scaled = grad * gain
    change = r * (scaled - values * (r * r) * jnp.mean(scaled * values, axis=-1, keepdims=True))
    return change


def middle_epilogue(index, here, total, extra, outs, block):
    source_ref, gain_ref = extra
    middle = source_ref[here, :].astype(jnp.float32) + total
    outs[1][here, :] = middle
    r = lax.rsqrt(jnp.mean(middle * middle, axis=-1, keepdims=True) + EPS)
    block[here, :] = low(middle * r * gain_ref[...])


def branch_epilogue(index, here, total, extra, outs, block):
    middle_ref, upstream_ref, gain_ref = extra
    change = rms_back(total, middle_ref[here, :], gain_ref[...])
    grad = upstream_ref[here, :].astype(jnp.float32) + change
    outs[1][here, :] = grad
    block[here, :] = low(grad)


def input_epilogue(index, here, total, extra, outs, block):
    source_ref, carried_ref, gain_ref = extra
    change = rms_back(total, source_ref[here, :].astype(jnp.float32), gain_ref[...])
    outs[0][here, :] = carried_ref[here, :] + change


def fused_reduce(name, number, flip, gathers, epilogue, outs, lefts, right, *extra):
    side = lax.axis_size("seq")
    length = lefts[0].shape[0]
    rows = length // side
    width = right.shape[0] if flip else right.shape[1]
    split = half_of(rows)
    scratch = [
        pltpu.VMEM((rows, width), jnp.bfloat16),
        pltpu.VMEM((rows, width), jnp.bfloat16),
        pltpu.VMEM((rows, width), jnp.bfloat16),
        pltpu.VMEM((rows, width), jnp.float32),
        pltpu.VMEM((split, width), jnp.bfloat16),
        pltpu.VMEM((rows - split, width), jnp.bfloat16),
        pltpu.VMEM((rows, width), jnp.bfloat16),
        pltpu.VMEM((rows, width), jnp.bfloat16),
        pltpu.SemaphoreType.DMA((6,)),
        pltpu.SemaphoreType.DMA((6,)),
    ]
    out_specs = in_vmem(len(outs))
    if gathers:
        scratch += [
            pltpu.VMEM((rows, width), jnp.bfloat16),
            pltpu.SemaphoreType.DMA((4,)),
            pltpu.SemaphoreType.DMA((4,)),
            pltpu.SemaphoreType.DMA((1,)),
        ]
        out_specs[0] = pl.BlockSpec(memory_space=pl.ANY)
    return pl.pallas_call(
        functools.partial(
            reduce_rows_kernel,
            flip,
            gathers,
            epilogue,
            len(lefts),
            len(lefts) + 1 + len(extra),
            len(outs),
        ),
        out_shape=outs,
        in_specs=in_vmem(len(lefts) + 1 + len(extra)),
        out_specs=out_specs,
        scratch_shapes=scratch,
        compiler_params=pltpu.CompilerParams(
            collective_id=number, has_side_effects=True, vmem_limit_bytes=50 * 2**20
        ),
        cost_estimate=pl.CostEstimate(
            flops=2 * sum(left.size for left in lefts) * width,
            bytes_accessed=(320 if gathers else 160) * rows * width,
            transcendentals=0,
        ),
        name=name,
    )(*lefts, right, *extra)


def seq_sum(partial, side):
    block = low(partial).reshape(side, -1, partial.shape[-1])
    return lax.psum_scatter(block, "seq", scatter_dimension=0).astype(jnp.float32)


def out_and_norm(attn_in, weight, source, gain):
    side = lax.axis_size("seq")
    rows, width = source.shape
    if side != 4:
        middle = source.astype(jnp.float32) + seq_sum(dotf(attn_in, weight, NN), side)
        r = lax.rsqrt(jnp.mean(middle * middle, axis=-1, keepdims=True) + EPS)
        return lax.all_gather(low(middle * r * gain), "seq", axis=0), middle
    outs = (
        jax.ShapeDtypeStruct((side, rows, width), jnp.bfloat16),
        jax.ShapeDtypeStruct((rows, width), jnp.float32),
    )
    return fused_reduce(
        "out_and_norm", 2, False, True, middle_epilogue, outs, [attn_in], weight, source, gain
    )


def place_kernel(side, *refs):
    target_ref = refs[side]
    me = lax.axis_index("seq")
    for spot in range(side):

        @pl.when(me == spot)
        def _():
            for index in range(side):
                target_ref[index] = refs[index ^ spot][...].astype(target_ref.dtype)


def place(blocks, kind):
    side = len(blocks)
    rows, width = blocks[0].shape
    tile = 512
    return pl.pallas_call(
        functools.partial(place_kernel, side),
        grid=(width // tile,),
        out_shape=jax.ShapeDtypeStruct((side, rows, width), kind),
        in_specs=[pl.BlockSpec((rows, tile), lambda i: (0, i))] * side,
        out_specs=pl.BlockSpec((side, rows, tile), lambda i: (0, 0, i)),
        name="place",
    )(*blocks)


def swap(block, step):
    pairs = [(i, i ^ step) for i in range(lax.axis_size("seq"))]
    return lax.ppermute(block, "seq", pairs)


def branch_grad(grads, weight, middle, upstream, gain):
    side = lax.axis_size("seq")
    rows, width = middle.shape
    if side != 4:
        grad = jnp.concatenate(grads, axis=1)
        change = rms_back(seq_sum(dotf(grad, weight, NT), side), middle, gain)
        total = upstream.astype(jnp.float32) + change
        return lax.all_gather(low(total), "seq", axis=0), total
    outs = (
        jax.ShapeDtypeStruct((side, rows, width), jnp.bfloat16),
        jax.ShapeDtypeStruct((rows, width), jnp.float32),
    )
    return fused_reduce(
        "branch_grad", 4, True, True, branch_epilogue, outs, grads, weight, middle, upstream, gain
    )


def input_grad(grad, weight, source, carried, gain):
    side = lax.axis_size("seq")
    if side != 4:
        return carried + rms_back(
            seq_sum(dotf(grad, weight[:, : grad.shape[1]], NT), side), source.astype(jnp.float32), gain
        )
    outs = (jax.ShapeDtypeStruct(carried.shape, jnp.float32),)
    return fused_reduce(
        "input_grad", 5, True, False, input_epilogue, outs, [grad], weight, source, carried, gain
    )[0]


def signal_all(peers):
    barrier = pltpu.get_barrier_semaphore()
    for peer in peers:
        pl.semaphore_signal(barrier, inc=1, device_id=peer, device_id_type=pl.DeviceIdType.MESH)
    pl.semaphore_wait(barrier, len(peers))


def send_share(row, first, where, mine, boxes, send, arrive):
    axis, spot, size = where
    copies = []
    for step in range(1, size):
        copies.append(
            pltpu.make_async_remote_copy(
                src_ref=mine.at[row],
                dst_ref=boxes.at[row, spot],
                send_sem=send.at[first + step - 1],
                recv_sem=arrive.at[first + step - 1],
                device_id={axis: (spot + step) % size},
                device_id_type=pl.DeviceIdType.MESH,
            )
        )
        copies[-1].start()
    boxes[row, spot] = mine[row]
    return copies


def add_shares(row, size, copies, boxes):
    for copy in copies:
        copy.wait()
    total = boxes[row, 0]
    for index in range(1, size):
        total = total + boxes[row, index]
    return total


def gather_total_kernel(count, *refs):
    sources, value_ref = refs[:count], refs[count]
    targets, total_ref = refs[count + 1 : 2 * count + 1], refs[2 * count + 1]
    mine, boxes, send_t, arrive_t, send, arrive, keep = refs[2 * count + 2 :]
    near = neighbours()
    spots = [(axis, lax.axis_index(axis), lax.axis_size(axis)) for axis in ("seq", "fsdp")]
    signal_all(
        [{axis: (spot + step) % size} for axis, spot, size in spots for step in range(1, size)]
    )
    mine[0] = value_ref[...]
    copies = send_share(0, 0, spots[0], mine, boxes, send_t, arrive_t)
    mine[1] = add_shares(0, spots[0][2], copies, boxes)
    copies = send_share(1, spots[0][2] - 1, spots[1], mine, boxes, send_t, arrive_t)
    started = [
        gather_start(sources[i], targets[i], near, send.at[i], arrive.at[i], keep.at[i])
        for i in range(count)
    ]
    for i in range(count):
        gather_finish(started[i], targets[i], near, send.at[i], arrive.at[i])
    total_ref[...] = add_shares(1, spots[1][2], copies, boxes)


def gather_total(value, *blocks):
    side, f_count = lax.axis_size("seq"), lax.axis_size("fsdp")
    if side != 4:
        summed = lax.psum(value, ("fsdp", "seq"))
        return [lax.all_gather(block, "seq", axis=0) for block in blocks] + [summed]
    count, peers = len(blocks), side + f_count - 2
    moved = sum(block.size for block in blocks)
    return pl.pallas_call(
        functools.partial(gather_total_kernel, count),
        out_shape=[jax.ShapeDtypeStruct((side,) + b.shape, b.dtype) for b in blocks]
        + [jax.ShapeDtypeStruct(value.shape, value.dtype)],
        in_specs=[pl.BlockSpec(memory_space=pl.ANY)] * count + in_vmem(1),
        out_specs=[pl.BlockSpec(memory_space=pl.ANY)] * count + in_vmem(1),
        scratch_shapes=[
            pltpu.VMEM((3,) + value.shape, value.dtype),
            pltpu.VMEM((2, max(side, f_count)) + value.shape, value.dtype),
            pltpu.SemaphoreType.DMA((peers,)),
            pltpu.SemaphoreType.DMA((peers,)),
            pltpu.SemaphoreType.DMA((count, 4)),
            pltpu.SemaphoreType.DMA((count, 4)),
            pltpu.SemaphoreType.DMA((count,)),
        ],
        compiler_params=pltpu.CompilerParams(collective_id=7, has_side_effects=True),
        cost_estimate=pl.CostEstimate(flops=0, bytes_accessed=160 * moved, transcendentals=0),
        name="gather_total",
    )(*blocks, value)


def pick_kernel(side, share, source_ref, target_ref):
    me = lax.axis_index("seq")
    count = target_ref.shape[1] // share
    for index in range(side):

        @pl.when(me == index)
        def _():
            pieces = [
                source_ref[:, pl.ds((k * side + index) * share, share)].astype(jnp.float32)
                for k in range(count)
            ]
            target_ref[...] = low(jnp.concatenate(pieces, axis=1))


def pick_columns(weight, share):
    side = lax.axis_size("seq")
    rows, width = weight.shape
    tile = 32
    return pl.pallas_call(
        functools.partial(pick_kernel, side, share),
        grid=(rows // tile,),
        out_shape=jax.ShapeDtypeStruct((rows, width // side), weight.dtype),
        in_specs=[pl.BlockSpec((tile, width), lambda i: (i, 0))],
        out_specs=pl.BlockSpec((tile, width // side), lambda i: (i, 0)),
        name="pick_columns",
    )(weight)


def spread_kernel(side, share, *refs):
    gate_refs, (up_ref, weight_ref, target_ref, total_ref) = refs[:side], refs[side:]
    count = up_ref.shape[2] // share
    me = lax.axis_index("seq")
    half = target_ref.shape[1] // 2

    def place(pieces, base):
        grad = jnp.concatenate([piece.astype(jnp.float32) for piece in pieces], axis=1)
        target_ref[:, pl.ds(base, half)] = grad
        weight = weight_ref[:, pl.ds(base, half)].astype(jnp.float32)
        return jnp.sum(grad * weight, axis=1, keepdims=True)

    spans = [(pl.ds(k * share, share), index) for k in range(count) for index in range(side)]
    total = place([up_ref[index, :, span] for span, index in spans], half)
    for spot in range(side):

        @pl.when(me == spot)
        def _():
            whole = total + place([gate_refs[index ^ spot][:, span] for span, index in spans], 0)
            total_ref[...] = jnp.broadcast_to(whole, total_ref.shape)


def spread_columns(gates, up, weight, share):
    side, rows, width = up.shape
    tile = 32
    by_row = pl.BlockSpec((tile, 2 * width * side), lambda i: (i, 0))
    return pl.pallas_call(
        functools.partial(spread_kernel, side, share),
        grid=(rows // tile,),
        out_shape=(
            jax.ShapeDtypeStruct((rows, 2 * width * side), jnp.float32),
            jax.ShapeDtypeStruct((rows, DK), jnp.float32),
        ),
        in_specs=[pl.BlockSpec((tile, width), lambda i: (i, 0))] * side
        + [pl.BlockSpec((side, tile, width), lambda i: (0, i, 0)), by_row],
        out_specs=(by_row, pl.BlockSpec((tile, DK), lambda i: (i, 0))),
        name="spread_columns",
    )(*gates, up, weight)


def assemble_kernel(side, wide, grad_ref, weight_ref, target_ref, total_ref):
    total = 0.0
    for part in range(3):
        for index in range(side):
            columns = pl.ds((part * side + index) * wide, wide)
            grad = grad_ref[index, :, pl.ds(part * wide, wide)].astype(jnp.float32)
            target_ref[:, columns] = grad
            weight = weight_ref[:, columns].astype(jnp.float32)
            total = total + jnp.sum(grad * weight, axis=1, keepdims=True)
    total_ref[...] = jnp.broadcast_to(total, total_ref.shape)


def assemble_columns(grad, weight, wide):
    side, rows, depth = grad.shape
    tile = 32
    by_row = pl.BlockSpec((tile, weight.shape[1]), lambda i: (i, 0))
    return pl.pallas_call(
        functools.partial(assemble_kernel, side, wide),
        grid=(rows // tile,),
        out_shape=(
            jax.ShapeDtypeStruct(weight.shape, jnp.float32),
            jax.ShapeDtypeStruct((rows, DK), jnp.float32),
        ),
        in_specs=[pl.BlockSpec((side, tile, depth), lambda i: (0, i, 0)), by_row],
        out_specs=(by_row, pl.BlockSpec((tile, DK), lambda i: (i, 0))),
        name="assemble_columns",
    )(grad, weight)


def fsdp_sum(term):
    return lax.psum_scatter(low(term), "fsdp", scatter_dimension=0, tiled=True)


def per_device(
    inputs,
    cotangent,
    norm1_gain,
    w_qkv,
    w_beta,
    conv_weight,
    out_gain,
    w_out,
    norm2_gain,
    w_gate_up,
    w_down,
):
    side = lax.axis_size("seq")
    s = lax.axis_index("seq")
    shape = inputs.shape
    width = shape[2]
    source = inputs.reshape(-1, width)
    upstream = cotangent.reshape(-1, width)
    length = source.shape[0] * side
    heads = H // side
    wide = heads * DK
    rows = w_qkv.shape[0]
    share = w_down.shape[0] // side
    taps = conv_weight.shape[1] // 3

    f_count = lax.axis_size("fsdp")
    depth = 3 * wide + DK
    homes = [
        (f * side + i, (side * (f % 2) + i) * side + f // 2)
        for f in range(f_count)
        for i in range(side)
    ]
    strip = rows // side

    def everywhere(block):
        return lax.all_gather(block, "fsdp", axis=0, tiled=True)

    parts = [
        lax.dynamic_slice_in_dim(w_qkv, part * width + s * wide, wide, 1) for part in range(3)
    ]
    beta_part = lax.dynamic_slice_in_dim(w_beta, s * heads, heads, 1)
    parts.append(jnp.pad(beta_part, ((0, 0), (0, DK - heads))))
    qkv_part = everywhere(jnp.concatenate(parts, axis=1))
    small = jnp.concatenate([norm1_gain[None], norm2_gain[None], conv_weight.T], axis=0)
    small = jnp.pad(small, ((0, 16 - small.shape[0]), (0, 0)))
    piece = lax.dynamic_slice_in_dim(w_out, s * strip, strip, 0)
    piece = lax.ppermute(piece, ("fsdp", "seq"), homes)
    source_all, small = start_gathers(source, small)
    sent, source_all = lax.optimization_barrier((upstream, source_all))
    upstreams = [upstream] + [swap(sent, step) for step in range(1, side)]
    out_part = everywhere(piece)
    small = small.transpose(1, 0, 2).reshape(small.shape[1], width).astype(jnp.float32)
    gain_first = small[0:1]
    gain_second = small[1:2]
    table = lax.dynamic_slice_in_dim(small[2 : 2 + 3 * taps], s * wide, wide, 1)
    gain_heads = out_gain.astype(jnp.float32)[None]
    source_all = source_all.reshape(length, width).astype(jnp.float32)

    picked = pick_columns(w_gate_up, share)
    gate_up_part = everywhere(picked)
    down_part = everywhere(lax.dynamic_slice_in_dim(w_down, s * share, share, 0))

    normed_first = low(
        source_all
        * lax.rsqrt(jnp.mean(source_all * source_all, axis=-1, keepdims=True) + EPS)
        * gain_first
    )
    projected = low(dotf(normed_first, qkv_part[:, : 3 * wide], NN))
    beta_logits = dotf(normed_first, qkv_part[:, 3 * wide : depth], NN)
    attn_in, *kept = mix_forward(projected, beta_logits, table, gain_heads)
    attn_in, *upstreams = lax.optimization_barrier((attn_in, *upstreams))
    upstream_all = place(upstreams, jnp.bfloat16).reshape(length, width)
    ffn_in, middle = out_and_norm(attn_in, out_part, source, gain_second)
    ffn_in = ffn_in.reshape(length, width)
    gate_up = dotf(ffn_in, gate_up_part, NN)
    hidden_width = gate_up.shape[1] // 2
    gate = gate_up[:, :hidden_width]
    upward = gate_up[:, hidden_width:]
    sigma = jax.nn.sigmoid(gate)
    hidden = low(gate * sigma * upward)

    down_term = low(dotf(hidden, upstream_all, TN))
    grad_down = fsdp_sum(down_term)
    hidden, _ = lax.optimization_barrier((hidden, down_term))
    result = low(dotf(hidden, down_part, NN)).reshape((side, -1, width))
    upstream_all, result = lax.optimization_barrier((upstream_all, result))
    swapped = [
        swap(lax.dynamic_index_in_dim(result, s ^ step, 0, keepdims=False), step)
        for step in range(1, side)
    ]
    swapped.insert(0, lax.dynamic_index_in_dim(result, s, 0, keepdims=False))
    grad_hidden = dotf(upstream_all, down_part, NT)
    grad_gate = low(grad_hidden * upward * sigma * (1.0 + gate * (1.0 - sigma)))
    grad_up = low(grad_hidden * gate * sigma)
    grad_gate, *swapped[1:3] = lax.optimization_barrier((grad_gate, *swapped[1:3]))
    gate_term = low(dotf(ffn_in, grad_gate, TN))
    grad_up, swapped[3:], _ = lax.optimization_barrier((grad_up, swapped[3:], gate_term))
    up_term = low(dotf(ffn_in, grad_up, TN))
    gate_sum = fsdp_sum(gate_term)
    up_sum = fsdp_sum(up_term)
    grad_gate, grad_up, _, *swapped = lax.optimization_barrier(
        (grad_gate, grad_up, up_term, *swapped)
    )
    output = low(middle + sum(block.astype(jnp.float32) for block in swapped))
    grad_branch, grad_middle = branch_grad(
        [grad_gate, grad_up], gate_up_part, middle, upstream, gain_second
    )
    grad_branch, grad_down, gate_sum = lax.optimization_barrier(
        (grad_branch, grad_down, gate_sum)
    )
    grad_branch = grad_branch.reshape(length, width)
    downs = [grad_down] + [swap(grad_down, step) for step in range(1, side)]
    gates = [gate_sum] + [swap(gate_sum, step) for step in range(1, side)]

    out_term = low(dotf(attn_in, grad_branch, TN))
    out_sum = fsdp_sum(out_term)
    grad_attn_in, _ = lax.optimization_barrier((dotf(grad_branch, out_part, NT), out_term))
    grad_proj, grad_table, grad_gain_heads = mix_backward(
        projected, beta_logits, table, gain_heads, *kept, grad_attn_in
    )
    grad_proj, up_sum, *downs = lax.optimization_barrier((grad_proj, up_sum, *downs))
    grad_qkv = low(dotf(normed_first, grad_proj, TN))
    grad_qkv = lax.dynamic_update_slice(
        grad_qkv, low(grad_table.T), (s * wide, 3 * wide + heads)
    )
    grad_proj, grad_qkv, *gates = lax.optimization_barrier((grad_proj, grad_qkv, *gates))
    grad_qkv = fsdp_sum(grad_qkv)
    grad_input = input_grad(grad_proj, qkv_part, source, grad_middle, gain_first)
    out_sum = lax.ppermute(out_sum, ("fsdp", "seq"), [(b, a) for a, b in homes])
    up_sum, grad_input = lax.optimization_barrier((up_sum, grad_input))
    up_sum, grad_w_out, grad_out_gain = gather_total(
        jnp.broadcast_to(grad_gain_heads, (8, DK)), up_sum, out_sum
    )
    (grad_qkv,) = seq_gather("gather_qkv", 9, grad_qkv)
    grad_down = place(downs, jnp.float32).reshape(side * share, width)
    grad_w_qkv, first_total = assemble_columns(grad_qkv, w_qkv, wide)
    grad_w_gate_up, second_total = spread_columns(gates, up_sum, w_gate_up, share)
    sides = grad_qkv[:, :, 3 * wide :].astype(jnp.float32)
    grad_w_beta = jnp.concatenate([sides[i, :, :heads] for i in range(side)], axis=1)
    grad_conv = jnp.sum(sides[:, :, heads : heads + 3 * taps], axis=0)
    first_total = first_total[:, 0] + jnp.sum(
        w_beta.astype(jnp.float32) * grad_w_beta, axis=1
    )
    return (
        output.reshape(shape),
        grad_input.reshape(shape),
        first_total / norm1_gain.astype(jnp.float32),
        grad_w_qkv,
        grad_w_beta,
        grad_conv,
        grad_out_gain[0],
        grad_w_out.reshape(rows, width).astype(jnp.float32),
        second_total[:, 0] / norm2_gain.astype(jnp.float32),
        grad_w_gate_up,
        grad_down,
    )


def solution(mesh):
    by_row = P("fsdp", None)
    tokens = P("fsdp", "seq", None)
    specs = (tokens, tokens, P("fsdp"), by_row, by_row, by_row, P(), by_row, P("fsdp"))
    specs = specs + (by_row, by_row)
    return jax.shard_map(per_device, mesh=mesh, in_specs=specs, out_specs=specs, check_vma=False)
```

```python
import functools

import jax
import jax.numpy as jnp
from jax import lax
from jax.experimental import pallas as pl
from jax.experimental.pallas import tpu as pltpu
from jax.sharding import PartitionSpec as P

H = 16
DK = 128
EPS = 1e-06
CHUNK = 128
HEAD_ROOM = 8


def dotf(left, right, dims):
    return lax.dot_general(left, right, (dims, ((), ())), preferred_element_type=jnp.float32)


NN = ((1,), (0,))
NT = ((1,), (1,))
TN = ((0,), (0,))


def low(value):
    return value.astype(jnp.bfloat16)


def square_iota(axis):
    return lax.broadcasted_iota(jnp.int32, (CHUNK, CHUNK), axis)


def sigmoid(value):
    return 1.0 / (1.0 + jnp.exp(-value))


def conv_chunk(window, taps, count):
    mixed = window[HEAD_ROOM:] * taps[count - 1]
    for back in range(1, count):
        mixed = mixed + pltpu.roll(window, back, 0)[HEAD_ROOM:] * taps[count - 1 - back]
    return mixed


def window_of(ahead_ref, proj_ref, chunk, column):
    lanes = pl.ds(column, DK)
    before = ahead_ref[:, lanes].astype(jnp.float32)[8:]
    before = jnp.where(chunk > 0, before, 0.0)
    return jnp.concatenate([before, proj_ref[:, lanes].astype(jnp.float32)], axis=0)


def head_inputs(ahead_ref, proj_ref, table_ref, chunk, head, heads, taps):
    wide = heads * DK
    found = []
    for part in range(3):
        window = window_of(ahead_ref, proj_ref, chunk, part * wide + head * DK)
        weights = [
            table_ref[pl.ds(part * taps + tap, 1), pl.ds(head * DK, DK)] for tap in range(taps)
        ]
        mixed = conv_chunk(window, weights, taps)
        gate = sigmoid(mixed)
        found.append((window, weights, mixed, gate, mixed * gate))
    active_key = found[1][4]
    scale = lax.rsqrt(jnp.sum(active_key * active_key, axis=-1, keepdims=True) + EPS)
    key = active_key * scale
    return found, found[0][4] * DK**-0.5, key, scale, found[2][4]


def inverses_of(stricts):
    row, column = square_iota(0), square_iota(1)
    eye = (row == column).astype(jnp.float32)
    solved = [eye - jnp.where(row // 2 == column // 2, strict, 0.0) for strict in stricts]
    half = 2
    while half < CHUNK:
        below = (row // (2 * half) == column // (2 * half)) & (row // half != column // half)
        off = [low(jnp.where(below, strict, 0.0)) for strict in stricts]
        known = [low(item) for item in solved]
        first = [low(dotf(k, o, NN)) for k, o in zip(known, off)]
        second = [dotf(p, k, NN) for p, k in zip(first, known)]
        solved = [item - change for item, change in zip(solved, second)]
        half *= 2
    return [low(item) for item in solved]


def forward_kernel(
    heads, taps, ahead_ref, proj_ref, logit_ref, table_ref, gain_ref,
    normed_ref, raw_ref, fresh_ref, solve_ref, state_ref, carry,
):
    every = range(heads)
    chunk = pl.program_id(0)

    @pl.when(chunk == 0)
    def _():
        carry[...] = jnp.zeros_like(carry)

    row, column = square_iota(0), square_iota(1)
    beta_all = low(sigmoid(logit_ref[...])).astype(jnp.float32)
    beta = [beta_all[:, h : h + 1] for h in every]
    ready = [head_inputs(ahead_ref, proj_ref, table_ref, chunk, h, heads, taps) for h in every]
    query = [low(item[1]) for item in ready]
    key = [low(item[2]) for item in ready]
    value = [low(item[4]) for item in ready]
    gram = [dotf(key[h], key[h], NT) for h in every]
    score = [dotf(query[h], key[h], NT) for h in every]
    strict = [jnp.where(row > column, gram[h] * beta[h], 0.0) for h in every]
    within = [low(jnp.where(row >= column, score[h], 0.0)) for h in every]
    solved = inverses_of(strict)
    state = [carry[h] for h in every]
    state_low = [low(item) for item in state]
    recalled = [dotf(key[h], state_low[h], NN) for h in every]
    rest = [low(beta[h] * (value[h].astype(jnp.float32) - recalled[h])) for h in every]
    fresh = [low(dotf(solved[h], rest[h], NN)) for h in every]
    grown = [dotf(key[h], fresh[h], TN) for h in every]
    for h in every:
        carry[h] = state[h] + grown[h]
    past = [dotf(query[h], state_low[h], NN) for h in every]
    inner = [dotf(within[h], fresh[h], NN) for h in every]
    for h in every:
        lanes = pl.ds(h * DK, DK)
        raw = low(past[h] + inner[h])
        wide_raw = raw.astype(jnp.float32)
        normed = wide_raw * lax.rsqrt(
            jnp.mean(wide_raw * wide_raw, axis=-1, keepdims=True) + EPS
        )
        normed_ref[:, lanes] = low(normed * gain_ref[...])
        raw_ref[:, lanes] = raw
        fresh_ref[:, lanes] = fresh[h]
        solve_ref[0, h] = solved[h]
        state_ref[0, h] = state_low[h]


def backward_kernel(
    heads, taps, ahead_ref, proj_ref, logit_ref, table_ref, gain_ref, raw_ref, fresh_ref, solve_ref,
    state_ref, grad_ref, gproj_ref, gtable_ref, ggain_ref, carry, after,
):
    wide = heads * DK
    every = range(heads)
    chunk = pl.num_programs(0) - 1 - pl.program_id(0)

    @pl.when(pl.program_id(0) == 0)
    def _():
        carry[...] = jnp.zeros_like(carry)
        after[...] = jnp.zeros_like(after)
        gtable_ref[...] = jnp.zeros_like(gtable_ref)
        ggain_ref[...] = jnp.zeros_like(ggain_ref)

    row, column = square_iota(0), square_iota(1)
    beta_wide = sigmoid(logit_ref[...])
    beta_all = low(beta_wide).astype(jnp.float32)
    beta = [beta_all[:, h : h + 1] for h in every]
    lane = lax.broadcasted_iota(jnp.int32, (CHUNK, DK), 1)
    ready = [head_inputs(ahead_ref, proj_ref, table_ref, chunk, h, heads, taps) for h in every]
    query = [low(item[1]) for item in ready]
    key = [low(item[2]) for item in ready]
    value = [low(item[4]) for item in ready]
    grad_out = []
    for h in every:
        lanes = pl.ds(h * DK, DK)
        raw = raw_ref[:, lanes].astype(jnp.float32)
        grad_normed = grad_ref[:, lanes].astype(jnp.float32)
        r = lax.rsqrt(jnp.mean(raw * raw, axis=-1, keepdims=True) + EPS)
        scaled = grad_normed * gain_ref[...]
        mean = jnp.mean(scaled * raw, axis=-1, keepdims=True)
        grad_out.append(low(r * (scaled - raw * (r * r) * mean)))
        ggain_ref[...] += jnp.sum(grad_normed * raw * r, axis=0, keepdims=True)
    state = [state_ref[0, h] for h in every]
    solved = [solve_ref[0, h] for h in every]
    fresh = [fresh_ref[:, pl.ds(h * DK, DK)] for h in every]
    later = [carry[h] for h in every]
    later_low = [low(item) for item in later]
    score = [dotf(query[h], key[h], NT) for h in every]
    onward = [dotf(key[h], later_low[h], NN) for h in every]
    within = [low(jnp.where(row >= column, item, 0.0)) for item in score]
    grad_fresh = [low(dotf(within[h], grad_out[h], TN) + onward[h]) for h in every]
    grad_solved = [dotf(solved[h], grad_fresh[h], TN) for h in every]
    grad_value = [beta[h] * grad_solved[h] for h in every]
    grad_rest = [low(item) for item in grad_value]
    asked = [dotf(query[h], grad_out[h], TN) for h in every]
    taken = [dotf(key[h], grad_rest[h], TN) for h in every]
    for h in every:
        carry[h] = later[h] + asked[h] - taken[h]
    gram = [dotf(key[h], key[h], NT) for h in every]
    recalled = [dotf(key[h], state[h], NN) for h in every]
    product = [dotf(grad_out[h], fresh[h], NT) for h in every]
    cross = [dotf(low(grad_solved[h]), fresh[h], NT) for h in every]
    grad_within = [low(jnp.where(row >= column, item, 0.0)) for item in product]
    grad_strict = [jnp.where(row > column, -item, 0.0) for item in cross]
    mixing = [low(beta[h] * grad_strict[h]) for h in every]
    grad_query = [
        dotf(grad_out[h], state[h], NT) + dotf(grad_within[h], key[h], NN) for h in every
    ]
    grad_key = [
        dotf(grad_within[h], query[h], TN)
        + dotf(fresh[h], later_low[h], NT)
        - dotf(grad_rest[h], state[h], NT)
        + dotf(mixing[h], key[h], NN)
        + dotf(mixing[h], key[h], TN)
        for h in every
    ]
    glogit = jnp.zeros((CHUNK, DK), jnp.float32)
    for h in every:
        rest = value[h].astype(jnp.float32) - recalled[h]
        grad_beta = jnp.sum(grad_solved[h] * rest, axis=-1, keepdims=True) + jnp.sum(
            grad_strict[h] * gram[h], axis=-1, keepdims=True
        )
        bw = beta_wide[:, h : h + 1]
        grad_beta = low(grad_beta).astype(jnp.float32) * bw * (1.0 - bw)
        glogit = glogit + jnp.where(lane == h, grad_beta, 0.0)
    gproj_ref[:, pl.ds(3 * wide, DK)] = low(glogit)
    for h in every:
        found, _, key_wide, scale, _ = ready[h]
        lanes = pl.ds(h * DK, DK)
        back_query = low(grad_query[h]).astype(jnp.float32) * DK**-0.5
        back_key = low(grad_key[h]).astype(jnp.float32)
        back_key = scale * (
            back_key - key_wide * jnp.sum(back_key * key_wide, axis=-1, keepdims=True)
        )
        back_value = low(grad_value[h]).astype(jnp.float32)
        for part, grad_active in enumerate((back_query, back_key, back_value)):
            window, weights, mixed, gate, _ = found[part]
            grad_conv = grad_active * (gate * (1.0 + mixed * (1.0 - gate)))
            columns = pl.ds(part * wide + h * DK, DK)
            tail = jnp.concatenate([grad_conv, after[:, columns]], axis=0)
            size = CHUNK + HEAD_ROOM
            total = grad_conv * weights[taps - 1]
            for back in range(1, taps):
                ahead = pltpu.roll(tail, size - back, 0)[:CHUNK]
                total = total + ahead * weights[taps - 1 - back]
            gproj_ref[:, columns] = low(total)
            after[:, columns] = grad_conv[:HEAD_ROOM]
            for back in range(taps):
                shifted = pltpu.roll(window, back, 0)[HEAD_ROOM:] if back else window[HEAD_ROOM:]
                spot = pl.ds(part * taps + taps - 1 - back, 1)
                gtable_ref[spot, lanes] += jnp.sum(grad_conv * shifted, axis=0, keepdims=True)


def in_vmem(count):
    return [pl.BlockSpec(memory_space=pltpu.VMEM)] * count


def mix_specs(heads, wide, turn):
    ratio = CHUNK // 16
    proj = [
        pl.BlockSpec((16, 3 * wide), lambda i: (jnp.maximum(turn(i) * ratio - 1, 0), 0)),
        pl.BlockSpec((CHUNK, 3 * wide), lambda i: (turn(i), 0)),
        pl.BlockSpec((CHUNK, DK), lambda i: (turn(i), 0)),
    ]
    rows = pl.BlockSpec((CHUNK, wide), lambda i: (turn(i), 0))
    square = [
        pl.BlockSpec((1, heads, size, size), lambda i: (turn(i), 0, 0, 0)) for size in (CHUNK, DK)
    ]
    return proj, rows, square


def whole_of(shape):
    return pl.BlockSpec(shape, lambda i: (0,) * len(shape))


def mix_forward(proj, logits, table, gain):
    length = proj.shape[0]
    heads = table.shape[1] // DK
    taps = table.shape[0] // 3
    count = length // CHUNK
    wide = heads * DK
    shape = jax.ShapeDtypeStruct
    specs, rows, square = mix_specs(heads, wide, lambda i: i)
    return pl.pallas_call(
        functools.partial(forward_kernel, heads, taps),
        grid=(count,),
        out_shape=(
            shape((length, wide), jnp.bfloat16),
            shape((length, wide), jnp.bfloat16),
            shape((length, wide), jnp.bfloat16),
            shape((count, heads, CHUNK, CHUNK), jnp.bfloat16),
            shape((count, heads, DK, DK), jnp.bfloat16),
        ),
        in_specs=specs + [whole_of(table.shape), whole_of(gain.shape)],
        out_specs=(rows, rows, rows, *square),
        scratch_shapes=[pltpu.VMEM((heads, DK, DK), jnp.float32)],
        compiler_params=pltpu.CompilerParams(vmem_limit_bytes=32 * 2**20),
        cost_estimate=pl.CostEstimate(
            flops=length * heads * DK * 40000,
            bytes_accessed=16 * length * wide,
            transcendentals=3 * length * wide,
        ),
        name="mix_forward",
    )(proj, proj, logits, table, gain)


def mix_backward(proj, logits, table, gain, raw, fresh, solved, states, grad):
    length = proj.shape[0]
    heads = table.shape[1] // DK
    taps = table.shape[0] // 3
    count = length // CHUNK
    wide = heads * DK
    shape = jax.ShapeDtypeStruct

    def turn(i):
        return count - 1 - i

    specs, rows, square = mix_specs(heads, wide, turn)
    return pl.pallas_call(
        functools.partial(backward_kernel, heads, taps),
        grid=(count,),
        out_shape=(
            shape((length, 3 * wide + DK), jnp.bfloat16),
            shape((3 * taps, wide), jnp.float32),
            shape((1, DK), jnp.float32),
        ),
        in_specs=specs
        + [whole_of(table.shape), whole_of(gain.shape), rows, rows, *square, rows],
        out_specs=(
            pl.BlockSpec((CHUNK, 3 * wide + DK), lambda i: (turn(i), 0)),
            whole_of((3 * taps, wide)),
            whole_of((1, DK)),
        ),
        scratch_shapes=[
            pltpu.VMEM((heads, DK, DK), jnp.float32),
            pltpu.VMEM((HEAD_ROOM, 3 * wide), jnp.float32),
        ],
        compiler_params=pltpu.CompilerParams(vmem_limit_bytes=32 * 2**20),
        cost_estimate=pl.CostEstimate(
            flops=length * heads * DK * 40000,
            bytes_accessed=26 * length * wide,
            transcendentals=3 * length * wide,
        ),
        name="mix_backward",
    )(proj, proj, logits, table, gain, raw, fresh, solved, states, grad)


def neighbours():
    me = lax.axis_index("seq")
    return me, me + 1 - 2 * (me % 2), me + 2 - 4 * (me // 2), 3 - me


def greet(across, along):
    barrier = pltpu.get_barrier_semaphore()
    for other in (across, along):
        pl.semaphore_signal(
            barrier, inc=1, device_id={"seq": other}, device_id_type=pl.DeviceIdType.MESH
        )
    pl.semaphore_wait(barrier, 2)


def remote(source, target, send, arrive, slot, other):
    return pltpu.make_async_remote_copy(
        src_ref=source,
        dst_ref=target,
        send_sem=send.at[slot],
        recv_sem=arrive.at[slot],
        device_id={"seq": other},
        device_id_type=pl.DeviceIdType.MESH,
    )


def half_of(rows):
    return (rows // 2 + 15) // 16 * 16


def gather_copies(source, target, near, send, arrive, keep):
    me, across, along, _ = near
    return (
        pltpu.make_async_copy(source, target.at[me], keep),
        remote(source, target.at[me], send, arrive, 0, across),
        remote(source, target.at[me], send, arrive, 1, along),
    )


def gather_start(source, target, near, send, arrive, keep):
    started = gather_copies(source, target, near, send, arrive, keep)
    for copy in started:
        copy.start()
    return started


def gather_finish(started, target, near, send, arrive):
    _, across, along, _ = near
    own, first, second = started
    rows = target.shape[1]
    split = half_of(rows)
    head, rest = pl.ds(0, split), pl.ds(split, rows - split)
    first.wait_recv()
    third = remote(target.at[across, head], target.at[across, head], send, arrive, 2, along)
    third.start()
    second.wait_recv()
    fourth = remote(target.at[along, rest], target.at[along, rest], send, arrive, 3, across)
    fourth.start()
    third.wait_recv()
    fourth.wait_recv()
    for copy in (first, second, third, fourth):
        copy.wait_send()
    own.wait()


def gather_kernel(count, inputs, outputs, body, *refs):
    sources, operands = refs[:count], refs[count : count + inputs]
    targets = refs[count + inputs : 2 * count + inputs]
    results = refs[2 * count + inputs : 2 * count + inputs + outputs]
    send, arrive, keep = refs[2 * count + inputs + outputs :]
    near = neighbours()

    def copies(i):
        return gather_copies(sources[i], targets[i], near, send.at[i], arrive.at[i], keep.at[i])

    @pl.when(pl.program_id(0) == 0)
    def _():
        greet(near[1], near[2])
        for i in range(count):
            for copy in copies(i):
                copy.start()

    body(*operands, *results)

    @pl.when(pl.program_id(0) == pl.num_programs(0) - 1)
    def _():
        for i in range(count):
            gather_finish(copies(i), targets[i], near, send.at[i], arrive.at[i])


def nothing(*refs):
    del refs


def beside_gather(number, blocks, work=(nothing, "gather", (1,), [], [], [], [])):
    side, count = lax.axis_size("seq"), len(blocks)
    body, name, grid, out_shape, in_specs, out_specs, operands = work
    if side != 4 and not operands:
        return [lax.all_gather(block, "seq", axis=0) for block in blocks], []
    if side != 4:
        results = pl.pallas_call(
            body, grid=grid, out_shape=out_shape, in_specs=in_specs, out_specs=out_specs, name=name
        )(*operands)
        return [lax.all_gather(block, "seq", axis=0) for block in blocks], results
    anywhere = [pl.BlockSpec(memory_space=pl.ANY)] * count
    moved = sum(block.size for block in blocks)
    results = pl.pallas_call(
        functools.partial(gather_kernel, count, len(operands), len(out_shape), body),
        grid=grid,
        out_shape=[
            jax.ShapeDtypeStruct((side,) + block.shape, block.dtype) for block in blocks
        ]
        + out_shape,
        in_specs=anywhere + in_specs,
        out_specs=anywhere + out_specs,
        scratch_shapes=[
            pltpu.SemaphoreType.DMA((count, 4)),
            pltpu.SemaphoreType.DMA((count, 4)),
            pltpu.SemaphoreType.DMA((count,)),
        ],
        compiler_params=pltpu.CompilerParams(
            collective_id=number, has_side_effects=True, vmem_limit_bytes=40 * 2**20
        ),
        cost_estimate=pl.CostEstimate(flops=0, bytes_accessed=160 * moved, transcendentals=0),
        name=name,
    )(*blocks, *operands)
    return results[:count], results[count:]


def signal_all(peers):
    barrier = pltpu.get_barrier_semaphore()
    for peer in peers:
        pl.semaphore_signal(barrier, inc=1, device_id=peer, device_id_type=pl.DeviceIdType.MESH)
    pl.semaphore_wait(barrier, len(peers))


def send_share(row, first, where, mine, boxes, send, arrive):
    axis, spot, size = where
    copies = []
    for step in range(1, size):
        copies.append(
            pltpu.make_async_remote_copy(
                src_ref=mine.at[row],
                dst_ref=boxes.at[row, spot],
                send_sem=send.at[first + step - 1],
                recv_sem=arrive.at[first + step - 1],
                device_id={axis: (spot + step) % size},
                device_id_type=pl.DeviceIdType.MESH,
            )
        )
        copies[-1].start()
    boxes[row, spot] = mine[row]
    return copies


def add_shares(row, size, copies, boxes):
    for copy in copies:
        copy.wait()
    total = boxes[row, 0]
    for index in range(1, size):
        total = total + boxes[row, index]
    return total


def start_kernel(
    source_ref, small_ref, sources, smalls,
    send, arrive, keep, send_z, arrive_z, keep_z,
):
    near = neighbours()
    _, across, along, _ = near
    here, count = lax.axis_index("fsdp"), lax.axis_size("fsdp")
    sibling = here + 1 - 2 * (here % 2)
    others = [(here + 2 * step) % count for step in range(1, count // 2)]
    barrier = pltpu.get_barrier_semaphore()
    peers = [{"seq": across}, {"seq": along}, {"fsdp": sibling}]
    peers += [{"fsdp": other} for other in others]
    for peer in peers:
        pl.semaphore_signal(barrier, inc=1, device_id=peer, device_id_type=pl.DeviceIdType.MESH)
    pl.semaphore_wait(barrier, len(peers))

    def send_to(source, target, row, slot, other):
        return pltpu.make_async_remote_copy(
            src_ref=source,
            dst_ref=target,
            send_sem=send_z.at[row, slot],
            recv_sem=arrive_z.at[row, slot],
            device_id={"fsdp": other},
            device_id_type=pl.DeviceIdType.MESH,
        )

    flow = [(small_ref, smalls)]
    first = []
    for row, (source, target) in enumerate(flow):
        own = pltpu.make_async_copy(source, target.at[here], keep_z.at[row])
        own.start()
        copies = [send_to(source, target.at[here], row, 0, sibling)]
        copies += [
            send_to(source, target.at[here], row, 1 + i, other) for i, other in enumerate(others)
        ]
        for copy in copies:
            copy.start()
        first.append((own, copies))
    started = [
        gather_start(block, target, near, send.at[i], arrive.at[i], keep.at[i])
        for i, (block, target) in enumerate([(source_ref, sources)])
    ]
    gather_finish(started[0], sources, near, send.at[0], arrive.at[0])
    for row, (source, target) in enumerate(flow):
        own, copies = first[row]
        passed = []
        for i in range(len(others)):
            copies[1 + i].wait_recv()
            origin = target.at[(here + count - 2 * (i + 1)) % count]
            passed.append(send_to(origin, origin, row, 1 + len(others) + i, sibling))
            passed[-1].start()
        copies[0].wait_recv()
        for copy in passed:
            copy.wait_recv()
        for copy in copies + passed:
            copy.wait_send()
        own.wait()


def start_gathers(source, small):
    side, count = lax.axis_size("seq"), lax.axis_size("fsdp")
    if side != 4:
        return (
            lax.all_gather(source, "seq", axis=0),
            lax.all_gather(small, "fsdp", axis=0),
        )
    slots = count - 1
    return pl.pallas_call(
        start_kernel,
        out_shape=[
            jax.ShapeDtypeStruct((many,) + block.shape, block.dtype)
            for block, many in ((source, side), (small, count))
        ],
        in_specs=[pl.BlockSpec(memory_space=pl.ANY)] * 2,
        out_specs=[pl.BlockSpec(memory_space=pl.ANY)] * 2,
        scratch_shapes=[
            pltpu.SemaphoreType.DMA((2, 4)),
            pltpu.SemaphoreType.DMA((2, 4)),
            pltpu.SemaphoreType.DMA((2,)),
            pltpu.SemaphoreType.DMA((2, slots)),
            pltpu.SemaphoreType.DMA((2, slots)),
            pltpu.SemaphoreType.DMA((2,)),
        ],
        compiler_params=pltpu.CompilerParams(collective_id=1, has_side_effects=True),
        cost_estimate=pl.CostEstimate(
            flops=0, bytes_accessed=160 * source.size, transcendentals=0
        ),
        name="start_gathers",
    )(source, small)


TILE = 256
STEP = 16


def reduce_rows_kernel(flip, gathers, totals, fills, epilogue, lefts, in_count, out_count, *refs):
    left_refs, right_ref, extra = refs[:lefts], refs[lefts], refs[lefts + 1 : in_count]
    outs = refs[in_count : in_count + out_count]
    far, wide_x, wide_y, own, get_a, get_b, get_x, get_y, send, arrive = refs[
        in_count + out_count : in_count + out_count + 10
    ]
    rest_refs = refs[in_count + out_count + 10 :]
    near = neighbours()
    me, across, along, opposite = near
    if totals:
        mine, boxes, send_t, arrive_t = rest_refs
        spots = [(axis, lax.axis_index(axis), lax.axis_size(axis)) for axis in ("seq", "fsdp")]
        signal_all(
            [{axis: (spot + step) % size} for axis, spot, size in spots for step in range(1, size)]
        )
        mine[0] = extra[-1][...]
        shares = send_share(0, 0, spots[0], mine, boxes, send_t, arrive_t)
    else:
        greet(across, along)
    rows, width = own.shape
    split = half_of(rows)
    head, rest = pl.ds(0, split), pl.ds(split, rows - split)

    def part(block, store):
        here = pl.ds(pl.multiple_of(block * rows, rows), rows)

        @pl.loop(0, width // TILE)
        def _(tile):
            columns = pl.ds(pl.multiple_of(tile * TILE, TILE), TILE)
            value, base = 0.0, 0
            for left_ref in left_refs:
                depth = pl.ds(base, left_ref.shape[1])
                if flip:
                    value = value + dotf(left_ref[here, :], right_ref[columns, depth], NT)
                else:
                    value = value + dotf(left_ref[here, :], right_ref[depth, columns], NN)
                base += left_ref.shape[1]
            store[:, columns] = value.astype(store.dtype)

    def term(rows_ref, grads_ref, store):
        @pl.loop(0, rows_ref.shape[1] // TILE)
        def _(tile):
            columns = pl.ds(pl.multiple_of(tile * TILE, TILE), TILE)
            store[columns, :] = low(dotf(rows_ref[:, columns], grads_ref[...], TN))

    def add_into(store, base, source):
        @pl.loop(0, source.shape[0] // STEP)
        def _(index):
            start = pl.multiple_of(index * STEP, STEP)
            there = pl.ds(pl.multiple_of(base + start, STEP), STEP)
            total = store[there, :].astype(jnp.float32) + source[pl.ds(start, STEP), :].astype(
                jnp.float32
            )
            store[there, :] = low(total)

    part(opposite, far)
    if totals:
        mine[1] = add_shares(0, spots[0][2], shares, boxes)
        shares = send_share(1, spots[0][2] - 1, spots[1], mine, boxes, send_t, arrive_t)
    copies = [
        remote(far.at[head], get_a, send, arrive, 0, across),
        remote(far.at[rest], get_b, send, arrive, 1, along),
    ]
    copies[0].start()
    copies[1].start()
    part(across, wide_x)
    copies.append(remote(wide_x.at[head], get_x.at[head], send, arrive, 2, across))
    copies[2].start()
    part(along, wide_y)
    if fills:
        copies.append(remote(wide_y.at[rest], get_y.at[rest], send, arrive, 3, along))
        copies[3].start()
        term(extra[1], extra[2], outs[1])
    else:
        copies.append(remote(wide_y.at[rest], get_y.at[rest], send, arrive, 3, along))
        copies[3].start()
    copies[0].wait_recv()
    add_into(wide_y, 0, get_a)
    copies.append(remote(wide_y.at[head], get_y.at[head], send, arrive, 4, along))
    copies[4].start()
    copies[1].wait_recv()
    add_into(wide_x, split, get_b)
    copies.append(remote(wide_x.at[rest], get_x.at[rest], send, arrive, 5, across))
    copies[5].start()
    if fills:
        term(extra[1], extra[3], outs[2])
    part(me, own)
    for copy in copies[2:]:
        copy.wait_recv()
    epilogue_prepare = rest_refs[0] if gathers else None

    @pl.loop(0, rows // STEP)
    def _(index):
        here = pl.ds(pl.multiple_of(index * STEP, STEP), STEP)
        total = (
            own[here, :] + get_x[here, :].astype(jnp.float32) + get_y[here, :].astype(jnp.float32)
        )
        epilogue(index, here, total, extra, outs, epilogue_prepare)

    for copy in copies:
        copy.wait_send()
    if totals:
        outs[-1][...] = add_shares(1, spots[1][2], shares, boxes)
    if gathers:
        block, send_2, arrive_2, keep = rest_refs
        target = outs[0]
        started = gather_start(block, target, near, send_2, arrive_2, keep.at[0])
        gather_finish(started, target, near, send_2, arrive_2)


def rms_back(grad, values, gain):
    r = lax.rsqrt(jnp.mean(values * values, axis=-1, keepdims=True) + EPS)
    scaled = grad * gain
    change = r * (scaled - values * (r * r) * jnp.mean(scaled * values, axis=-1, keepdims=True))
    return change


def middle_epilogue(index, here, total, extra, outs, block):
    source_ref, gain_ref = extra
    middle = source_ref[here, :].astype(jnp.float32) + total
    outs[1][here, :] = middle
    r = lax.rsqrt(jnp.mean(middle * middle, axis=-1, keepdims=True) + EPS)
    block[here, :] = low(middle * r * gain_ref[...])


def output_epilogue(index, here, total, extra, outs, block):
    outs[0][here, :] = low(extra[0][here, :] + total)


def branch_epilogue(index, here, total, extra, outs, block):
    middle_ref, upstream_ref, gain_ref = extra
    change = rms_back(total, middle_ref[here, :], gain_ref[...])
    grad = upstream_ref[here, :].astype(jnp.float32) + change
    outs[1][here, :] = grad
    block[here, :] = low(grad)


def input_epilogue(index, here, total, extra, outs, block):
    source_ref, carried_ref, gain_ref, _ = extra
    change = rms_back(total, source_ref[here, :].astype(jnp.float32), gain_ref[...])
    outs[0][here, :] = carried_ref[here, :] + change


def fused_reduce(name, number, flip, mode, epilogue, outs, lefts, right, *extra):
    gathers, totals = mode == "gather", mode == "total"
    side = lax.axis_size("seq")
    length = lefts[0].shape[0]
    rows = length // side
    width = right.shape[0] if flip else right.shape[1]
    split = half_of(rows)
    scratch = [
        pltpu.VMEM((rows, width), jnp.bfloat16),
        pltpu.VMEM((rows, width), jnp.bfloat16),
        pltpu.VMEM((rows, width), jnp.bfloat16),
        pltpu.VMEM((rows, width), jnp.float32),
        pltpu.VMEM((split, width), jnp.bfloat16),
        pltpu.VMEM((rows - split, width), jnp.bfloat16),
        pltpu.VMEM((rows, width), jnp.bfloat16),
        pltpu.VMEM((rows, width), jnp.bfloat16),
        pltpu.SemaphoreType.DMA((6,)),
        pltpu.SemaphoreType.DMA((6,)),
    ]
    out_specs = in_vmem(len(outs))
    if totals:
        shape, f_count = extra[-1].shape, lax.axis_size("fsdp")
        peers = side + f_count - 2
        scratch += [
            pltpu.VMEM((2,) + shape, jnp.float32),
            pltpu.VMEM((2, max(side, f_count)) + shape, jnp.float32),
            pltpu.SemaphoreType.DMA((peers,)),
            pltpu.SemaphoreType.DMA((peers,)),
        ]
    if gathers:
        scratch += [
            pltpu.VMEM((rows, width), jnp.bfloat16),
            pltpu.SemaphoreType.DMA((4,)),
            pltpu.SemaphoreType.DMA((4,)),
            pltpu.SemaphoreType.DMA((1,)),
        ]
        out_specs[0] = pl.BlockSpec(memory_space=pl.ANY)
    return pl.pallas_call(
        functools.partial(
            reduce_rows_kernel,
            flip,
            gathers,
            totals,
            mode == "fill",
            epilogue,
            len(lefts),
            len(lefts) + 1 + len(extra),
            len(outs),
        ),
        out_shape=outs,
        in_specs=in_vmem(len(lefts) + 1 + len(extra)),
        out_specs=out_specs,
        scratch_shapes=scratch,
        compiler_params=pltpu.CompilerParams(
            collective_id=number, has_side_effects=True, vmem_limit_bytes=56 * 2**20
        ),
        cost_estimate=pl.CostEstimate(
            flops=2 * sum(left.size for left in lefts) * width,
            bytes_accessed=(320 if gathers else 160) * rows * width,
            transcendentals=0,
        ),
        name=name,
    )(*lefts, right, *extra)


def seq_sum(partial, side):
    block = low(partial).reshape(side, -1, partial.shape[-1])
    return lax.psum_scatter(block, "seq", scatter_dimension=0).astype(jnp.float32)


def out_and_norm(attn_in, weight, source, gain):
    side = lax.axis_size("seq")
    rows, width = source.shape
    if side != 4:
        middle = source.astype(jnp.float32) + seq_sum(dotf(attn_in, weight, NN), side)
        r = lax.rsqrt(jnp.mean(middle * middle, axis=-1, keepdims=True) + EPS)
        return lax.all_gather(low(middle * r * gain), "seq", axis=0), middle
    outs = (
        jax.ShapeDtypeStruct((side, rows, width), jnp.bfloat16),
        jax.ShapeDtypeStruct((rows, width), jnp.float32),
    )
    return fused_reduce(
        "out_and_norm", 2, False, "gather", middle_epilogue, outs, [attn_in], weight, source, gain
    )


def place_kernel(side, *refs):
    target_ref = refs[side]
    me = lax.axis_index("seq")
    for spot in range(side):

        @pl.when(me == spot)
        def _():
            for index in range(side):
                target_ref[index] = refs[index ^ spot][...].astype(target_ref.dtype)


def place_work(blocks, kind):
    side = len(blocks)
    rows, width = blocks[0].shape
    tile = 512
    return (
        functools.partial(place_kernel, side),
        "place",
        (width // tile,),
        [jax.ShapeDtypeStruct((side, rows, width), kind)],
        [pl.BlockSpec((rows, tile), lambda i: (0, i))] * side,
        [pl.BlockSpec((side, rows, tile), lambda i: (0, 0, i))],
        blocks,
    )


def place(blocks, kind):
    body, name, grid, out_shape, in_specs, out_specs, operands = place_work(blocks, kind)
    return pl.pallas_call(
        body, grid=grid, out_shape=out_shape, in_specs=in_specs, out_specs=out_specs, name=name
    )(*operands)[0]


def swap(block, step):
    pairs = [(i, i ^ step) for i in range(lax.axis_size("seq"))]
    return lax.ppermute(block, "seq", pairs)


def down_and_terms(hidden, weight, middle, ffn_in, grads):
    side = lax.axis_size("seq")
    if side != 4:
        output = low(middle + seq_sum(dotf(hidden, weight, NN), side))
        return output, *[low(dotf(ffn_in, grad, TN)) for grad in grads]
    term = jax.ShapeDtypeStruct((ffn_in.shape[1], grads[0].shape[1]), jnp.bfloat16)
    outs = (jax.ShapeDtypeStruct(middle.shape, jnp.bfloat16), term, term)
    return fused_reduce(
        "down_and_terms", 3, False, "fill", output_epilogue, outs, [hidden], weight, middle, ffn_in,
        *grads,
    )


def branch_grad(grads, weight, middle, upstream, gain):
    side = lax.axis_size("seq")
    rows, width = middle.shape
    if side != 4:
        grad = jnp.concatenate(grads, axis=1)
        change = rms_back(seq_sum(dotf(grad, weight, NT), side), middle, gain)
        total = upstream.astype(jnp.float32) + change
        return lax.all_gather(low(total), "seq", axis=0), total
    outs = (
        jax.ShapeDtypeStruct((side, rows, width), jnp.bfloat16),
        jax.ShapeDtypeStruct((rows, width), jnp.float32),
    )
    return fused_reduce(
        "branch_grad", 4, True, "gather", branch_epilogue, outs, grads, weight, middle, upstream, gain
    )


def input_grad(grad, weight, source, carried, gain, value):
    side = lax.axis_size("seq")
    if side != 4:
        partial = dotf(grad, weight[:, : grad.shape[1]], NT)
        change = rms_back(seq_sum(partial, side), source.astype(jnp.float32), gain)
        return carried + change, lax.psum(value, ("fsdp", "seq"))
    outs = (
        jax.ShapeDtypeStruct(carried.shape, jnp.float32),
        jax.ShapeDtypeStruct(value.shape, jnp.float32),
    )
    return fused_reduce(
        "input_grad", 5, True, "total", input_epilogue, outs, [grad], weight, source, carried, gain,
        value,
    )


def pick_kernel(side, share, source_ref, target_ref):
    me = lax.axis_index("seq")
    count = target_ref.shape[1] // share
    for index in range(side):

        @pl.when(me == index)
        def _():
            pieces = [
                source_ref[:, pl.ds((k * side + index) * share, share)].astype(jnp.float32)
                for k in range(count)
            ]
            target_ref[...] = low(jnp.concatenate(pieces, axis=1))


def pick_columns(weight, share):
    side = lax.axis_size("seq")
    rows, width = weight.shape
    tile = 32
    return pl.pallas_call(
        functools.partial(pick_kernel, side, share),
        grid=(rows // tile,),
        out_shape=jax.ShapeDtypeStruct((rows, width // side), weight.dtype),
        in_specs=[pl.BlockSpec((tile, width), lambda i: (i, 0))],
        out_specs=pl.BlockSpec((tile, width // side), lambda i: (i, 0)),
        name="pick_columns",
    )(weight)


def spread_kernel(side, share, *refs):
    gate_refs, (up_ref, weight_ref, target_ref, total_ref) = refs[:side], refs[side:]
    count = up_ref.shape[2] // share
    me = lax.axis_index("seq")
    half = target_ref.shape[1] // 2

    def place(pieces, base):
        grad = jnp.concatenate([piece.astype(jnp.float32) for piece in pieces], axis=1)
        target_ref[:, pl.ds(base, half)] = low(grad)
        weight = weight_ref[:, pl.ds(base, half)].astype(jnp.float32)
        return jnp.sum(grad * weight, axis=1, keepdims=True)

    spans = [(pl.ds(k * share, share), index) for k in range(count) for index in range(side)]
    total = place([up_ref[index, :, span] for span, index in spans], half)
    for spot in range(side):

        @pl.when(me == spot)
        def _():
            whole = total + place([gate_refs[index ^ spot][:, span] for span, index in spans], 0)
            total_ref[...] = jnp.broadcast_to(whole, total_ref.shape)


def spread_work(gates, up, weight, share):
    side, rows, width = up.shape
    tile = 32
    by_row = pl.BlockSpec((tile, 2 * width * side), lambda i: (i, 0))
    return (
        functools.partial(spread_kernel, side, share),
        "spread",
        (rows // tile,),
        [
            jax.ShapeDtypeStruct((rows, 2 * width * side), jnp.bfloat16),
            jax.ShapeDtypeStruct((rows, DK), jnp.float32),
        ],
        [pl.BlockSpec((tile, width), lambda i: (i, 0))] * side
        + [pl.BlockSpec((side, tile, width), lambda i: (0, i, 0)), by_row],
        [by_row, pl.BlockSpec((tile, DK), lambda i: (i, 0))],
        [*gates, up, weight],
    )


def assemble_kernel(
    side, wide, taps, grad_ref, weight_ref, beta_ref, target_ref, total_ref, rest_ref
):
    heads = wide // DK
    total = 0.0
    for part in range(3):
        for index in range(side):
            columns = pl.ds((part * side + index) * wide, wide)
            grad = grad_ref[index, :, pl.ds(part * wide, wide)].astype(jnp.float32)
            target_ref[:, columns] = grad
            weight = weight_ref[:, columns].astype(jnp.float32)
            total = total + jnp.sum(grad * weight, axis=1, keepdims=True)
    lane = lax.broadcasted_iota(jnp.int32, beta_ref.shape, 1)
    beta, conv = 0.0, 0.0
    for index in range(side):
        rest = grad_ref[index, :, pl.ds(3 * wide, DK)].astype(jnp.float32)
        mine = jnp.where(lane < heads, rest, 0.0)
        beta = beta + (pltpu.roll(mine, index * heads, 1) if index else mine)
        conv = conv + rest
    conv = jnp.where((lane >= heads) & (lane < heads + 3 * taps), conv, 0.0)
    if side > 1:
        conv = pltpu.roll(conv, H - heads, 1)
    total = total + jnp.sum(beta * beta_ref[...].astype(jnp.float32), axis=1, keepdims=True)
    total_ref[...] = jnp.broadcast_to(total, total_ref.shape)
    rest_ref[...] = (beta + conv).T


def assemble_columns(grad, weight, beta, wide, taps):
    side, rows, depth = grad.shape
    tile = min(rows, DK)
    by_row = pl.BlockSpec((tile, weight.shape[1]), lambda i: (i, 0))
    narrow = pl.BlockSpec((tile, DK), lambda i: (i, 0))
    return pl.pallas_call(
        functools.partial(assemble_kernel, side, wide, taps),
        grid=(rows // tile,),
        out_shape=(
            jax.ShapeDtypeStruct(weight.shape, jnp.float32),
            jax.ShapeDtypeStruct((rows, DK), jnp.float32),
            jax.ShapeDtypeStruct((DK, rows), jnp.float32),
        ),
        in_specs=[pl.BlockSpec((side, tile, depth), lambda i: (0, i, 0)), by_row, narrow],
        out_specs=(by_row, narrow, pl.BlockSpec((DK, tile), lambda i: (0, i))),
        compiler_params=pltpu.CompilerParams(vmem_limit_bytes=40 * 2**20),
        name="assemble_columns",
    )(grad, weight, beta)


def fsdp_sum(term):
    return lax.psum_scatter(low(term), "fsdp", scatter_dimension=0, tiled=True)


def per_device(
    inputs,
    cotangent,
    norm1_gain,
    w_qkv,
    w_beta,
    conv_weight,
    out_gain,
    w_out,
    norm2_gain,
    w_gate_up,
    w_down,
):
    side = lax.axis_size("seq")
    s = lax.axis_index("seq")
    shape = inputs.shape
    width = shape[2]
    source = inputs.reshape(-1, width)
    upstream = cotangent.reshape(-1, width)
    length = source.shape[0] * side
    heads = H // side
    wide = heads * DK
    rows = w_qkv.shape[0]
    share = w_down.shape[0] // side
    taps = conv_weight.shape[1] // 3

    f_count = lax.axis_size("fsdp")
    depth = 3 * wide + DK
    homes = [
        (f * side + i, (side * (f % 2) + i) * side + f // 2)
        for f in range(f_count)
        for i in range(side)
    ]
    strip = rows // side

    def everywhere(block):
        return lax.all_gather(block, "fsdp", axis=0, tiled=True)

    parts = [
        lax.dynamic_slice_in_dim(w_qkv, part * width + s * wide, wide, 1) for part in range(3)
    ]
    beta_part = lax.dynamic_slice_in_dim(w_beta, s * heads, heads, 1)
    parts.append(jnp.pad(beta_part, ((0, 0), (0, DK - heads))))
    qkv_part = everywhere(jnp.concatenate(parts, axis=1))
    small = jnp.concatenate([norm1_gain[None], norm2_gain[None], conv_weight.T], axis=0)
    small = jnp.pad(small, ((0, 16 - small.shape[0]), (0, 0)))
    piece = lax.dynamic_slice_in_dim(w_out, s * strip, strip, 0)
    piece = lax.ppermute(piece, ("fsdp", "seq"), homes)
    source_all, small = start_gathers(source, small)
    sent, source_all = lax.optimization_barrier((upstream, source_all))
    out_part = everywhere(piece)
    upstreams = [upstream] + [swap(sent, step) for step in range(1, side)]
    small = small.transpose(1, 0, 2).reshape(small.shape[1], width).astype(jnp.float32)
    gain_first = small[0:1]
    gain_second = small[1:2]
    table = lax.dynamic_slice_in_dim(small[2 : 2 + 3 * taps], s * wide, wide, 1)
    gain_heads = out_gain.astype(jnp.float32)[None]
    source_all = source_all.reshape(length, width).astype(jnp.float32)

    picked = pick_columns(w_gate_up, share)
    gate_up_part = everywhere(picked)
    down_part = everywhere(lax.dynamic_slice_in_dim(w_down, s * share, share, 0))

    normed_first = low(
        source_all
        * lax.rsqrt(jnp.mean(source_all * source_all, axis=-1, keepdims=True) + EPS)
        * gain_first
    )
    projected = low(dotf(normed_first, qkv_part[:, : 3 * wide], NN))
    beta_logits = dotf(normed_first, qkv_part[:, 3 * wide : depth], NN)
    attn_in, *kept = mix_forward(projected, beta_logits, table, gain_heads)
    attn_in, *upstreams = lax.optimization_barrier((attn_in, *upstreams))
    upstream_all = place(upstreams, jnp.bfloat16).reshape(length, width)
    ffn_in, middle = out_and_norm(attn_in, out_part, source, gain_second)
    ffn_in = ffn_in.reshape(length, width)
    gate_up = dotf(ffn_in, gate_up_part, NN)
    hidden_width = gate_up.shape[1] // 2
    gate = gate_up[:, :hidden_width]
    upward = gate_up[:, hidden_width:]
    sigma = jax.nn.sigmoid(gate)
    hidden = low(gate * sigma * upward)

    down_term = low(dotf(hidden, upstream_all, TN))
    grad_down = fsdp_sum(down_term)
    upstream_all, _ = lax.optimization_barrier((upstream_all, down_term))
    grad_hidden = dotf(upstream_all, down_part, NT)
    grad_gate = low(grad_hidden * upward * sigma * (1.0 + gate * (1.0 - sigma)))
    grad_up = low(grad_hidden * gate * sigma)
    output, gate_term, up_term = down_and_terms(
        hidden, down_part, middle, ffn_in, [grad_gate, grad_up]
    )
    gate_sum = fsdp_sum(gate_term)
    up_sum = fsdp_sum(up_term)
    grad_gate, grad_up, grad_down = lax.optimization_barrier((grad_gate, grad_up, grad_down))
    grad_branch, grad_middle = branch_grad(
        [grad_gate, grad_up], gate_up_part, middle, upstream, gain_second
    )
    grad_branch, grad_down, gate_sum = lax.optimization_barrier(
        (grad_branch, grad_down, gate_sum)
    )
    grad_branch = grad_branch.reshape(length, width)
    downs = [grad_down] + [swap(grad_down, step) for step in range(1, side)]
    gates = [gate_sum] + [swap(gate_sum, step) for step in range(1, side)]

    out_term = low(dotf(attn_in, grad_branch, TN))
    grad_attn_in, _ = lax.optimization_barrier((dotf(grad_branch, out_part, NT), out_term))
    grad_proj, grad_table, grad_gain_heads = mix_backward(
        projected, beta_logits, table, gain_heads, *kept, grad_attn_in
    )
    grad_proj, up_sum, *downs = lax.optimization_barrier((grad_proj, up_sum, *downs))
    grad_qkv = low(dotf(normed_first, grad_proj, TN))
    grad_qkv = lax.dynamic_update_slice(
        grad_qkv, low(grad_table.T), (s * wide, 3 * wide + heads)
    )
    grad_down = place(downs, jnp.float32)
    grad_proj, grad_qkv, out_term, grad_down, *gates = lax.optimization_barrier(
        (grad_proj, grad_qkv, out_term, grad_down, *gates)
    )
    grad_qkv = fsdp_sum(grad_qkv)
    grad_input, grad_out_gain = input_grad(
        grad_proj, qkv_part, source, grad_middle, gain_first,
        jnp.broadcast_to(grad_gain_heads, (8, DK)),
    )
    up_sum, grad_input = lax.optimization_barrier((up_sum, grad_input))
    (up_sum,), _ = beside_gather(7, [up_sum])
    out_term, grad_qkv, up_sum = lax.optimization_barrier((out_term, grad_qkv, up_sum))
    out_sum = fsdp_sum(out_term)
    (grad_qkv,), (grad_w_gate_up, second_total) = beside_gather(
        9, [grad_qkv], spread_work(gates, up_sum, w_gate_up, share)
    )
    out_sum = lax.ppermute(out_sum, ("fsdp", "seq"), [(b, a) for a, b in homes])
    (grad_w_out,), _ = beside_gather(8, [out_sum])
    wide_beta = jnp.pad(w_beta, ((0, 0), (0, DK - H)))
    grad_w_qkv, first_total, rest = assemble_columns(grad_qkv, w_qkv, wide_beta, wide, taps)
    return (
        output.reshape(shape),
        grad_input.reshape(shape),
        first_total[:, 0] / norm1_gain.astype(jnp.float32),
        grad_w_qkv,
        rest[:H].T,
        rest[H : H + 3 * taps].T,
        grad_out_gain[0],
        grad_w_out.reshape(rows, width).astype(jnp.float32),
        second_total[:, 0] / norm2_gain.astype(jnp.float32),
        grad_w_gate_up.astype(jnp.float32),
        grad_down.reshape(side * share, width),
    )


def solution(mesh):
    by_row = P("fsdp", None)
    tokens = P("fsdp", "seq", None)
    specs = (tokens, tokens, P("fsdp"), by_row, by_row, by_row, P(), by_row, P("fsdp"))
    specs = specs + (by_row, by_row)
    return jax.shard_map(per_device, mesh=mesh, in_specs=specs, out_specs=specs, check_vma=False)
```

```python
import functools

import jax
import jax.numpy as jnp
from jax import lax
from jax.experimental import pallas as pl
from jax.experimental.pallas import tpu as pltpu
from jax.sharding import PartitionSpec as P

H = 16
DK = 128
EPS = 1e-06
CHUNK = 128
HEAD_ROOM = 8


def dotf(left, right, dims):
    return lax.dot_general(left, right, (dims, ((), ())), preferred_element_type=jnp.float32)


NN = ((1,), (0,))
NT = ((1,), (1,))
TN = ((0,), (0,))


def low(value):
    return value.astype(jnp.bfloat16)


def square_iota(axis):
    return lax.broadcasted_iota(jnp.int32, (CHUNK, CHUNK), axis)


def sigmoid(value):
    return 1.0 / (1.0 + jnp.exp(-value))


def conv_chunk(window, taps, count):
    mixed = window[HEAD_ROOM:] * taps[count - 1]
    for back in range(1, count):
        mixed = mixed + pltpu.roll(window, back, 0)[HEAD_ROOM:] * taps[count - 1 - back]
    return mixed


def window_of(ahead_ref, proj_ref, chunk, column):
    lanes = pl.ds(column, DK)
    before = ahead_ref[:, lanes].astype(jnp.float32)[8:]
    before = jnp.where(chunk > 0, before, 0.0)
    return jnp.concatenate([before, proj_ref[:, lanes].astype(jnp.float32)], axis=0)


def head_inputs(ahead_ref, proj_ref, table_ref, chunk, head, heads, taps):
    wide = heads * DK
    found = []
    for part in range(3):
        window = window_of(ahead_ref, proj_ref, chunk, part * wide + head * DK)
        weights = [
            table_ref[pl.ds(part * taps + tap, 1), pl.ds(head * DK, DK)] for tap in range(taps)
        ]
        mixed = conv_chunk(window, weights, taps)
        gate = sigmoid(mixed)
        found.append((window, weights, mixed, gate, mixed * gate))
    active_key = found[1][4]
    scale = lax.rsqrt(jnp.sum(active_key * active_key, axis=-1, keepdims=True) + EPS)
    key = active_key * scale
    return found, found[0][4] * DK**-0.5, key, scale, found[2][4]


def inverses_of(stricts):
    row, column = square_iota(0), square_iota(1)
    eye = (row == column).astype(jnp.float32)
    solved = [eye - jnp.where(row // 2 == column // 2, strict, 0.0) for strict in stricts]
    half = 2
    while half < CHUNK:
        below = (row // (2 * half) == column // (2 * half)) & (row // half != column // half)
        off = [low(jnp.where(below, strict, 0.0)) for strict in stricts]
        known = [low(item) for item in solved]
        first = [low(dotf(k, o, NN)) for k, o in zip(known, off)]
        second = [dotf(p, k, NN) for p, k in zip(first, known)]
        solved = [item - change for item, change in zip(solved, second)]
        half *= 2
    return [low(item) for item in solved]


def forward_kernel(
    heads, taps, ahead_ref, proj_ref, logit_ref, table_ref, gain_ref,
    normed_ref, raw_ref, fresh_ref, solve_ref, state_ref, carry,
):
    every = range(heads)
    chunk = pl.program_id(0)

    @pl.when(chunk == 0)
    def _():
        carry[...] = jnp.zeros_like(carry)

    row, column = square_iota(0), square_iota(1)
    beta_all = low(sigmoid(logit_ref[...])).astype(jnp.float32)
    beta = [beta_all[:, h : h + 1] for h in every]
    ready = [head_inputs(ahead_ref, proj_ref, table_ref, chunk, h, heads, taps) for h in every]
    query = [low(item[1]) for item in ready]
    key = [low(item[2]) for item in ready]
    value = [low(item[4]) for item in ready]
    gram = [dotf(key[h], key[h], NT) for h in every]
    score = [dotf(query[h], key[h], NT) for h in every]
    strict = [jnp.where(row > column, gram[h] * beta[h], 0.0) for h in every]
    within = [low(jnp.where(row >= column, score[h], 0.0)) for h in every]
    solved = inverses_of(strict)
    state = [carry[h] for h in every]
    state_low = [low(item) for item in state]
    recalled = [dotf(key[h], state_low[h], NN) for h in every]
    rest = [low(beta[h] * (value[h].astype(jnp.float32) - recalled[h])) for h in every]
    fresh = [low(dotf(solved[h], rest[h], NN)) for h in every]
    grown = [dotf(key[h], fresh[h], TN) for h in every]
    for h in every:
        carry[h] = state[h] + grown[h]
    past = [dotf(query[h], state_low[h], NN) for h in every]
    inner = [dotf(within[h], fresh[h], NN) for h in every]
    for h in every:
        lanes = pl.ds(h * DK, DK)
        raw = low(past[h] + inner[h])
        wide_raw = raw.astype(jnp.float32)
        normed = wide_raw * lax.rsqrt(
            jnp.mean(wide_raw * wide_raw, axis=-1, keepdims=True) + EPS
        )
        normed_ref[:, lanes] = low(normed * gain_ref[...])
        raw_ref[:, lanes] = raw
        fresh_ref[:, lanes] = fresh[h]
        solve_ref[0, h] = solved[h]
        state_ref[0, h] = state_low[h]


def backward_kernel(
    heads, taps, ahead_ref, proj_ref, logit_ref, table_ref, gain_ref, raw_ref, fresh_ref, solve_ref,
    state_ref, grad_ref, gproj_ref, gtable_ref, ggain_ref, carry, after,
):
    wide = heads * DK
    every = range(heads)
    chunk = pl.num_programs(0) - 1 - pl.program_id(0)

    @pl.when(pl.program_id(0) == 0)
    def _():
        carry[...] = jnp.zeros_like(carry)
        after[...] = jnp.zeros_like(after)
        gtable_ref[...] = jnp.zeros_like(gtable_ref)
        ggain_ref[...] = jnp.zeros_like(ggain_ref)

    row, column = square_iota(0), square_iota(1)
    beta_wide = sigmoid(logit_ref[...])
    beta_all = low(beta_wide).astype(jnp.float32)
    beta = [beta_all[:, h : h + 1] for h in every]
    lane = lax.broadcasted_iota(jnp.int32, (CHUNK, DK), 1)
    ready = [head_inputs(ahead_ref, proj_ref, table_ref, chunk, h, heads, taps) for h in every]
    query = [low(item[1]) for item in ready]
    key = [low(item[2]) for item in ready]
    value = [low(item[4]) for item in ready]
    grad_out = []
    for h in every:
        lanes = pl.ds(h * DK, DK)
        raw = raw_ref[:, lanes].astype(jnp.float32)
        grad_normed = grad_ref[:, lanes].astype(jnp.float32)
        r = lax.rsqrt(jnp.mean(raw * raw, axis=-1, keepdims=True) + EPS)
        scaled = grad_normed * gain_ref[...]
        mean = jnp.mean(scaled * raw, axis=-1, keepdims=True)
        grad_out.append(low(r * (scaled - raw * (r * r) * mean)))
        ggain_ref[...] += jnp.sum(grad_normed * raw * r, axis=0, keepdims=True)
    state = [state_ref[0, h] for h in every]
    solved = [solve_ref[0, h] for h in every]
    fresh = [fresh_ref[:, pl.ds(h * DK, DK)] for h in every]
    later = [carry[h] for h in every]
    later_low = [low(item) for item in later]
    score = [dotf(query[h], key[h], NT) for h in every]
    onward = [dotf(key[h], later_low[h], NN) for h in every]
    within = [low(jnp.where(row >= column, item, 0.0)) for item in score]
    grad_fresh = [low(dotf(within[h], grad_out[h], TN) + onward[h]) for h in every]
    grad_solved = [dotf(solved[h], grad_fresh[h], TN) for h in every]
    grad_value = [beta[h] * grad_solved[h] for h in every]
    grad_rest = [low(item) for item in grad_value]
    asked = [dotf(query[h], grad_out[h], TN) for h in every]
    taken = [dotf(key[h], grad_rest[h], TN) for h in every]
    for h in every:
        carry[h] = later[h] + asked[h] - taken[h]
    gram = [dotf(key[h], key[h], NT) for h in every]
    recalled = [dotf(key[h], state[h], NN) for h in every]
    product = [dotf(grad_out[h], fresh[h], NT) for h in every]
    cross = [dotf(low(grad_solved[h]), fresh[h], NT) for h in every]
    grad_within = [low(jnp.where(row >= column, item, 0.0)) for item in product]
    grad_strict = [jnp.where(row > column, -item, 0.0) for item in cross]
    mixing = [low(beta[h] * grad_strict[h]) for h in every]
    grad_query = [
        dotf(grad_out[h], state[h], NT) + dotf(grad_within[h], key[h], NN) for h in every
    ]
    grad_key = [
        dotf(grad_within[h], query[h], TN)
        + dotf(fresh[h], later_low[h], NT)
        - dotf(grad_rest[h], state[h], NT)
        + dotf(mixing[h], key[h], NN)
        + dotf(mixing[h], key[h], TN)
        for h in every
    ]
    glogit = jnp.zeros((CHUNK, DK), jnp.float32)
    for h in every:
        rest = value[h].astype(jnp.float32) - recalled[h]
        grad_beta = jnp.sum(grad_solved[h] * rest, axis=-1, keepdims=True) + jnp.sum(
            grad_strict[h] * gram[h], axis=-1, keepdims=True
        )
        bw = beta_wide[:, h : h + 1]
        grad_beta = low(grad_beta).astype(jnp.float32) * bw * (1.0 - bw)
        glogit = glogit + jnp.where(lane == h, grad_beta, 0.0)
    gproj_ref[:, pl.ds(3 * wide, DK)] = low(glogit)
    for h in every:
        found, _, key_wide, scale, _ = ready[h]
        lanes = pl.ds(h * DK, DK)
        back_query = low(grad_query[h]).astype(jnp.float32) * DK**-0.5
        back_key = low(grad_key[h]).astype(jnp.float32)
        back_key = scale * (
            back_key - key_wide * jnp.sum(back_key * key_wide, axis=-1, keepdims=True)
        )
        back_value = low(grad_value[h]).astype(jnp.float32)
        for part, grad_active in enumerate((back_query, back_key, back_value)):
            window, weights, mixed, gate, _ = found[part]
            grad_conv = grad_active * (gate * (1.0 + mixed * (1.0 - gate)))
            columns = pl.ds(part * wide + h * DK, DK)
            tail = jnp.concatenate([grad_conv, after[:, columns]], axis=0)
            size = CHUNK + HEAD_ROOM
            total = grad_conv * weights[taps - 1]
            for back in range(1, taps):
                ahead = pltpu.roll(tail, size - back, 0)[:CHUNK]
                total = total + ahead * weights[taps - 1 - back]
            gproj_ref[:, columns] = low(total)
            after[:, columns] = grad_conv[:HEAD_ROOM]
            for back in range(taps):
                shifted = pltpu.roll(window, back, 0)[HEAD_ROOM:] if back else window[HEAD_ROOM:]
                spot = pl.ds(part * taps + taps - 1 - back, 1)
                gtable_ref[spot, lanes] += jnp.sum(grad_conv * shifted, axis=0, keepdims=True)


def in_vmem(count):
    return [pl.BlockSpec(memory_space=pltpu.VMEM)] * count


def mix_specs(heads, wide, turn):
    ratio = CHUNK // 16
    proj = [
        pl.BlockSpec((16, 3 * wide), lambda i: (jnp.maximum(turn(i) * ratio - 1, 0), 0)),
        pl.BlockSpec((CHUNK, 3 * wide), lambda i: (turn(i), 0)),
        pl.BlockSpec((CHUNK, DK), lambda i: (turn(i), 0)),
    ]
    rows = pl.BlockSpec((CHUNK, wide), lambda i: (turn(i), 0))
    square = [
        pl.BlockSpec((1, heads, size, size), lambda i: (turn(i), 0, 0, 0)) for size in (CHUNK, DK)
    ]
    return proj, rows, square


def whole_of(shape):
    return pl.BlockSpec(shape, lambda i: (0,) * len(shape))


def mix_forward(proj, logits, table, gain):
    length = proj.shape[0]
    heads = table.shape[1] // DK
    taps = table.shape[0] // 3
    count = length // CHUNK
    wide = heads * DK
    shape = jax.ShapeDtypeStruct
    specs, rows, square = mix_specs(heads, wide, lambda i: i)
    return pl.pallas_call(
        functools.partial(forward_kernel, heads, taps),
        grid=(count,),
        out_shape=(
            shape((length, wide), jnp.bfloat16),
            shape((length, wide), jnp.bfloat16),
            shape((length, wide), jnp.bfloat16),
            shape((count, heads, CHUNK, CHUNK), jnp.bfloat16),
            shape((count, heads, DK, DK), jnp.bfloat16),
        ),
        in_specs=specs + [whole_of(table.shape), whole_of(gain.shape)],
        out_specs=(rows, rows, rows, *square),
        scratch_shapes=[pltpu.VMEM((heads, DK, DK), jnp.float32)],
        compiler_params=pltpu.CompilerParams(vmem_limit_bytes=32 * 2**20),
        cost_estimate=pl.CostEstimate(
            flops=length * heads * DK * 40000,
            bytes_accessed=16 * length * wide,
            transcendentals=3 * length * wide,
        ),
        name="mix_forward",
    )(proj, proj, logits, table, gain)


def mix_backward(proj, logits, table, gain, raw, fresh, solved, states, grad):
    length = proj.shape[0]
    heads = table.shape[1] // DK
    taps = table.shape[0] // 3
    count = length // CHUNK
    wide = heads * DK
    shape = jax.ShapeDtypeStruct

    def turn(i):
        return count - 1 - i

    specs, rows, square = mix_specs(heads, wide, turn)
    return pl.pallas_call(
        functools.partial(backward_kernel, heads, taps),
        grid=(count,),
        out_shape=(
            shape((length, 3 * wide + DK), jnp.bfloat16),
            shape((3 * taps, wide), jnp.float32),
            shape((1, DK), jnp.float32),
        ),
        in_specs=specs
        + [whole_of(table.shape), whole_of(gain.shape), rows, rows, *square, rows],
        out_specs=(
            pl.BlockSpec((CHUNK, 3 * wide + DK), lambda i: (turn(i), 0)),
            whole_of((3 * taps, wide)),
            whole_of((1, DK)),
        ),
        scratch_shapes=[
            pltpu.VMEM((heads, DK, DK), jnp.float32),
            pltpu.VMEM((HEAD_ROOM, 3 * wide), jnp.float32),
        ],
        compiler_params=pltpu.CompilerParams(vmem_limit_bytes=32 * 2**20),
        cost_estimate=pl.CostEstimate(
            flops=length * heads * DK * 40000,
            bytes_accessed=26 * length * wide,
            transcendentals=3 * length * wide,
        ),
        name="mix_backward",
    )(proj, proj, logits, table, gain, raw, fresh, solved, states, grad)


def neighbours():
    me = lax.axis_index("seq")
    return me, me + 1 - 2 * (me % 2), me + 2 - 4 * (me // 2), 3 - me


def greet(across, along):
    barrier = pltpu.get_barrier_semaphore()
    for other in (across, along):
        pl.semaphore_signal(
            barrier, inc=1, device_id={"seq": other}, device_id_type=pl.DeviceIdType.MESH
        )
    pl.semaphore_wait(barrier, 2)


def remote(source, target, send, arrive, slot, other):
    return pltpu.make_async_remote_copy(
        src_ref=source,
        dst_ref=target,
        send_sem=send.at[slot],
        recv_sem=arrive.at[slot],
        device_id={"seq": other},
        device_id_type=pl.DeviceIdType.MESH,
    )


def half_of(rows):
    return (rows // 2 + 15) // 16 * 16


def gather_copies(source, target, near, send, arrive, keep):
    me, across, along, _ = near
    return (
        pltpu.make_async_copy(source, target.at[me], keep),
        remote(source, target.at[me], send, arrive, 0, across),
        remote(source, target.at[me], send, arrive, 1, along),
    )


def gather_start(source, target, near, send, arrive, keep):
    started = gather_copies(source, target, near, send, arrive, keep)
    for copy in started:
        copy.start()
    return started


def gather_finish(started, target, near, send, arrive):
    _, across, along, _ = near
    own, first, second = started
    rows = target.shape[1]
    split = half_of(rows)
    head, rest = pl.ds(0, split), pl.ds(split, rows - split)
    first.wait_recv()
    third = remote(target.at[across, head], target.at[across, head], send, arrive, 2, along)
    third.start()
    second.wait_recv()
    fourth = remote(target.at[along, rest], target.at[along, rest], send, arrive, 3, across)
    fourth.start()
    third.wait_recv()
    fourth.wait_recv()
    for copy in (first, second, third, fourth):
        copy.wait_send()
    own.wait()


def gather_kernel(count, inputs, outputs, body, *refs):
    sources, operands = refs[:count], refs[count : count + inputs]
    targets = refs[count + inputs : 2 * count + inputs]
    results = refs[2 * count + inputs : 2 * count + inputs + outputs]
    send, arrive, keep = refs[2 * count + inputs + outputs :]
    near = neighbours()

    def copies(i):
        return gather_copies(sources[i], targets[i], near, send.at[i], arrive.at[i], keep.at[i])

    @pl.when(pl.program_id(0) == 0)
    def _():
        greet(near[1], near[2])
        for i in range(count):
            for copy in copies(i):
                copy.start()

    body(*operands, *results)

    @pl.when(pl.program_id(0) == pl.num_programs(0) - 1)
    def _():
        for i in range(count):
            gather_finish(copies(i), targets[i], near, send.at[i], arrive.at[i])


def nothing(*refs):
    del refs


def beside_gather(number, blocks, work=(nothing, "gather", (1,), [], [], [], [])):
    side, count = lax.axis_size("seq"), len(blocks)
    body, name, grid, out_shape, in_specs, out_specs, operands = work
    if side != 4 and not operands:
        return [lax.all_gather(block, "seq", axis=0) for block in blocks], []
    if side != 4:
        results = pl.pallas_call(
            body, grid=grid, out_shape=out_shape, in_specs=in_specs, out_specs=out_specs, name=name
        )(*operands)
        return [lax.all_gather(block, "seq", axis=0) for block in blocks], results
    anywhere = [pl.BlockSpec(memory_space=pl.ANY)] * count
    moved = sum(block.size for block in blocks)
    results = pl.pallas_call(
        functools.partial(gather_kernel, count, len(operands), len(out_shape), body),
        grid=grid,
        out_shape=[
            jax.ShapeDtypeStruct((side,) + block.shape, block.dtype) for block in blocks
        ]
        + out_shape,
        in_specs=anywhere + in_specs,
        out_specs=anywhere + out_specs,
        scratch_shapes=[
            pltpu.SemaphoreType.DMA((count, 4)),
            pltpu.SemaphoreType.DMA((count, 4)),
            pltpu.SemaphoreType.DMA((count,)),
        ],
        compiler_params=pltpu.CompilerParams(
            collective_id=number, has_side_effects=True, vmem_limit_bytes=40 * 2**20
        ),
        cost_estimate=pl.CostEstimate(flops=0, bytes_accessed=160 * moved, transcendentals=0),
        name=name,
    )(*blocks, *operands)
    return results[:count], results[count:]


def signal_all(peers):
    barrier = pltpu.get_barrier_semaphore()
    for peer in peers:
        pl.semaphore_signal(barrier, inc=1, device_id=peer, device_id_type=pl.DeviceIdType.MESH)
    pl.semaphore_wait(barrier, len(peers))


def send_share(row, first, where, mine, boxes, send, arrive):
    axis, spot, size = where
    copies = []
    for step in range(1, size):
        copies.append(
            pltpu.make_async_remote_copy(
                src_ref=mine.at[row],
                dst_ref=boxes.at[row, spot],
                send_sem=send.at[first + step - 1],
                recv_sem=arrive.at[first + step - 1],
                device_id={axis: (spot + step) % size},
                device_id_type=pl.DeviceIdType.MESH,
            )
        )
        copies[-1].start()
    boxes[row, spot] = mine[row]
    return copies


def add_shares(row, size, copies, boxes):
    for copy in copies:
        copy.wait()
    total = boxes[row, 0]
    for index in range(1, size):
        total = total + boxes[row, index]
    return total


def start_kernel(
    source_ref, small_ref, sources, smalls,
    send, arrive, keep, send_z, arrive_z, keep_z,
):
    near = neighbours()
    _, across, along, _ = near
    here, count = lax.axis_index("fsdp"), lax.axis_size("fsdp")
    sibling = here + 1 - 2 * (here % 2)
    others = [(here + 2 * step) % count for step in range(1, count // 2)]
    barrier = pltpu.get_barrier_semaphore()
    peers = [{"seq": across}, {"seq": along}, {"fsdp": sibling}]
    peers += [{"fsdp": other} for other in others]
    for peer in peers:
        pl.semaphore_signal(barrier, inc=1, device_id=peer, device_id_type=pl.DeviceIdType.MESH)
    pl.semaphore_wait(barrier, len(peers))

    def send_to(source, target, row, slot, other):
        return pltpu.make_async_remote_copy(
            src_ref=source,
            dst_ref=target,
            send_sem=send_z.at[row, slot],
            recv_sem=arrive_z.at[row, slot],
            device_id={"fsdp": other},
            device_id_type=pl.DeviceIdType.MESH,
        )

    flow = [(small_ref, smalls)]
    first = []
    for row, (source, target) in enumerate(flow):
        own = pltpu.make_async_copy(source, target.at[here], keep_z.at[row])
        own.start()
        copies = [send_to(source, target.at[here], row, 0, sibling)]
        copies += [
            send_to(source, target.at[here], row, 1 + i, other) for i, other in enumerate(others)
        ]
        for copy in copies:
            copy.start()
        first.append((own, copies))
    started = [
        gather_start(block, target, near, send.at[i], arrive.at[i], keep.at[i])
        for i, (block, target) in enumerate([(source_ref, sources)])
    ]
    gather_finish(started[0], sources, near, send.at[0], arrive.at[0])
    for row, (source, target) in enumerate(flow):
        own, copies = first[row]
        passed = []
        for i in range(len(others)):
            copies[1 + i].wait_recv()
            origin = target.at[(here + count - 2 * (i + 1)) % count]
            passed.append(send_to(origin, origin, row, 1 + len(others) + i, sibling))
            passed[-1].start()
        copies[0].wait_recv()
        for copy in passed:
            copy.wait_recv()
        for copy in copies + passed:
            copy.wait_send()
        own.wait()


def start_gathers(source, small):
    side, count = lax.axis_size("seq"), lax.axis_size("fsdp")
    if side != 4:
        return (
            lax.all_gather(source, "seq", axis=0),
            lax.all_gather(small, "fsdp", axis=0),
        )
    slots = count - 1
    return pl.pallas_call(
        start_kernel,
        out_shape=[
            jax.ShapeDtypeStruct((many,) + block.shape, block.dtype)
            for block, many in ((source, side), (small, count))
        ],
        in_specs=[pl.BlockSpec(memory_space=pl.ANY)] * 2,
        out_specs=[pl.BlockSpec(memory_space=pl.ANY)] * 2,
        scratch_shapes=[
            pltpu.SemaphoreType.DMA((2, 4)),
            pltpu.SemaphoreType.DMA((2, 4)),
            pltpu.SemaphoreType.DMA((2,)),
            pltpu.SemaphoreType.DMA((2, slots)),
            pltpu.SemaphoreType.DMA((2, slots)),
            pltpu.SemaphoreType.DMA((2,)),
        ],
        compiler_params=pltpu.CompilerParams(collective_id=1, has_side_effects=True),
        cost_estimate=pl.CostEstimate(
            flops=0, bytes_accessed=160 * source.size, transcendentals=0
        ),
        name="start_gathers",
    )(source, small)


TILE = 256
STEP = 16


def reduce_rows_kernel(
    flip, gathers, totals, fills, streamed, epilogue, lefts, in_count, out_count, *refs
):
    streams, refs = refs[-1], refs[:-1]
    held_count = sum(streamed)
    held, refs = refs[-held_count:], refs[:-held_count]
    loads, inputs, spot = [], [], 0
    for source, wanted in zip(refs[:in_count], streamed):
        inputs.append(held[spot] if wanted else source)
        loads.append((source, held[spot]) if wanted else None)
        spot += wanted
    left_refs, right_ref, extra = inputs[:lefts], inputs[lefts], inputs[lefts + 1 :]
    outs = refs[in_count : in_count + out_count]
    far, wide_x, wide_y, own, get_a, get_b, get_x, get_y, send, arrive = refs[
        in_count + out_count : in_count + out_count + 10
    ]
    rest_refs = refs[in_count + out_count + 10 :]
    near = neighbours()
    me, across, along, opposite = near
    rows, width = own.shape
    tiles = width // TILE
    turns = (opposite, across, along, me)

    def left_copy(index, turn):
        source, target = loads[index]
        here = pl.ds(pl.multiple_of(turns[turn] * rows, rows), rows)
        return pltpu.make_async_copy(
            source.at[here], target.at[here], streams.at[index * 4 + turn]
        )

    def right_copy(tile):
        source, target = loads[lefts]
        columns = pl.ds(pl.multiple_of(tile * TILE, TILE), TILE)
        if flip:
            source, target = source.at[columns], target.at[columns]
        else:
            source, target = source.at[:, columns], target.at[:, columns]
        return pltpu.make_async_copy(source, target, streams.at[lefts * 4 + tile])

    def extra_copy(index):
        source, target = loads[lefts + 1 + index]
        return pltpu.make_async_copy(source, target, streams.at[lefts * 4 + tiles + index])

    def need(*indices):
        for index in indices:
            if loads[lefts + 1 + index] is not None:
                extra_copy(index).wait()

    for turn in range(4):
        for index in range(lefts):
            left_copy(index, turn).start()
        if turn == 0:
            for tile in range(tiles):
                right_copy(tile).start()
    for index in range(len(extra)):
        if loads[lefts + 1 + index] is not None:
            extra_copy(index).start()
    if totals:
        mine, boxes, send_t, arrive_t = rest_refs
        spots = [(axis, lax.axis_index(axis), lax.axis_size(axis)) for axis in ("seq", "fsdp")]
        signal_all(
            [{axis: (spot + step) % size} for axis, spot, size in spots for step in range(1, size)]
        )
        mine[0] = extra[-1][...]
        shares = send_share(0, 0, spots[0], mine, boxes, send_t, arrive_t)
    else:
        greet(across, along)
    split = half_of(rows)
    head, rest = pl.ds(0, split), pl.ds(split, rows - split)

    def part(turn, store):
        here = pl.ds(pl.multiple_of(turns[turn] * rows, rows), rows)
        for index in range(lefts):
            left_copy(index, turn).wait()

        @pl.loop(0, tiles)
        def _(tile):
            columns = pl.ds(pl.multiple_of(tile * TILE, TILE), TILE)
            if turn == 0:
                right_copy(tile).wait()
            value, base = 0.0, 0
            for left_ref in left_refs:
                depth = pl.ds(base, left_ref.shape[1])
                if flip:
                    value = value + dotf(left_ref[here, :], right_ref[columns, depth], NT)
                else:
                    value = value + dotf(left_ref[here, :], right_ref[depth, columns], NN)
                base += left_ref.shape[1]
            store[:, columns] = value.astype(store.dtype)

    def term(rows_ref, grads_ref, store):
        @pl.loop(0, rows_ref.shape[1] // TILE)
        def _(tile):
            columns = pl.ds(pl.multiple_of(tile * TILE, TILE), TILE)
            store[columns, :] = low(dotf(rows_ref[:, columns], grads_ref[...], TN))

    def add_into(store, base, source):
        @pl.loop(0, source.shape[0] // STEP)
        def _(index):
            start = pl.multiple_of(index * STEP, STEP)
            there = pl.ds(pl.multiple_of(base + start, STEP), STEP)
            total = store[there, :].astype(jnp.float32) + source[pl.ds(start, STEP), :].astype(
                jnp.float32
            )
            store[there, :] = low(total)

    part(0, far)
    if totals:
        mine[1] = add_shares(0, spots[0][2], shares, boxes)
        shares = send_share(1, spots[0][2] - 1, spots[1], mine, boxes, send_t, arrive_t)
    copies = [
        remote(far.at[head], get_a, send, arrive, 0, across),
        remote(far.at[rest], get_b, send, arrive, 1, along),
    ]
    copies[0].start()
    copies[1].start()
    part(1, wide_x)
    copies.append(remote(wide_x.at[head], get_x.at[head], send, arrive, 2, across))
    copies[2].start()
    part(2, wide_y)
    if fills:
        copies.append(remote(wide_y.at[rest], get_y.at[rest], send, arrive, 3, along))
        copies[3].start()
        need(1, 2)
        term(extra[1], extra[2], outs[1])
    else:
        copies.append(remote(wide_y.at[rest], get_y.at[rest], send, arrive, 3, along))
        copies[3].start()
    copies[0].wait_recv()
    add_into(wide_y, 0, get_a)
    copies.append(remote(wide_y.at[head], get_y.at[head], send, arrive, 4, along))
    copies[4].start()
    copies[1].wait_recv()
    add_into(wide_x, split, get_b)
    copies.append(remote(wide_x.at[rest], get_x.at[rest], send, arrive, 5, across))
    copies[5].start()
    if fills:
        need(3)
        term(extra[1], extra[3], outs[2])
    part(3, own)
    need(*([0] if fills else range(len(extra))))
    for copy in copies[2:]:
        copy.wait_recv()
    epilogue_prepare = rest_refs[0] if gathers else None

    @pl.loop(0, rows // STEP)
    def _(index):
        here = pl.ds(pl.multiple_of(index * STEP, STEP), STEP)
        total = (
            own[here, :] + get_x[here, :].astype(jnp.float32) + get_y[here, :].astype(jnp.float32)
        )
        epilogue(index, here, total, extra, outs, epilogue_prepare)

    for copy in copies:
        copy.wait_send()
    if totals:
        outs[-1][...] = add_shares(1, spots[1][2], shares, boxes)
    if gathers:
        block, send_2, arrive_2, keep = rest_refs
        target = outs[0]
        started = gather_start(block, target, near, send_2, arrive_2, keep.at[0])
        gather_finish(started, target, near, send_2, arrive_2)


def rms_back(grad, values, gain):
    r = lax.rsqrt(jnp.mean(values * values, axis=-1, keepdims=True) + EPS)
    scaled = grad * gain
    change = r * (scaled - values * (r * r) * jnp.mean(scaled * values, axis=-1, keepdims=True))
    return change


def middle_epilogue(index, here, total, extra, outs, block):
    source_ref, gain_ref = extra
    middle = source_ref[here, :].astype(jnp.float32) + total
    outs[1][here, :] = middle
    r = lax.rsqrt(jnp.mean(middle * middle, axis=-1, keepdims=True) + EPS)
    block[here, :] = low(middle * r * gain_ref[...])


def output_epilogue(index, here, total, extra, outs, block):
    outs[0][here, :] = low(extra[0][here, :] + total)


def branch_epilogue(index, here, total, extra, outs, block):
    middle_ref, upstream_ref, gain_ref = extra
    change = rms_back(total, middle_ref[here, :], gain_ref[...])
    grad = upstream_ref[here, :].astype(jnp.float32) + change
    outs[1][here, :] = grad
    block[here, :] = low(grad)


def input_epilogue(index, here, total, extra, outs, block):
    source_ref, carried_ref, gain_ref, _ = extra
    change = rms_back(total, source_ref[here, :].astype(jnp.float32), gain_ref[...])
    outs[0][here, :] = carried_ref[here, :] + change


def fused_reduce(name, number, flip, mode, epilogue, outs, lefts, right, *extra):
    gathers, totals = mode == "gather", mode == "total"
    side = lax.axis_size("seq")
    length = lefts[0].shape[0]
    rows = length // side
    width = right.shape[0] if flip else right.shape[1]
    split = half_of(rows)
    scratch = [
        pltpu.VMEM((rows, width), jnp.bfloat16),
        pltpu.VMEM((rows, width), jnp.bfloat16),
        pltpu.VMEM((rows, width), jnp.bfloat16),
        pltpu.VMEM((rows, width), jnp.float32),
        pltpu.VMEM((split, width), jnp.bfloat16),
        pltpu.VMEM((rows - split, width), jnp.bfloat16),
        pltpu.VMEM((rows, width), jnp.bfloat16),
        pltpu.VMEM((rows, width), jnp.bfloat16),
        pltpu.SemaphoreType.DMA((6,)),
        pltpu.SemaphoreType.DMA((6,)),
    ]
    out_specs = in_vmem(len(outs))
    if totals:
        shape, f_count = extra[-1].shape, lax.axis_size("fsdp")
        peers = side + f_count - 2
        scratch += [
            pltpu.VMEM((2,) + shape, jnp.float32),
            pltpu.VMEM((2, max(side, f_count)) + shape, jnp.float32),
            pltpu.SemaphoreType.DMA((peers,)),
            pltpu.SemaphoreType.DMA((peers,)),
        ]
    if gathers:
        scratch += [
            pltpu.VMEM((rows, width), jnp.bfloat16),
            pltpu.SemaphoreType.DMA((4,)),
            pltpu.SemaphoreType.DMA((4,)),
            pltpu.SemaphoreType.DMA((1,)),
        ]
        out_specs[0] = pl.BlockSpec(memory_space=pl.ANY)
    inputs = [*lefts, right, *extra]
    streamed = tuple(array.size > 2**16 for array in inputs)
    scratch += [
        pltpu.VMEM(array.shape, array.dtype) for array, wanted in zip(inputs, streamed) if wanted
    ]
    scratch.append(pltpu.SemaphoreType.DMA((len(lefts) * 4 + width // TILE + len(extra),)))
    return pl.pallas_call(
        functools.partial(
            reduce_rows_kernel,
            flip,
            gathers,
            totals,
            mode == "fill",
            streamed,
            epilogue,
            len(lefts),
            len(lefts) + 1 + len(extra),
            len(outs),
        ),
        out_shape=outs,
        in_specs=[
            pl.BlockSpec(memory_space=pl.ANY if wanted else pltpu.VMEM) for wanted in streamed
        ],
        out_specs=out_specs,
        scratch_shapes=scratch,
        compiler_params=pltpu.CompilerParams(
            collective_id=number, has_side_effects=True, vmem_limit_bytes=56 * 2**20
        ),
        cost_estimate=pl.CostEstimate(
            flops=2 * sum(left.size for left in lefts) * width,
            bytes_accessed=(320 if gathers else 160) * rows * width,
            transcendentals=0,
        ),
        name=name,
    )(*lefts, right, *extra)


def seq_sum(partial, side):
    block = low(partial).reshape(side, -1, partial.shape[-1])
    return lax.psum_scatter(block, "seq", scatter_dimension=0).astype(jnp.float32)


def out_and_norm(attn_in, weight, source, gain):
    side = lax.axis_size("seq")
    rows, width = source.shape
    if side != 4:
        middle = source.astype(jnp.float32) + seq_sum(dotf(attn_in, weight, NN), side)
        r = lax.rsqrt(jnp.mean(middle * middle, axis=-1, keepdims=True) + EPS)
        return lax.all_gather(low(middle * r * gain), "seq", axis=0), middle
    outs = (
        jax.ShapeDtypeStruct((side, rows, width), jnp.bfloat16),
        jax.ShapeDtypeStruct((rows, width), jnp.float32),
    )
    return fused_reduce(
        "out_and_norm", 2, False, "gather", middle_epilogue, outs, [attn_in], weight, source, gain
    )


def place_kernel(side, *refs):
    target_ref = refs[side]
    me = lax.axis_index("seq")
    for spot in range(side):

        @pl.when(me == spot)
        def _():
            for index in range(side):
                target_ref[index] = refs[index ^ spot][...].astype(target_ref.dtype)


def place_work(blocks, kind):
    side = len(blocks)
    rows, width = blocks[0].shape
    tile = 512
    return (
        functools.partial(place_kernel, side),
        "place",
        (width // tile,),
        [jax.ShapeDtypeStruct((side, rows, width), kind)],
        [pl.BlockSpec((rows, tile), lambda i: (0, i))] * side,
        [pl.BlockSpec((side, rows, tile), lambda i: (0, 0, i))],
        blocks,
    )


def place(blocks, kind):
    body, name, grid, out_shape, in_specs, out_specs, operands = place_work(blocks, kind)
    return pl.pallas_call(
        body, grid=grid, out_shape=out_shape, in_specs=in_specs, out_specs=out_specs, name=name
    )(*operands)[0]


def swap(block, step):
    pairs = [(i, i ^ step) for i in range(lax.axis_size("seq"))]
    return lax.ppermute(block, "seq", pairs)


def down_and_terms(hidden, weight, middle, ffn_in, grads):
    side = lax.axis_size("seq")
    if side != 4:
        output = low(middle + seq_sum(dotf(hidden, weight, NN), side))
        return output, *[low(dotf(ffn_in, grad, TN)) for grad in grads]
    term = jax.ShapeDtypeStruct((ffn_in.shape[1], grads[0].shape[1]), jnp.bfloat16)
    outs = (jax.ShapeDtypeStruct(middle.shape, jnp.bfloat16), term, term)
    return fused_reduce(
        "down_and_terms", 3, False, "fill", output_epilogue, outs, [hidden], weight, middle, ffn_in,
        *grads,
    )


def branch_grad(grads, weight, middle, upstream, gain):
    side = lax.axis_size("seq")
    rows, width = middle.shape
    if side != 4:
        grad = jnp.concatenate(grads, axis=1)
        change = rms_back(seq_sum(dotf(grad, weight, NT), side), middle, gain)
        total = upstream.astype(jnp.float32) + change
        return lax.all_gather(low(total), "seq", axis=0), total
    outs = (
        jax.ShapeDtypeStruct((side, rows, width), jnp.bfloat16),
        jax.ShapeDtypeStruct((rows, width), jnp.float32),
    )
    return fused_reduce(
        "branch_grad", 4, True, "gather", branch_epilogue, outs, grads, weight, middle, upstream, gain
    )


def input_grad(grad, weight, source, carried, gain, value):
    side = lax.axis_size("seq")
    if side != 4:
        partial = dotf(grad, weight[:, : grad.shape[1]], NT)
        change = rms_back(seq_sum(partial, side), source.astype(jnp.float32), gain)
        return carried + change, lax.psum(value, ("fsdp", "seq"))
    outs = (
        jax.ShapeDtypeStruct(carried.shape, jnp.float32),
        jax.ShapeDtypeStruct(value.shape, jnp.float32),
    )
    return fused_reduce(
        "input_grad", 5, True, "total", input_epilogue, outs, [grad], weight, source, carried, gain,
        value,
    )


def pick_kernel(side, share, source_ref, target_ref):
    me = lax.axis_index("seq")
    count = target_ref.shape[1] // share
    for index in range(side):

        @pl.when(me == index)
        def _():
            pieces = [
                source_ref[:, pl.ds((k * side + index) * share, share)].astype(jnp.float32)
                for k in range(count)
            ]
            target_ref[...] = low(jnp.concatenate(pieces, axis=1))


def pick_columns(weight, share):
    side = lax.axis_size("seq")
    rows, width = weight.shape
    tile = 32
    return pl.pallas_call(
        functools.partial(pick_kernel, side, share),
        grid=(rows // tile,),
        out_shape=jax.ShapeDtypeStruct((rows, width // side), weight.dtype),
        in_specs=[pl.BlockSpec((tile, width), lambda i: (i, 0))],
        out_specs=pl.BlockSpec((tile, width // side), lambda i: (i, 0)),
        name="pick_columns",
    )(weight)


def spread_kernel(side, share, *refs):
    gate_refs, (up_ref, weight_ref, target_ref, total_ref) = refs[:side], refs[side:]
    count = up_ref.shape[2] // share
    me = lax.axis_index("seq")
    half = target_ref.shape[1] // 2

    def place(pieces, base):
        grad = jnp.concatenate([piece.astype(jnp.float32) for piece in pieces], axis=1)
        target_ref[:, pl.ds(base, half)] = low(grad)
        weight = weight_ref[:, pl.ds(base, half)].astype(jnp.float32)
        return jnp.sum(grad * weight, axis=1, keepdims=True)

    spans = [(pl.ds(k * share, share), index) for k in range(count) for index in range(side)]
    total = place([up_ref[index, :, span] for span, index in spans], half)
    for spot in range(side):

        @pl.when(me == spot)
        def _():
            whole = total + place([gate_refs[index ^ spot][:, span] for span, index in spans], 0)
            total_ref[...] = jnp.broadcast_to(whole, total_ref.shape)


def spread_work(gates, up, weight, share):
    side, rows, width = up.shape
    tile = 32
    by_row = pl.BlockSpec((tile, 2 * width * side), lambda i: (i, 0))
    return (
        functools.partial(spread_kernel, side, share),
        "spread",
        (rows // tile,),
        [
            jax.ShapeDtypeStruct((rows, 2 * width * side), jnp.bfloat16),
            jax.ShapeDtypeStruct((rows, DK), jnp.float32),
        ],
        [pl.BlockSpec((tile, width), lambda i: (i, 0))] * side
        + [pl.BlockSpec((side, tile, width), lambda i: (0, i, 0)), by_row],
        [by_row, pl.BlockSpec((tile, DK), lambda i: (i, 0))],
        [*gates, up, weight],
    )


def assemble_kernel(
    side, wide, taps, grad_ref, weight_ref, beta_ref, target_ref, total_ref, rest_ref
):
    heads = wide // DK
    total = 0.0
    for part in range(3):
        for index in range(side):
            columns = pl.ds((part * side + index) * wide, wide)
            grad = grad_ref[index, :, pl.ds(part * wide, wide)].astype(jnp.float32)
            target_ref[:, columns] = grad
            weight = weight_ref[:, columns].astype(jnp.float32)
            total = total + jnp.sum(grad * weight, axis=1, keepdims=True)
    lane = lax.broadcasted_iota(jnp.int32, beta_ref.shape, 1)
    beta, conv = 0.0, 0.0
    for index in range(side):
        rest = grad_ref[index, :, pl.ds(3 * wide, DK)].astype(jnp.float32)
        mine = jnp.where(lane < heads, rest, 0.0)
        beta = beta + (pltpu.roll(mine, index * heads, 1) if index else mine)
        conv = conv + rest
    conv = jnp.where((lane >= heads) & (lane < heads + 3 * taps), conv, 0.0)
    if side > 1:
        conv = pltpu.roll(conv, H - heads, 1)
    total = total + jnp.sum(beta * beta_ref[...].astype(jnp.float32), axis=1, keepdims=True)
    total_ref[...] = jnp.broadcast_to(total, total_ref.shape)
    rest_ref[...] = (beta + conv).T


def assemble_columns(grad, weight, beta, wide, taps):
    side, rows, depth = grad.shape
    tile = min(rows, DK)
    by_row = pl.BlockSpec((tile, weight.shape[1]), lambda i: (i, 0))
    narrow = pl.BlockSpec((tile, DK), lambda i: (i, 0))
    return pl.pallas_call(
        functools.partial(assemble_kernel, side, wide, taps),
        grid=(rows // tile,),
        out_shape=(
            jax.ShapeDtypeStruct(weight.shape, jnp.float32),
            jax.ShapeDtypeStruct((rows, DK), jnp.float32),
            jax.ShapeDtypeStruct((DK, rows), jnp.float32),
        ),
        in_specs=[pl.BlockSpec((side, tile, depth), lambda i: (0, i, 0)), by_row, narrow],
        out_specs=(by_row, narrow, pl.BlockSpec((DK, tile), lambda i: (0, i))),
        compiler_params=pltpu.CompilerParams(vmem_limit_bytes=40 * 2**20),
        name="assemble_columns",
    )(grad, weight, beta)


def fsdp_sum(term):
    return lax.psum_scatter(low(term), "fsdp", scatter_dimension=0, tiled=True)


def per_device(
    inputs,
    cotangent,
    norm1_gain,
    w_qkv,
    w_beta,
    conv_weight,
    out_gain,
    w_out,
    norm2_gain,
    w_gate_up,
    w_down,
):
    side = lax.axis_size("seq")
    s = lax.axis_index("seq")
    shape = inputs.shape
    width = shape[2]
    source = inputs.reshape(-1, width)
    upstream = cotangent.reshape(-1, width)
    length = source.shape[0] * side
    heads = H // side
    wide = heads * DK
    rows = w_qkv.shape[0]
    share = w_down.shape[0] // side
    taps = conv_weight.shape[1] // 3

    f_count = lax.axis_size("fsdp")
    depth = 3 * wide + DK
    homes = [
        (f * side + i, (side * (f % 2) + i) * side + f // 2)
        for f in range(f_count)
        for i in range(side)
    ]

    def everywhere(block):
        return lax.all_gather(block, "fsdp", axis=0, tiled=True)

    parts = [
        lax.dynamic_slice_in_dim(w_qkv, part * width + s * wide, wide, 1) for part in range(3)
    ]
    beta_part = lax.dynamic_slice_in_dim(w_beta, s * heads, heads, 1)
    parts.append(jnp.pad(beta_part, ((0, 0), (0, DK - heads))))
    parts.append(lax.dynamic_slice_in_dim(w_out, s * wide, wide, 1))
    qkv_part = everywhere(jnp.concatenate(parts, axis=1))
    small = jnp.concatenate([norm1_gain[None], norm2_gain[None], conv_weight.T], axis=0)
    small = jnp.pad(small, ((0, 16 - small.shape[0]), (0, 0)))
    source_all, small = start_gathers(source, small)
    sent, source_all = lax.optimization_barrier((upstream, source_all))
    out_part = lax.all_to_all(
        qkv_part[:, depth:], "seq", split_axis=0, concat_axis=1, tiled=True
    )
    upstreams = [upstream] + [swap(sent, step) for step in range(1, side)]
    small = small.transpose(1, 0, 2).reshape(small.shape[1], width).astype(jnp.float32)
    gain_first = small[0:1]
    gain_second = small[1:2]
    table = lax.dynamic_slice_in_dim(small[2 : 2 + 3 * taps], s * wide, wide, 1)
    gain_heads = out_gain.astype(jnp.float32)[None]
    source_all = source_all.reshape(length, width).astype(jnp.float32)

    picked = pick_columns(w_gate_up, share)
    gate_up_part = everywhere(picked)
    down_part = everywhere(lax.dynamic_slice_in_dim(w_down, s * share, share, 0))

    normed_first = low(
        source_all
        * lax.rsqrt(jnp.mean(source_all * source_all, axis=-1, keepdims=True) + EPS)
        * gain_first
    )
    projected = low(dotf(normed_first, qkv_part[:, : 3 * wide], NN))
    beta_logits = dotf(normed_first, qkv_part[:, 3 * wide : depth], NN)
    attn_in, *kept = mix_forward(projected, beta_logits, table, gain_heads)
    attn_in, *upstreams = lax.optimization_barrier((attn_in, *upstreams))
    upstream_all = place(upstreams, jnp.bfloat16).reshape(length, width)
    ffn_in, middle = out_and_norm(attn_in, out_part, source, gain_second)
    ffn_in = ffn_in.reshape(length, width)
    gate_up = dotf(ffn_in, gate_up_part, NN)
    hidden_width = gate_up.shape[1] // 2
    gate = gate_up[:, :hidden_width]
    upward = gate_up[:, hidden_width:]
    sigma = jax.nn.sigmoid(gate)
    hidden = low(gate * sigma * upward)

    down_term = low(dotf(hidden, upstream_all, TN))
    grad_down = fsdp_sum(down_term)
    upstream_all, _ = lax.optimization_barrier((upstream_all, down_term))
    grad_hidden = dotf(upstream_all, down_part, NT)
    grad_gate = low(grad_hidden * upward * sigma * (1.0 + gate * (1.0 - sigma)))
    grad_up = low(grad_hidden * gate * sigma)
    output, gate_term, up_term = down_and_terms(
        hidden, down_part, middle, ffn_in, [grad_gate, grad_up]
    )
    gate_sum = fsdp_sum(gate_term)
    up_sum = fsdp_sum(up_term)
    grad_gate, grad_up, grad_down = lax.optimization_barrier((grad_gate, grad_up, grad_down))
    grad_branch, grad_middle = branch_grad(
        [grad_gate, grad_up], gate_up_part, middle, upstream, gain_second
    )
    grad_branch, grad_down, gate_sum = lax.optimization_barrier(
        (grad_branch, grad_down, gate_sum)
    )
    grad_branch = grad_branch.reshape(length, width)
    downs = [grad_down] + [swap(grad_down, step) for step in range(1, side)]
    gates = [gate_sum] + [swap(gate_sum, step) for step in range(1, side)]

    out_term = low(dotf(attn_in, grad_branch, TN))
    grad_attn_in, _ = lax.optimization_barrier((dotf(grad_branch, out_part, NT), out_term))
    grad_proj, grad_table, grad_gain_heads = mix_backward(
        projected, beta_logits, table, gain_heads, *kept, grad_attn_in
    )
    grad_proj, up_sum, *downs = lax.optimization_barrier((grad_proj, up_sum, *downs))
    grad_qkv = low(dotf(normed_first, grad_proj, TN))
    grad_qkv = lax.dynamic_update_slice(
        grad_qkv, low(grad_table.T), (s * wide, 3 * wide + heads)
    )
    grad_down = place(downs, jnp.float32)
    grad_proj, grad_qkv, out_term, grad_down, *gates = lax.optimization_barrier(
        (grad_proj, grad_qkv, out_term, grad_down, *gates)
    )
    grad_qkv = fsdp_sum(grad_qkv)
    grad_input, grad_out_gain = input_grad(
        grad_proj, qkv_part, source, grad_middle, gain_first,
        jnp.broadcast_to(grad_gain_heads, (8, DK)),
    )
    up_sum, grad_input = lax.optimization_barrier((up_sum, grad_input))
    (up_sum,), _ = beside_gather(7, [up_sum])
    out_term, grad_qkv, up_sum = lax.optimization_barrier((out_term, grad_qkv, up_sum))
    out_sum = fsdp_sum(out_term)
    (grad_qkv,), (grad_w_gate_up, second_total) = beside_gather(
        9, [grad_qkv], spread_work(gates, up_sum, w_gate_up, share)
    )
    out_sum = lax.ppermute(out_sum, ("fsdp", "seq"), [(b, a) for a, b in homes])
    (grad_w_out,), _ = beside_gather(8, [out_sum])
    wide_beta = jnp.pad(w_beta, ((0, 0), (0, DK - H)))
    grad_w_qkv, first_total, rest = assemble_columns(grad_qkv, w_qkv, wide_beta, wide, taps)
    return (
        output.reshape(shape),
        grad_input.reshape(shape),
        first_total[:, 0] / norm1_gain.astype(jnp.float32),
        grad_w_qkv,
        rest[:H].T,
        rest[H : H + 3 * taps].T,
        grad_out_gain[0],
        grad_w_out.reshape(rows, width).astype(jnp.float32),
        second_total[:, 0] / norm2_gain.astype(jnp.float32),
        grad_w_gate_up.astype(jnp.float32),
        grad_down.reshape(side * share, width),
    )


def solution(mesh):
    by_row = P("fsdp", None)
    tokens = P("fsdp", "seq", None)
    specs = (tokens, tokens, P("fsdp"), by_row, by_row, by_row, P(), by_row, P("fsdp"))
    specs = specs + (by_row, by_row)
    return jax.shard_map(per_device, mesh=mesh, in_specs=specs, out_specs=specs, check_vma=False)
```

```python
import functools

import jax
import jax.numpy as jnp
from jax import lax
from jax.experimental import pallas as pl
from jax.experimental.pallas import tpu as pltpu
from jax.sharding import PartitionSpec as P

H = 16
DK = 128
EPS = 1e-06
CHUNK = 128
HEAD_ROOM = 8


def dotf(left, right, dims):
    return lax.dot_general(left, right, (dims, ((), ())), preferred_element_type=jnp.float32)


NN = ((1,), (0,))
NT = ((1,), (1,))
TN = ((0,), (0,))


def low(value):
    return value.astype(jnp.bfloat16)


def square_iota(axis):
    return lax.broadcasted_iota(jnp.int32, (CHUNK, CHUNK), axis)


def sigmoid(value):
    return 1.0 / (1.0 + jnp.exp(-value))


def conv_chunk(window, taps, count):
    mixed = window[HEAD_ROOM:] * taps[count - 1]
    for back in range(1, count):
        mixed = mixed + pltpu.roll(window, back, 0)[HEAD_ROOM:] * taps[count - 1 - back]
    return mixed


def window_of(ahead_ref, proj_ref, chunk, column):
    lanes = pl.ds(column, DK)
    before = ahead_ref[:, lanes].astype(jnp.float32)[8:]
    before = jnp.where(chunk > 0, before, 0.0)
    return jnp.concatenate([before, proj_ref[:, lanes].astype(jnp.float32)], axis=0)


def head_inputs(ahead_ref, proj_ref, table_ref, chunk, head, heads, taps):
    wide = heads * DK
    found = []
    for part in range(3):
        window = window_of(ahead_ref, proj_ref, chunk, part * wide + head * DK)
        weights = [
            table_ref[pl.ds(part * taps + tap, 1), pl.ds(head * DK, DK)] for tap in range(taps)
        ]
        mixed = conv_chunk(window, weights, taps)
        gate = sigmoid(mixed)
        found.append((window, weights, mixed, gate, mixed * gate))
    active_key = found[1][4]
    scale = lax.rsqrt(jnp.sum(active_key * active_key, axis=-1, keepdims=True) + EPS)
    key = active_key * scale
    return found, found[0][4] * DK**-0.5, key, scale, found[2][4]


def inverses_of(stricts):
    row, column = square_iota(0), square_iota(1)
    eye = (row == column).astype(jnp.float32)
    solved = [eye - jnp.where(row // 2 == column // 2, strict, 0.0) for strict in stricts]
    half = 2
    while half < CHUNK:
        below = (row // (2 * half) == column // (2 * half)) & (row // half != column // half)
        off = [low(jnp.where(below, strict, 0.0)) for strict in stricts]
        known = [low(item) for item in solved]
        first = [low(dotf(k, o, NN)) for k, o in zip(known, off)]
        second = [dotf(p, k, NN) for p, k in zip(first, known)]
        solved = [item - change for item, change in zip(solved, second)]
        half *= 2
    return [low(item) for item in solved]


def forward_kernel(
    heads, taps, ahead_ref, proj_ref, logit_ref, table_ref, gain_ref,
    normed_ref, raw_ref, fresh_ref, solve_ref, state_ref, carry,
):
    every = range(heads)
    chunk = pl.program_id(0)

    @pl.when(chunk == 0)
    def _():
        carry[...] = jnp.zeros_like(carry)

    row, column = square_iota(0), square_iota(1)
    beta_all = low(sigmoid(logit_ref[...])).astype(jnp.float32)
    beta = [beta_all[:, h : h + 1] for h in every]
    ready = [head_inputs(ahead_ref, proj_ref, table_ref, chunk, h, heads, taps) for h in every]
    query = [low(item[1]) for item in ready]
    key = [low(item[2]) for item in ready]
    value = [low(item[4]) for item in ready]
    gram = [dotf(key[h], key[h], NT) for h in every]
    score = [dotf(query[h], key[h], NT) for h in every]
    strict = [jnp.where(row > column, gram[h] * beta[h], 0.0) for h in every]
    within = [low(jnp.where(row >= column, score[h], 0.0)) for h in every]
    solved = inverses_of(strict)
    state = [carry[h] for h in every]
    state_low = [low(item) for item in state]
    recalled = [dotf(key[h], state_low[h], NN) for h in every]
    rest = [low(beta[h] * (value[h].astype(jnp.float32) - recalled[h])) for h in every]
    fresh = [low(dotf(solved[h], rest[h], NN)) for h in every]
    grown = [dotf(key[h], fresh[h], TN) for h in every]
    for h in every:
        carry[h] = state[h] + grown[h]
    past = [dotf(query[h], state_low[h], NN) for h in every]
    inner = [dotf(within[h], fresh[h], NN) for h in every]
    for h in every:
        lanes = pl.ds(h * DK, DK)
        raw = low(past[h] + inner[h])
        wide_raw = raw.astype(jnp.float32)
        normed = wide_raw * lax.rsqrt(
            jnp.mean(wide_raw * wide_raw, axis=-1, keepdims=True) + EPS
        )
        normed_ref[:, lanes] = low(normed * gain_ref[...])
        raw_ref[:, lanes] = raw
        fresh_ref[:, lanes] = fresh[h]
        solve_ref[0, h] = solved[h]
        state_ref[0, h] = state_low[h]


def backward_kernel(
    heads, taps, ahead_ref, proj_ref, logit_ref, table_ref, gain_ref, raw_ref, fresh_ref, solve_ref,
    state_ref, grad_ref, gproj_ref, gtable_ref, ggain_ref, carry, after,
):
    wide = heads * DK
    every = range(heads)
    chunk = pl.num_programs(0) - 1 - pl.program_id(0)

    @pl.when(pl.program_id(0) == 0)
    def _():
        carry[...] = jnp.zeros_like(carry)
        after[...] = jnp.zeros_like(after)
        gtable_ref[...] = jnp.zeros_like(gtable_ref)
        ggain_ref[...] = jnp.zeros_like(ggain_ref)

    row, column = square_iota(0), square_iota(1)
    beta_wide = sigmoid(logit_ref[...])
    beta_all = low(beta_wide).astype(jnp.float32)
    beta = [beta_all[:, h : h + 1] for h in every]
    lane = lax.broadcasted_iota(jnp.int32, (CHUNK, DK), 1)
    ready = [head_inputs(ahead_ref, proj_ref, table_ref, chunk, h, heads, taps) for h in every]
    query = [low(item[1]) for item in ready]
    key = [low(item[2]) for item in ready]
    value = [low(item[4]) for item in ready]
    grad_out = []
    for h in every:
        lanes = pl.ds(h * DK, DK)
        raw = raw_ref[:, lanes].astype(jnp.float32)
        grad_normed = grad_ref[:, lanes].astype(jnp.float32)
        r = lax.rsqrt(jnp.mean(raw * raw, axis=-1, keepdims=True) + EPS)
        scaled = grad_normed * gain_ref[...]
        mean = jnp.mean(scaled * raw, axis=-1, keepdims=True)
        grad_out.append(low(r * (scaled - raw * (r * r) * mean)))
        ggain_ref[...] += jnp.sum(grad_normed * raw * r, axis=0, keepdims=True)
    state = [state_ref[0, h] for h in every]
    solved = [solve_ref[0, h] for h in every]
    fresh = [fresh_ref[:, pl.ds(h * DK, DK)] for h in every]
    later = [carry[h] for h in every]
    later_low = [low(item) for item in later]
    score = [dotf(query[h], key[h], NT) for h in every]
    onward = [dotf(key[h], later_low[h], NN) for h in every]
    within = [low(jnp.where(row >= column, item, 0.0)) for item in score]
    grad_fresh = [low(dotf(within[h], grad_out[h], TN) + onward[h]) for h in every]
    grad_solved = [dotf(solved[h], grad_fresh[h], TN) for h in every]
    grad_value = [beta[h] * grad_solved[h] for h in every]
    grad_rest = [low(item) for item in grad_value]
    asked = [dotf(query[h], grad_out[h], TN) for h in every]
    taken = [dotf(key[h], grad_rest[h], TN) for h in every]
    for h in every:
        carry[h] = later[h] + asked[h] - taken[h]
    gram = [dotf(key[h], key[h], NT) for h in every]
    recalled = [dotf(key[h], state[h], NN) for h in every]
    product = [dotf(grad_out[h], fresh[h], NT) for h in every]
    cross = [dotf(low(grad_solved[h]), fresh[h], NT) for h in every]
    grad_within = [low(jnp.where(row >= column, item, 0.0)) for item in product]
    grad_strict = [jnp.where(row > column, -item, 0.0) for item in cross]
    mixing = [low(beta[h] * grad_strict[h]) for h in every]
    grad_query = [
        dotf(grad_out[h], state[h], NT) + dotf(grad_within[h], key[h], NN) for h in every
    ]
    grad_key = [
        dotf(grad_within[h], query[h], TN)
        + dotf(fresh[h], later_low[h], NT)
        - dotf(grad_rest[h], state[h], NT)
        + dotf(mixing[h], key[h], NN)
        + dotf(mixing[h], key[h], TN)
        for h in every
    ]
    glogit = jnp.zeros((CHUNK, DK), jnp.float32)
    for h in every:
        rest = value[h].astype(jnp.float32) - recalled[h]
        grad_beta = jnp.sum(grad_solved[h] * rest, axis=-1, keepdims=True) + jnp.sum(
            grad_strict[h] * gram[h], axis=-1, keepdims=True
        )
        bw = beta_wide[:, h : h + 1]
        grad_beta = low(grad_beta).astype(jnp.float32) * bw * (1.0 - bw)
        glogit = glogit + jnp.where(lane == h, grad_beta, 0.0)
    gproj_ref[:, pl.ds(3 * wide, DK)] = low(glogit)
    for h in every:
        found, _, key_wide, scale, _ = ready[h]
        lanes = pl.ds(h * DK, DK)
        back_query = low(grad_query[h]).astype(jnp.float32) * DK**-0.5
        back_key = low(grad_key[h]).astype(jnp.float32)
        back_key = scale * (
            back_key - key_wide * jnp.sum(back_key * key_wide, axis=-1, keepdims=True)
        )
        back_value = low(grad_value[h]).astype(jnp.float32)
        for part, grad_active in enumerate((back_query, back_key, back_value)):
            window, weights, mixed, gate, _ = found[part]
            grad_conv = grad_active * (gate * (1.0 + mixed * (1.0 - gate)))
            columns = pl.ds(part * wide + h * DK, DK)
            tail = jnp.concatenate([grad_conv, after[:, columns]], axis=0)
            size = CHUNK + HEAD_ROOM
            total = grad_conv * weights[taps - 1]
            for back in range(1, taps):
                ahead = pltpu.roll(tail, size - back, 0)[:CHUNK]
                total = total + ahead * weights[taps - 1 - back]
            gproj_ref[:, columns] = low(total)
            after[:, columns] = grad_conv[:HEAD_ROOM]
            for back in range(taps):
                shifted = pltpu.roll(window, back, 0)[HEAD_ROOM:] if back else window[HEAD_ROOM:]
                spot = pl.ds(part * taps + taps - 1 - back, 1)
                gtable_ref[spot, lanes] += jnp.sum(grad_conv * shifted, axis=0, keepdims=True)


def in_vmem(count):
    return [pl.BlockSpec(memory_space=pltpu.VMEM)] * count


def mix_specs(heads, wide, turn):
    ratio = CHUNK // 16
    proj = [
        pl.BlockSpec((16, 3 * wide), lambda i: (jnp.maximum(turn(i) * ratio - 1, 0), 0)),
        pl.BlockSpec((CHUNK, 3 * wide), lambda i: (turn(i), 0)),
        pl.BlockSpec((CHUNK, DK), lambda i: (turn(i), 0)),
    ]
    rows = pl.BlockSpec((CHUNK, wide), lambda i: (turn(i), 0))
    square = [
        pl.BlockSpec((1, heads, size, size), lambda i: (turn(i), 0, 0, 0)) for size in (CHUNK, DK)
    ]
    return proj, rows, square


def whole_of(shape):
    return pl.BlockSpec(shape, lambda i: (0,) * len(shape))


def mix_forward(proj, logits, table, gain):
    length = proj.shape[0]
    heads = table.shape[1] // DK
    taps = table.shape[0] // 3
    count = length // CHUNK
    wide = heads * DK
    shape = jax.ShapeDtypeStruct
    specs, rows, square = mix_specs(heads, wide, lambda i: i)
    return pl.pallas_call(
        functools.partial(forward_kernel, heads, taps),
        grid=(count,),
        out_shape=(
            shape((length, wide), jnp.bfloat16),
            shape((length, wide), jnp.bfloat16),
            shape((length, wide), jnp.bfloat16),
            shape((count, heads, CHUNK, CHUNK), jnp.bfloat16),
            shape((count, heads, DK, DK), jnp.bfloat16),
        ),
        in_specs=specs + [whole_of(table.shape), whole_of(gain.shape)],
        out_specs=(rows, rows, rows, *square),
        scratch_shapes=[pltpu.VMEM((heads, DK, DK), jnp.float32)],
        compiler_params=pltpu.CompilerParams(vmem_limit_bytes=32 * 2**20),
        cost_estimate=pl.CostEstimate(
            flops=length * heads * DK * 40000,
            bytes_accessed=16 * length * wide,
            transcendentals=3 * length * wide,
        ),
        name="mix_forward",
    )(proj, proj, logits, table, gain)


def mix_backward(proj, logits, table, gain, raw, fresh, solved, states, grad):
    length = proj.shape[0]
    heads = table.shape[1] // DK
    taps = table.shape[0] // 3
    count = length // CHUNK
    wide = heads * DK
    shape = jax.ShapeDtypeStruct

    def turn(i):
        return count - 1 - i

    specs, rows, square = mix_specs(heads, wide, turn)
    return pl.pallas_call(
        functools.partial(backward_kernel, heads, taps),
        grid=(count,),
        out_shape=(
            shape((length, 3 * wide + DK), jnp.bfloat16),
            shape((3 * taps, wide), jnp.float32),
            shape((1, DK), jnp.float32),
        ),
        in_specs=specs
        + [whole_of(table.shape), whole_of(gain.shape), rows, rows, *square, rows],
        out_specs=(
            pl.BlockSpec((CHUNK, 3 * wide + DK), lambda i: (turn(i), 0)),
            whole_of((3 * taps, wide)),
            whole_of((1, DK)),
        ),
        scratch_shapes=[
            pltpu.VMEM((heads, DK, DK), jnp.float32),
            pltpu.VMEM((HEAD_ROOM, 3 * wide), jnp.float32),
        ],
        compiler_params=pltpu.CompilerParams(vmem_limit_bytes=32 * 2**20),
        cost_estimate=pl.CostEstimate(
            flops=length * heads * DK * 40000,
            bytes_accessed=26 * length * wide,
            transcendentals=3 * length * wide,
        ),
        name="mix_backward",
    )(proj, proj, logits, table, gain, raw, fresh, solved, states, grad)


def neighbours():
    me = lax.axis_index("seq")
    return me, me + 1 - 2 * (me % 2), me + 2 - 4 * (me // 2), 3 - me


def greet(across, along):
    barrier = pltpu.get_barrier_semaphore()
    for other in (across, along):
        pl.semaphore_signal(
            barrier, inc=1, device_id={"seq": other}, device_id_type=pl.DeviceIdType.MESH
        )
    pl.semaphore_wait(barrier, 2)


def remote(source, target, send, arrive, slot, other):
    return pltpu.make_async_remote_copy(
        src_ref=source,
        dst_ref=target,
        send_sem=send.at[slot],
        recv_sem=arrive.at[slot],
        device_id={"seq": other},
        device_id_type=pl.DeviceIdType.MESH,
    )


def half_of(rows):
    return (rows // 2 + 15) // 16 * 16


def gather_copies(source, target, near, send, arrive, keep):
    me, across, along, _ = near
    return (
        pltpu.make_async_copy(source, target.at[me], keep),
        remote(source, target.at[me], send, arrive, 0, across),
        remote(source, target.at[me], send, arrive, 1, along),
    )


def gather_start(source, target, near, send, arrive, keep):
    started = gather_copies(source, target, near, send, arrive, keep)
    for copy in started:
        copy.start()
    return started


def gather_finish(started, target, near, send, arrive):
    _, across, along, _ = near
    own, first, second = started
    rows = target.shape[1]
    split = half_of(rows)
    head, rest = pl.ds(0, split), pl.ds(split, rows - split)
    first.wait_recv()
    third = remote(target.at[across, head], target.at[across, head], send, arrive, 2, along)
    third.start()
    second.wait_recv()
    fourth = remote(target.at[along, rest], target.at[along, rest], send, arrive, 3, across)
    fourth.start()
    third.wait_recv()
    fourth.wait_recv()
    for copy in (first, second, third, fourth):
        copy.wait_send()
    own.wait()


def gather_kernel(count, inputs, outputs, body, *refs):
    sources, operands = refs[:count], refs[count : count + inputs]
    targets = refs[count + inputs : 2 * count + inputs]
    results = refs[2 * count + inputs : 2 * count + inputs + outputs]
    send, arrive, keep = refs[2 * count + inputs + outputs :]
    near = neighbours()

    def copies(i):
        return gather_copies(sources[i], targets[i], near, send.at[i], arrive.at[i], keep.at[i])

    @pl.when(pl.program_id(0) == 0)
    def _():
        greet(near[1], near[2])
        for i in range(count):
            for copy in copies(i):
                copy.start()

    body(*operands, *results)

    @pl.when(pl.program_id(0) == pl.num_programs(0) - 1)
    def _():
        for i in range(count):
            gather_finish(copies(i), targets[i], near, send.at[i], arrive.at[i])


def nothing(*refs):
    del refs


def beside_gather(number, blocks, work=(nothing, "gather", (1,), [], [], [], [])):
    side, count = lax.axis_size("seq"), len(blocks)
    body, name, grid, out_shape, in_specs, out_specs, operands = work
    if side != 4 and not operands:
        return [lax.all_gather(block, "seq", axis=0) for block in blocks], []
    if side != 4:
        results = pl.pallas_call(
            body, grid=grid, out_shape=out_shape, in_specs=in_specs, out_specs=out_specs, name=name
        )(*operands)
        return [lax.all_gather(block, "seq", axis=0) for block in blocks], results
    anywhere = [pl.BlockSpec(memory_space=pl.ANY)] * count
    moved = sum(block.size for block in blocks)
    results = pl.pallas_call(
        functools.partial(gather_kernel, count, len(operands), len(out_shape), body),
        grid=grid,
        out_shape=[
            jax.ShapeDtypeStruct((side,) + block.shape, block.dtype) for block in blocks
        ]
        + out_shape,
        in_specs=anywhere + in_specs,
        out_specs=anywhere + out_specs,
        scratch_shapes=[
            pltpu.SemaphoreType.DMA((count, 4)),
            pltpu.SemaphoreType.DMA((count, 4)),
            pltpu.SemaphoreType.DMA((count,)),
        ],
        compiler_params=pltpu.CompilerParams(
            collective_id=number, has_side_effects=True, vmem_limit_bytes=40 * 2**20
        ),
        cost_estimate=pl.CostEstimate(flops=0, bytes_accessed=160 * moved, transcendentals=0),
        name=name,
    )(*blocks, *operands)
    return results[:count], results[count:]


def signal_all(peers):
    barrier = pltpu.get_barrier_semaphore()
    for peer in peers:
        pl.semaphore_signal(barrier, inc=1, device_id=peer, device_id_type=pl.DeviceIdType.MESH)
    pl.semaphore_wait(barrier, len(peers))


def send_share(row, first, where, mine, boxes, send, arrive):
    axis, spot, size = where
    copies = []
    for step in range(1, size):
        copies.append(
            pltpu.make_async_remote_copy(
                src_ref=mine.at[row],
                dst_ref=boxes.at[row, spot],
                send_sem=send.at[first + step - 1],
                recv_sem=arrive.at[first + step - 1],
                device_id={axis: (spot + step) % size},
                device_id_type=pl.DeviceIdType.MESH,
            )
        )
        copies[-1].start()
    boxes[row, spot] = mine[row]
    return copies


def add_shares(row, size, copies, boxes):
    for copy in copies:
        copy.wait()
    total = boxes[row, 0]
    for index in range(1, size):
        total = total + boxes[row, index]
    return total


def start_kernel(
    source_ref, small_ref, sources, smalls,
    send, arrive, keep, send_z, arrive_z, keep_z,
):
    near = neighbours()
    _, across, along, _ = near
    here, count = lax.axis_index("fsdp"), lax.axis_size("fsdp")
    sibling = here + 1 - 2 * (here % 2)
    others = [(here + 2 * step) % count for step in range(1, count // 2)]
    barrier = pltpu.get_barrier_semaphore()
    peers = [{"seq": across}, {"seq": along}, {"fsdp": sibling}]
    peers += [{"fsdp": other} for other in others]
    for peer in peers:
        pl.semaphore_signal(barrier, inc=1, device_id=peer, device_id_type=pl.DeviceIdType.MESH)
    pl.semaphore_wait(barrier, len(peers))

    def send_to(source, target, row, slot, other):
        return pltpu.make_async_remote_copy(
            src_ref=source,
            dst_ref=target,
            send_sem=send_z.at[row, slot],
            recv_sem=arrive_z.at[row, slot],
            device_id={"fsdp": other},
            device_id_type=pl.DeviceIdType.MESH,
        )

    flow = [(small_ref, smalls)]
    first = []
    for row, (source, target) in enumerate(flow):
        own = pltpu.make_async_copy(source, target.at[here], keep_z.at[row])
        own.start()
        copies = [send_to(source, target.at[here], row, 0, sibling)]
        copies += [
            send_to(source, target.at[here], row, 1 + i, other) for i, other in enumerate(others)
        ]
        for copy in copies:
            copy.start()
        first.append((own, copies))
    started = [
        gather_start(block, target, near, send.at[i], arrive.at[i], keep.at[i])
        for i, (block, target) in enumerate([(source_ref, sources)])
    ]
    gather_finish(started[0], sources, near, send.at[0], arrive.at[0])
    for row, (source, target) in enumerate(flow):
        own, copies = first[row]
        passed = []
        for i in range(len(others)):
            copies[1 + i].wait_recv()
            origin = target.at[(here + count - 2 * (i + 1)) % count]
            passed.append(send_to(origin, origin, row, 1 + len(others) + i, sibling))
            passed[-1].start()
        copies[0].wait_recv()
        for copy in passed:
            copy.wait_recv()
        for copy in copies + passed:
            copy.wait_send()
        own.wait()


def start_gathers(source, small):
    side, count = lax.axis_size("seq"), lax.axis_size("fsdp")
    if side != 4:
        return (
            lax.all_gather(source, "seq", axis=0),
            lax.all_gather(small, "fsdp", axis=0),
        )
    slots = count - 1
    return pl.pallas_call(
        start_kernel,
        out_shape=[
            jax.ShapeDtypeStruct((many,) + block.shape, block.dtype)
            for block, many in ((source, side), (small, count))
        ],
        in_specs=[pl.BlockSpec(memory_space=pl.ANY)] * 2,
        out_specs=[pl.BlockSpec(memory_space=pl.ANY)] * 2,
        scratch_shapes=[
            pltpu.SemaphoreType.DMA((2, 4)),
            pltpu.SemaphoreType.DMA((2, 4)),
            pltpu.SemaphoreType.DMA((2,)),
            pltpu.SemaphoreType.DMA((2, slots)),
            pltpu.SemaphoreType.DMA((2, slots)),
            pltpu.SemaphoreType.DMA((2,)),
        ],
        compiler_params=pltpu.CompilerParams(collective_id=1, has_side_effects=True),
        cost_estimate=pl.CostEstimate(
            flops=0, bytes_accessed=160 * source.size, transcendentals=0
        ),
        name="start_gathers",
    )(source, small)


TILE = 256
STEP = 16


def reduce_rows_kernel(
    flip, gathers, totals, fills, streamed, epilogue, lefts, in_count, out_count, *refs
):
    streams, refs = refs[-1], refs[:-1]
    held_count = sum(streamed)
    held, refs = refs[-held_count:], refs[:-held_count]
    loads, inputs, spot = [], [], 0
    for source, wanted in zip(refs[:in_count], streamed):
        inputs.append(held[spot] if wanted else source)
        loads.append((source, held[spot]) if wanted else None)
        spot += wanted
    left_refs, right_ref, extra = inputs[:lefts], inputs[lefts], inputs[lefts + 1 :]
    outs = refs[in_count : in_count + out_count]
    far, wide_x, wide_y, own, get_a, get_b, get_x, get_y, send, arrive = refs[
        in_count + out_count : in_count + out_count + 10
    ]
    rest_refs = refs[in_count + out_count + 10 :]
    near = neighbours()
    me, across, along, opposite = near
    rows, width = own.shape
    tiles = width // TILE
    turns = (opposite, across, along, me)

    def left_copy(index, turn):
        source, target = loads[index]
        here = pl.ds(pl.multiple_of(turns[turn] * rows, rows), rows)
        return pltpu.make_async_copy(
            source.at[here], target.at[here], streams.at[index * 4 + turn]
        )

    def right_copy(tile):
        source, target = loads[lefts]
        columns = pl.ds(pl.multiple_of(tile * TILE, TILE), TILE)
        if flip:
            source, target = source.at[columns], target.at[columns]
        else:
            source, target = source.at[:, columns], target.at[:, columns]
        return pltpu.make_async_copy(source, target, streams.at[lefts * 4 + tile])

    def extra_copy(index):
        source, target = loads[lefts + 1 + index]
        return pltpu.make_async_copy(source, target, streams.at[lefts * 4 + tiles + index])

    def need(*indices):
        for index in indices:
            if loads[lefts + 1 + index] is not None:
                extra_copy(index).wait()

    for turn in range(4):
        for index in range(lefts):
            left_copy(index, turn).start()
        if turn == 0:
            for tile in range(tiles):
                right_copy(tile).start()
    for index in range(len(extra)):
        if loads[lefts + 1 + index] is not None:
            extra_copy(index).start()
    if totals:
        mine, boxes, send_t, arrive_t = rest_refs
        spots = [(axis, lax.axis_index(axis), lax.axis_size(axis)) for axis in ("seq", "fsdp")]
        signal_all(
            [{axis: (spot + step) % size} for axis, spot, size in spots for step in range(1, size)]
        )
        mine[0] = extra[-1][...]
        shares = send_share(0, 0, spots[0], mine, boxes, send_t, arrive_t)
    else:
        greet(across, along)
    split = half_of(rows)
    head, rest = pl.ds(0, split), pl.ds(split, rows - split)

    def part(turn, store):
        here = pl.ds(pl.multiple_of(turns[turn] * rows, rows), rows)
        for index in range(lefts):
            left_copy(index, turn).wait()

        @pl.loop(0, tiles)
        def _(tile):
            columns = pl.ds(pl.multiple_of(tile * TILE, TILE), TILE)
            if turn == 0:
                right_copy(tile).wait()
            value, base = 0.0, 0
            for left_ref in left_refs:
                depth = pl.ds(base, left_ref.shape[1])
                if flip:
                    value = value + dotf(left_ref[here, :], right_ref[columns, depth], NT)
                else:
                    value = value + dotf(left_ref[here, :], right_ref[depth, columns], NN)
                base += left_ref.shape[1]
            store[:, columns] = value.astype(store.dtype)

    def term(rows_ref, grads_ref, store):
        @pl.loop(0, rows_ref.shape[1] // TILE)
        def _(tile):
            columns = pl.ds(pl.multiple_of(tile * TILE, TILE), TILE)
            store[columns, :] = low(dotf(rows_ref[:, columns], grads_ref[...], TN))

    def add_into(store, base, source):
        @pl.loop(0, source.shape[0] // STEP)
        def _(index):
            start = pl.multiple_of(index * STEP, STEP)
            there = pl.ds(pl.multiple_of(base + start, STEP), STEP)
            total = store[there, :].astype(jnp.float32) + source[pl.ds(start, STEP), :].astype(
                jnp.float32
            )
            store[there, :] = low(total)

    part(0, far)
    if totals:
        mine[1] = add_shares(0, spots[0][2], shares, boxes)
        shares = send_share(1, spots[0][2] - 1, spots[1], mine, boxes, send_t, arrive_t)
    copies = [
        remote(far.at[head], get_a, send, arrive, 0, across),
        remote(far.at[rest], get_b, send, arrive, 1, along),
    ]
    copies[0].start()
    copies[1].start()
    part(1, wide_x)
    copies.append(remote(wide_x.at[head], get_x.at[head], send, arrive, 2, across))
    copies[2].start()
    part(2, wide_y)
    if fills:
        copies.append(remote(wide_y.at[rest], get_y.at[rest], send, arrive, 3, along))
        copies[3].start()
        need(1, 2)
        term(extra[1], extra[2], outs[1])
    else:
        copies.append(remote(wide_y.at[rest], get_y.at[rest], send, arrive, 3, along))
        copies[3].start()
    copies[0].wait_recv()
    add_into(wide_y, 0, get_a)
    copies.append(remote(wide_y.at[head], get_y.at[head], send, arrive, 4, along))
    copies[4].start()
    copies[1].wait_recv()
    add_into(wide_x, split, get_b)
    copies.append(remote(wide_x.at[rest], get_x.at[rest], send, arrive, 5, across))
    copies[5].start()
    if fills:
        need(3)
        term(extra[1], extra[3], outs[2])
    part(3, own)
    need(*([0] if fills else range(len(extra))))
    for copy in copies[2:]:
        copy.wait_recv()
    epilogue_prepare = rest_refs[0] if gathers else None

    @pl.loop(0, rows // STEP)
    def _(index):
        here = pl.ds(pl.multiple_of(index * STEP, STEP), STEP)
        total = (
            own[here, :] + get_x[here, :].astype(jnp.float32) + get_y[here, :].astype(jnp.float32)
        )
        epilogue(index, here, total, extra, outs, epilogue_prepare)

    for copy in copies:
        copy.wait_send()
    if totals:
        outs[-1][...] = add_shares(1, spots[1][2], shares, boxes)
    if gathers:
        block, send_2, arrive_2, keep = rest_refs
        target = outs[0]
        started = gather_start(block, target, near, send_2, arrive_2, keep.at[0])
        gather_finish(started, target, near, send_2, arrive_2)


def rms_back(grad, values, gain):
    r = lax.rsqrt(jnp.mean(values * values, axis=-1, keepdims=True) + EPS)
    scaled = grad * gain
    change = r * (scaled - values * (r * r) * jnp.mean(scaled * values, axis=-1, keepdims=True))
    return change


def middle_epilogue(index, here, total, extra, outs, block):
    source_ref, gain_ref = extra
    middle = source_ref[here, :].astype(jnp.float32) + total
    outs[1][here, :] = middle
    r = lax.rsqrt(jnp.mean(middle * middle, axis=-1, keepdims=True) + EPS)
    block[here, :] = low(middle * r * gain_ref[...])


def output_epilogue(index, here, total, extra, outs, block):
    outs[0][here, :] = low(extra[0][here, :] + total)


def branch_epilogue(index, here, total, extra, outs, block):
    middle_ref, upstream_ref, gain_ref = extra
    change = rms_back(total, middle_ref[here, :], gain_ref[...])
    grad = upstream_ref[here, :].astype(jnp.float32) + change
    outs[1][here, :] = grad
    block[here, :] = low(grad)


def input_epilogue(index, here, total, extra, outs, block):
    source_ref, carried_ref, gain_ref, _ = extra
    change = rms_back(total, source_ref[here, :].astype(jnp.float32), gain_ref[...])
    outs[0][here, :] = carried_ref[here, :] + change


def fused_reduce(name, number, flip, mode, epilogue, outs, lefts, right, *extra):
    gathers, totals = mode == "gather", mode == "total"
    side = lax.axis_size("seq")
    length = lefts[0].shape[0]
    rows = length // side
    width = right.shape[0] if flip else right.shape[1]
    split = half_of(rows)
    scratch = [
        pltpu.VMEM((rows, width), jnp.bfloat16),
        pltpu.VMEM((rows, width), jnp.bfloat16),
        pltpu.VMEM((rows, width), jnp.bfloat16),
        pltpu.VMEM((rows, width), jnp.float32),
        pltpu.VMEM((split, width), jnp.bfloat16),
        pltpu.VMEM((rows - split, width), jnp.bfloat16),
        pltpu.VMEM((rows, width), jnp.bfloat16),
        pltpu.VMEM((rows, width), jnp.bfloat16),
        pltpu.SemaphoreType.DMA((6,)),
        pltpu.SemaphoreType.DMA((6,)),
    ]
    out_specs = in_vmem(len(outs))
    if totals:
        shape, f_count = extra[-1].shape, lax.axis_size("fsdp")
        peers = side + f_count - 2
        scratch += [
            pltpu.VMEM((2,) + shape, jnp.float32),
            pltpu.VMEM((2, max(side, f_count)) + shape, jnp.float32),
            pltpu.SemaphoreType.DMA((peers,)),
            pltpu.SemaphoreType.DMA((peers,)),
        ]
    if gathers:
        scratch += [
            pltpu.VMEM((rows, width), jnp.bfloat16),
            pltpu.SemaphoreType.DMA((4,)),
            pltpu.SemaphoreType.DMA((4,)),
            pltpu.SemaphoreType.DMA((1,)),
        ]
        out_specs[0] = pl.BlockSpec(memory_space=pl.ANY)
    inputs = [*lefts, right, *extra]
    streamed = tuple(array.size > 2**16 for array in inputs)
    scratch += [
        pltpu.VMEM(array.shape, array.dtype) for array, wanted in zip(inputs, streamed) if wanted
    ]
    scratch.append(pltpu.SemaphoreType.DMA((len(lefts) * 4 + width // TILE + len(extra),)))
    return pl.pallas_call(
        functools.partial(
            reduce_rows_kernel,
            flip,
            gathers,
            totals,
            mode == "fill",
            streamed,
            epilogue,
            len(lefts),
            len(lefts) + 1 + len(extra),
            len(outs),
        ),
        out_shape=outs,
        in_specs=[
            pl.BlockSpec(memory_space=pl.ANY if wanted else pltpu.VMEM) for wanted in streamed
        ],
        out_specs=out_specs,
        scratch_shapes=scratch,
        compiler_params=pltpu.CompilerParams(
            collective_id=number, has_side_effects=True, vmem_limit_bytes=56 * 2**20
        ),
        cost_estimate=pl.CostEstimate(
            flops=2 * sum(left.size for left in lefts) * width,
            bytes_accessed=(320 if gathers else 160) * rows * width,
            transcendentals=0,
        ),
        name=name,
    )(*lefts, right, *extra)


def seq_sum(partial, side):
    block = low(partial).reshape(side, -1, partial.shape[-1])
    return lax.psum_scatter(block, "seq", scatter_dimension=0).astype(jnp.float32)


def out_and_norm(attn_in, weight, source, gain):
    side = lax.axis_size("seq")
    rows, width = source.shape
    if side != 4:
        middle = source.astype(jnp.float32) + seq_sum(dotf(attn_in, weight, NN), side)
        r = lax.rsqrt(jnp.mean(middle * middle, axis=-1, keepdims=True) + EPS)
        return lax.all_gather(low(middle * r * gain), "seq", axis=0), middle
    outs = (
        jax.ShapeDtypeStruct((side, rows, width), jnp.bfloat16),
        jax.ShapeDtypeStruct((rows, width), jnp.float32),
    )
    return fused_reduce(
        "out_and_norm", 2, False, "gather", middle_epilogue, outs, [attn_in], weight, source, gain
    )


def place_kernel(side, *refs):
    target_ref = refs[side]
    me = lax.axis_index("seq")
    for spot in range(side):

        @pl.when(me == spot)
        def _():
            for index in range(side):
                target_ref[index] = refs[index ^ spot][...].astype(target_ref.dtype)


def place_work(blocks, kind):
    side = len(blocks)
    rows, width = blocks[0].shape
    tile = 512
    return (
        functools.partial(place_kernel, side),
        "place",
        (width // tile,),
        [jax.ShapeDtypeStruct((side, rows, width), kind)],
        [pl.BlockSpec((rows, tile), lambda i: (0, i))] * side,
        [pl.BlockSpec((side, rows, tile), lambda i: (0, 0, i))],
        blocks,
    )


def place(blocks, kind):
    body, name, grid, out_shape, in_specs, out_specs, operands = place_work(blocks, kind)
    return pl.pallas_call(
        body, grid=grid, out_shape=out_shape, in_specs=in_specs, out_specs=out_specs, name=name
    )(*operands)[0]


def swap(block, step):
    pairs = [(i, i ^ step) for i in range(lax.axis_size("seq"))]
    return lax.ppermute(block, "seq", pairs)


def down_and_terms(hidden, weight, middle, ffn_in, grads):
    side = lax.axis_size("seq")
    if side != 4:
        output = low(middle + seq_sum(dotf(hidden, weight, NN), side))
        return output, *[low(dotf(ffn_in, grad, TN)) for grad in grads]
    term = jax.ShapeDtypeStruct((ffn_in.shape[1], grads[0].shape[1]), jnp.bfloat16)
    outs = (jax.ShapeDtypeStruct(middle.shape, jnp.bfloat16), term, term)
    return fused_reduce(
        "down_and_terms", 3, False, "fill", output_epilogue, outs, [hidden], weight, middle, ffn_in,
        *grads,
    )


def branch_grad(grads, weight, middle, upstream, gain):
    side = lax.axis_size("seq")
    rows, width = middle.shape
    if side != 4:
        grad = jnp.concatenate(grads, axis=1)
        change = rms_back(seq_sum(dotf(grad, weight, NT), side), middle, gain)
        total = upstream.astype(jnp.float32) + change
        return lax.all_gather(low(total), "seq", axis=0), total
    outs = (
        jax.ShapeDtypeStruct((side, rows, width), jnp.bfloat16),
        jax.ShapeDtypeStruct((rows, width), jnp.float32),
    )
    return fused_reduce(
        "branch_grad", 4, True, "gather", branch_epilogue, outs, grads, weight, middle, upstream, gain
    )


def input_grad(grad, weight, source, carried, gain, value):
    side = lax.axis_size("seq")
    if side != 4:
        partial = dotf(grad, weight[:, : grad.shape[1]], NT)
        change = rms_back(seq_sum(partial, side), source.astype(jnp.float32), gain)
        return carried + change, lax.psum(value, ("fsdp", "seq"))
    outs = (
        jax.ShapeDtypeStruct(carried.shape, jnp.float32),
        jax.ShapeDtypeStruct(value.shape, jnp.float32),
    )
    return fused_reduce(
        "input_grad", 5, True, "total", input_epilogue, outs, [grad], weight, source, carried, gain,
        value,
    )


def pack_kernel(wide, qkv_ref, beta_ref, out_ref, packed_ref):
    width = out_ref.shape[1]
    base = lax.axis_index("seq") * wide
    for part in range(3):
        columns = pl.ds(pl.multiple_of(part * width + base, DK), wide)
        packed_ref[:, pl.ds(part * wide, wide)] = qkv_ref[:, columns]
    packed_ref[:, pl.ds(3 * wide, DK)] = beta_ref[...]
    columns = pl.ds(pl.multiple_of(base, DK), wide)
    packed_ref[:, pl.ds(3 * wide + DK, wide)] = out_ref[:, columns]


def pack_parts(w_qkv, beta_part, w_out, wide):
    rows = w_qkv.shape[0]
    tile = 64
    widths = (w_qkv.shape[1], DK, w_out.shape[1], 4 * wide + DK)
    specs = [pl.BlockSpec((tile, size), lambda i: (i, 0)) for size in widths]
    return pl.pallas_call(
        functools.partial(pack_kernel, wide),
        grid=(rows // tile,),
        out_shape=jax.ShapeDtypeStruct((rows, widths[3]), w_qkv.dtype),
        in_specs=specs[:3],
        out_specs=specs[3],
        name="pack_parts",
    )(w_qkv, beta_part, w_out)


def pick_kernel(side, share, source_ref, target_ref):
    me = lax.axis_index("seq")
    count = target_ref.shape[1] // share
    for index in range(side):

        @pl.when(me == index)
        def _():
            pieces = [
                source_ref[:, pl.ds((k * side + index) * share, share)].astype(jnp.float32)
                for k in range(count)
            ]
            target_ref[...] = low(jnp.concatenate(pieces, axis=1))


def pick_columns(weight, share):
    side = lax.axis_size("seq")
    rows, width = weight.shape
    tile = 32
    return pl.pallas_call(
        functools.partial(pick_kernel, side, share),
        grid=(rows // tile,),
        out_shape=jax.ShapeDtypeStruct((rows, width // side), weight.dtype),
        in_specs=[pl.BlockSpec((tile, width), lambda i: (i, 0))],
        out_specs=pl.BlockSpec((tile, width // side), lambda i: (i, 0)),
        name="pick_columns",
    )(weight)


def spread_kernel(side, share, *refs):
    gate_refs, (up_ref, weight_ref, target_ref, total_ref) = refs[:side], refs[side:]
    count = up_ref.shape[2] // share
    me = lax.axis_index("seq")
    half = target_ref.shape[1] // 2

    def place(pieces, base):
        grad = jnp.concatenate([piece.astype(jnp.float32) for piece in pieces], axis=1)
        target_ref[:, pl.ds(base, half)] = low(grad)
        weight = weight_ref[:, pl.ds(base, half)].astype(jnp.float32)
        return jnp.sum(grad * weight, axis=1, keepdims=True)

    spans = [(pl.ds(k * share, share), index) for k in range(count) for index in range(side)]
    total = place([up_ref[index, :, span] for span, index in spans], half)
    for spot in range(side):

        @pl.when(me == spot)
        def _():
            whole = total + place([gate_refs[index ^ spot][:, span] for span, index in spans], 0)
            total_ref[...] = jnp.broadcast_to(whole, total_ref.shape)


def spread_work(gates, up, weight, share):
    side, rows, width = up.shape
    tile = 32
    by_row = pl.BlockSpec((tile, 2 * width * side), lambda i: (i, 0))
    return (
        functools.partial(spread_kernel, side, share),
        "spread",
        (rows // tile,),
        [
            jax.ShapeDtypeStruct((rows, 2 * width * side), jnp.bfloat16),
            jax.ShapeDtypeStruct((rows, DK), jnp.float32),
        ],
        [pl.BlockSpec((tile, width), lambda i: (i, 0))] * side
        + [pl.BlockSpec((side, tile, width), lambda i: (0, i, 0)), by_row],
        [by_row, pl.BlockSpec((tile, DK), lambda i: (i, 0))],
        [*gates, up, weight],
    )


def assemble_kernel(
    side, wide, taps, grad_ref, weight_ref, beta_ref, target_ref, total_ref, rest_ref
):
    heads = wide // DK
    total = 0.0
    for part in range(3):
        for index in range(side):
            columns = pl.ds((part * side + index) * wide, wide)
            grad = grad_ref[index, :, pl.ds(part * wide, wide)].astype(jnp.float32)
            target_ref[:, columns] = grad
            weight = weight_ref[:, columns].astype(jnp.float32)
            total = total + jnp.sum(grad * weight, axis=1, keepdims=True)
    lane = lax.broadcasted_iota(jnp.int32, beta_ref.shape, 1)
    beta, conv = 0.0, 0.0
    for index in range(side):
        rest = grad_ref[index, :, pl.ds(3 * wide, DK)].astype(jnp.float32)
        mine = jnp.where(lane < heads, rest, 0.0)
        beta = beta + (pltpu.roll(mine, index * heads, 1) if index else mine)
        conv = conv + rest
    conv = jnp.where((lane >= heads) & (lane < heads + 3 * taps), conv, 0.0)
    if side > 1:
        conv = pltpu.roll(conv, H - heads, 1)
    total = total + jnp.sum(beta * beta_ref[...].astype(jnp.float32), axis=1, keepdims=True)
    total_ref[...] = jnp.broadcast_to(total, total_ref.shape)
    rest_ref[...] = (beta + conv).T


def assemble_columns(grad, weight, beta, wide, taps):
    side, rows, depth = grad.shape
    tile = min(rows, DK)
    by_row = pl.BlockSpec((tile, weight.shape[1]), lambda i: (i, 0))
    narrow = pl.BlockSpec((tile, DK), lambda i: (i, 0))
    return pl.pallas_call(
        functools.partial(assemble_kernel, side, wide, taps),
        grid=(rows // tile,),
        out_shape=(
            jax.ShapeDtypeStruct(weight.shape, jnp.float32),
            jax.ShapeDtypeStruct((rows, DK), jnp.float32),
            jax.ShapeDtypeStruct((DK, rows), jnp.float32),
        ),
        in_specs=[pl.BlockSpec((side, tile, depth), lambda i: (0, i, 0)), by_row, narrow],
        out_specs=(by_row, narrow, pl.BlockSpec((DK, tile), lambda i: (0, i))),
        compiler_params=pltpu.CompilerParams(vmem_limit_bytes=40 * 2**20),
        name="assemble_columns",
    )(grad, weight, beta)


def fsdp_sum(term):
    return lax.psum_scatter(low(term), "fsdp", scatter_dimension=0, tiled=True)


def per_device(
    inputs,
    cotangent,
    norm1_gain,
    w_qkv,
    w_beta,
    conv_weight,
    out_gain,
    w_out,
    norm2_gain,
    w_gate_up,
    w_down,
):
    side = lax.axis_size("seq")
    s = lax.axis_index("seq")
    shape = inputs.shape
    width = shape[2]
    source = inputs.reshape(-1, width)
    upstream = cotangent.reshape(-1, width)
    length = source.shape[0] * side
    heads = H // side
    wide = heads * DK
    rows = w_qkv.shape[0]
    share = w_down.shape[0] // side
    taps = conv_weight.shape[1] // 3

    f_count = lax.axis_size("fsdp")
    depth = 3 * wide + DK
    homes = [
        (f * side + i, (side * (f % 2) + i) * side + f // 2)
        for f in range(f_count)
        for i in range(side)
    ]

    def everywhere(block):
        return lax.all_gather(block, "fsdp", axis=0, tiled=True)

    beta_part = lax.dynamic_slice_in_dim(w_beta, s * heads, heads, 1)
    beta_part = jnp.pad(beta_part, ((0, 0), (0, DK - heads)))
    qkv_part = everywhere(pack_parts(w_qkv, beta_part, w_out, wide))
    small = jnp.concatenate([norm1_gain[None], norm2_gain[None], conv_weight.T], axis=0)
    small = jnp.pad(small, ((0, 16 - small.shape[0]), (0, 0)))
    source_all, small = start_gathers(source, small)
    sent, source_all = lax.optimization_barrier((upstream, source_all))
    out_part = lax.all_to_all(
        qkv_part[:, depth:], "seq", split_axis=0, concat_axis=1, tiled=True
    )
    upstreams = [upstream] + [swap(sent, step) for step in range(1, side)]
    small = small.transpose(1, 0, 2).reshape(small.shape[1], width).astype(jnp.float32)
    gain_first = small[0:1]
    gain_second = small[1:2]
    table = lax.dynamic_slice_in_dim(small[2 : 2 + 3 * taps], s * wide, wide, 1)
    gain_heads = out_gain.astype(jnp.float32)[None]
    source_all = source_all.reshape(length, width).astype(jnp.float32)

    picked = pick_columns(w_gate_up, share)
    gate_up_part = everywhere(picked)
    down_part = everywhere(lax.dynamic_slice_in_dim(w_down, s * share, share, 0))

    normed_first = low(
        source_all
        * lax.rsqrt(jnp.mean(source_all * source_all, axis=-1, keepdims=True) + EPS)
        * gain_first
    )
    projected = low(dotf(normed_first, qkv_part[:, : 3 * wide], NN))
    beta_logits = dotf(normed_first, qkv_part[:, 3 * wide : depth], NN)
    attn_in, *kept = mix_forward(projected, beta_logits, table, gain_heads)
    attn_in, *upstreams = lax.optimization_barrier((attn_in, *upstreams))
    upstream_all = place(upstreams, jnp.bfloat16).reshape(length, width)
    ffn_in, middle = out_and_norm(attn_in, out_part, source, gain_second)
    ffn_in = ffn_in.reshape(length, width)
    gate_up = dotf(ffn_in, gate_up_part, NN)
    hidden_width = gate_up.shape[1] // 2
    gate = gate_up[:, :hidden_width]
    upward = gate_up[:, hidden_width:]
    sigma = jax.nn.sigmoid(gate)
    hidden = low(gate * sigma * upward)

    down_term = low(dotf(hidden, upstream_all, TN))
    grad_down = fsdp_sum(down_term)
    upstream_all, _ = lax.optimization_barrier((upstream_all, down_term))
    grad_hidden = dotf(upstream_all, down_part, NT)
    grad_gate = low(grad_hidden * upward * sigma * (1.0 + gate * (1.0 - sigma)))
    grad_up = low(grad_hidden * gate * sigma)
    output, gate_term, up_term = down_and_terms(
        hidden, down_part, middle, ffn_in, [grad_gate, grad_up]
    )
    gate_sum = fsdp_sum(gate_term)
    up_sum = fsdp_sum(up_term)
    grad_gate, grad_up, grad_down = lax.optimization_barrier((grad_gate, grad_up, grad_down))
    grad_branch, grad_middle = branch_grad(
        [grad_gate, grad_up], gate_up_part, middle, upstream, gain_second
    )
    grad_branch, grad_down, gate_sum = lax.optimization_barrier(
        (grad_branch, grad_down, gate_sum)
    )
    grad_branch = grad_branch.reshape(length, width)
    downs = [grad_down] + [swap(grad_down, step) for step in range(1, side)]
    gates = [gate_sum] + [swap(gate_sum, step) for step in range(1, side)]

    out_term = low(dotf(attn_in, grad_branch, TN))
    grad_attn_in, _ = lax.optimization_barrier((dotf(grad_branch, out_part, NT), out_term))
    grad_proj, grad_table, grad_gain_heads = mix_backward(
        projected, beta_logits, table, gain_heads, *kept, grad_attn_in
    )
    grad_proj, up_sum, *downs = lax.optimization_barrier((grad_proj, up_sum, *downs))
    grad_qkv = low(dotf(normed_first, grad_proj, TN))
    grad_qkv = lax.dynamic_update_slice(
        grad_qkv, low(grad_table.T), (s * wide, 3 * wide + heads)
    )
    grad_down = place(downs, jnp.float32)
    grad_proj, grad_qkv, out_term, grad_down, *gates = lax.optimization_barrier(
        (grad_proj, grad_qkv, out_term, grad_down, *gates)
    )
    grad_qkv = fsdp_sum(grad_qkv)
    grad_input, grad_out_gain = input_grad(
        grad_proj, qkv_part, source, grad_middle, gain_first,
        jnp.broadcast_to(grad_gain_heads, (8, DK)),
    )
    up_sum, grad_input = lax.optimization_barrier((up_sum, grad_input))
    (up_sum,), _ = beside_gather(7, [up_sum])
    out_term, grad_qkv, up_sum = lax.optimization_barrier((out_term, grad_qkv, up_sum))
    out_sum = fsdp_sum(out_term)
    (grad_qkv,), (grad_w_gate_up, second_total) = beside_gather(
        9, [grad_qkv], spread_work(gates, up_sum, w_gate_up, share)
    )
    out_sum = lax.ppermute(out_sum, ("fsdp", "seq"), [(b, a) for a, b in homes])
    (grad_w_out,), _ = beside_gather(8, [out_sum])
    wide_beta = jnp.pad(w_beta, ((0, 0), (0, DK - H)))
    grad_w_qkv, first_total, rest = assemble_columns(grad_qkv, w_qkv, wide_beta, wide, taps)
    return (
        output.reshape(shape),
        grad_input.reshape(shape),
        first_total[:, 0] / norm1_gain.astype(jnp.float32),
        grad_w_qkv,
        rest[:H].T,
        rest[H : H + 3 * taps].T,
        grad_out_gain[0],
        grad_w_out.reshape(rows, width).astype(jnp.float32),
        second_total[:, 0] / norm2_gain.astype(jnp.float32),
        grad_w_gate_up.astype(jnp.float32),
        grad_down.reshape(side * share, width),
    )


def solution(mesh):
    by_row = P("fsdp", None)
    tokens = P("fsdp", "seq", None)
    specs = (tokens, tokens, P("fsdp"), by_row, by_row, by_row, P(), by_row, P("fsdp"))
    specs = specs + (by_row, by_row)
    return jax.shard_map(per_device, mesh=mesh, in_specs=specs, out_specs=specs, check_vma=False)
```
